32 devices in a mesh: dp: 16 (over z, y, x), kv: 2 (over core).
Axes of the slice: x: 2, y: 2, z: 4, core: 2. Of those that a mesh axis runs over, the one named last changes fastest.
Arguments:
- tokens: bfloat16 [256, 64, 768], P(('dp', 'kv')), may hold values from -6 to 6
- images: bfloat16 [256, 576, 768], P('dp', 'kv'), may hold values from -6 to 6
- image_counts: int32 [256], P('dp'), may hold values from 196 to 576, as said below
- cotangent: bfloat16 [256, 64, 768], P(('dp', 'kv')), may hold values from -6 to 6
- norm1_gain: float32 [768], replicated, may hold values from 0.5 to 1.5
- norm1_shift: float32 [768], replicated, may hold values from -3 to 3
- self_qkv: bfloat16 [768, 2304], replicated, may hold values from -0.21875 to 0.21875
- self_out: bfloat16 [768, 768], replicated, may hold values from -0.875 to 0.875
- norm2_gain: float32 [768], replicated, may hold values from 0.5 to 1.5
- norm2_shift: float32 [768], replicated, may hold values from -3 to 3
- cross_q: bfloat16 [768, 768], replicated, may hold values from -0.21875 to 0.21875
- cross_kv: bfloat16 [768, 1536], replicated, may hold values from -0.21875 to 0.21875
- cross_out: bfloat16 [768, 768], replicated, may hold values from -1.75 to 1.75
- norm3_gain: float32 [768], replicated, may hold values from 0.5 to 1.5
- norm3_shift: float32 [768], replicated, may hold values from -3 to 3
- w_up: bfloat16 [768, 3072], replicated, may hold values from -0.21875 to 0.21875
- w_down: bfloat16 [3072, 768], replicated, may hold values from -0.109375 to 0.109375
Outputs:
- layer_out: bfloat16 [256, 64, 768], P(('dp', 'kv'))
- tokens_grad: bfloat16 [256, 64, 768], P(('dp', 'kv'))
- images_grad: bfloat16 [256, 576, 768], P('dp', 'kv')
- norm1_gain_grad: float32 [768], P('kv')
- norm1_shift_grad: float32 [768], P('kv')
- self_qkv_grad: float32 [768, 2304], P('dp', 'kv')
- self_out_grad: float32 [768, 768], P('dp', 'kv')
- norm2_gain_grad: float32 [768], P('kv')
- norm2_shift_grad: float32 [768], P('kv')
- cross_q_grad: float32 [768, 768], P('dp', 'kv')
- cross_kv_grad: float32 [768, 1536], P('dp', 'kv')
- cross_out_grad: float32 [768, 768], P('dp', 'kv')
- norm3_gain_grad: float32 [768], P('kv')
- norm3_shift_grad: float32 [768], P('kv')
- w_up_grad: float32 [768, 3072], P('dp', 'kv')
- down_weight_gradient: float32 [3072, 768], P('dp', 'kv')
The draws below stay inside these ranges and needn't reach their ends.
Inputs may be any that keep to these rules, and one draw needn't show every extreme that they name: `image_counts`: each caption's image fills its first 196 or all 576 patch slots.
All inputs are finite; a program needn't handle non-finite values.
Results may differ from the reference program's by a relative error of at most 0.02.
Values may be sent and summed in bfloat16 or wider, within the bound.
A program may use at most 256 MiB of HBM per device.

```python
import math
import jax
import jax.numpy as jnp
from jax import lax

D = 768
HEADS = 12
HEAD_DIM = 64
FF = 3072
LEN = 64
PATCH = 576
SHORT = 196
CAPS = 256


def draw_image_counts(key, part):
    picks = jax.random.randint(key, (CAPS,), 0, 2)
    places = jnp.arange(CAPS)
    picks = jnp.where(places == 0, 0, jnp.where(places == 1, 1, picks))
    return jnp.where(picks == 1, PATCH, SHORT).astype(jnp.int32)


def block_levels(stream_key, shape, cuts, smallest, high):
    def one(position, blocks):
        heights = jax.random.uniform(jax.random.fold_in(jax.random.fold_in(stream_key, 6), position), (blocks,), jnp.float32, smallest / len(cuts), high / len(cuts))
        return jnp.repeat(jnp.exp(heights), shape[position] // blocks).reshape((-1,) + (1,) * (len(shape) - position - 1))

    level = one(*cuts[0])
    for cut in cuts[1:]:
        level = level * one(*cut)
    return level


def centred(stream_key, shape, width, most, shards=(), held_as=jnp.bfloat16):
    level = block_levels(stream_key, shape, shards, -0.22, 0.18) if shards else 1.0
    values = jax.random.normal(stream_key, shape, jnp.float32) * width * level
    return jnp.minimum(jnp.maximum(values, -most), most).astype(held_as)


def setup_inputs(seed: int = 0) -> dict:
    streams_of = jax.random.split(jax.random.key(seed), 18)
    tokens = centred(streams_of[0], (CAPS, LEN, D), 1.0, 6.0, ((0, 32),))
    images = centred(streams_of[1], (CAPS, PATCH, D), 1.0, 6.0, ((0, 16), (1, 2)))
    image_counts = draw_image_counts(jax.random.fold_in(streams_of[17], 71), 0)
    cotangent = centred(streams_of[3], (CAPS, LEN, D), 1.0, 6.0, ((0, 32),))
    norm1_gain = jnp.clip(1.0 + 0.1 * jax.random.normal(streams_of[4], (D,), jnp.float32), 0.5, 1.5)
    norm1_shift = centred(streams_of[5], (D,), 0.5, 3.0, (), jnp.float32)
    self_qkv = centred(streams_of[6], (D, 3 * D), D ** -0.5, 0.21875)
    self_out = centred(streams_of[7], (D, D), (D // 16) ** -0.5, 0.875)
    norm2_gain = jnp.clip(1.0 + 0.1 * jax.random.normal(streams_of[8], (D,), jnp.float32), 0.5, 1.5)
    norm2_shift = centred(streams_of[9], (D,), 0.5, 3.0, (), jnp.float32)
    cross_q = centred(streams_of[10], (D, D), D ** -0.5, 0.21875)
    cross_kv = centred(streams_of[11], (D, 2 * D), D ** -0.5, 0.21875)
    cross_out = centred(streams_of[12], (D, D), (D // 64) ** -0.5, 1.75)
    norm3_gain = jnp.clip(1.0 + 0.1 * jax.random.normal(streams_of[13], (D,), jnp.float32), 0.5, 1.5)
    norm3_shift = centred(streams_of[14], (D,), 0.5, 3.0, (), jnp.float32)
    w_up = centred(streams_of[15], (D, FF), D ** -0.5, 0.21875)
    w_down = centred(streams_of[16], (FF, D), FF ** -0.5, 0.109375)
    return dict(tokens=tokens, images=images, image_counts=image_counts, cotangent=cotangent, norm1_gain=norm1_gain, norm1_shift=norm1_shift, self_qkv=self_qkv, self_out=self_out, norm2_gain=norm2_gain, norm2_shift=norm2_shift, cross_q=cross_q, cross_kv=cross_kv, cross_out=cross_out, norm3_gain=norm3_gain, norm3_shift=norm3_shift, w_up=w_up, w_down=w_down)


highest = lax.Precision.HIGHEST

@jax.custom_vjp
def low(v):
    return lax.optimization_barrier(v.astype(jnp.bfloat16)).astype(jnp.float32)

@jax.custom_vjp
def low_back(v):
    return v

def low_keep(v):
    return (low(v), None)

def low_pass(kept, grad):
    return (grad,)

def back_keep(v):
    return (v, None)

def back_low(kept, grad):
    return (low(grad),)
low.defvjp(low_keep, low_pass)
low_back.defvjp(back_keep, back_low)

def layer_norm(values, gain, shift):
    centered = values - lax.optimization_barrier(jnp.mean(values, axis=-1, keepdims=True))
    variance = lax.optimization_barrier(jnp.mean(centered * centered, axis=-1, keepdims=True))
    return centered * lax.rsqrt(variance + 1e-05) * gain + shift

def exact_gelu_activation(values):
    return 0.5 * values * (1.0 + jax.scipy.special.erf(values * 0.7071067811865476))

def softmax_rows(scores):
    peak = lax.optimization_barrier(jnp.max(scores, axis=-1, keepdims=True))
    exponent = jnp.exp(scores - peak)
    return exponent / lax.optimization_barrier(jnp.sum(exponent, axis=-1, keepdims=True))

def layer_block(params, inputs, pictures, counts):
    gain_one, shift_one, qkv_mat, out_mat, gain_two, shift_two, query_mat, keyval_mat, cross_mat, gain_three, shift_three, up_mat, down_mat = params
    captions = inputs.shape[0]
    row_count = captions * LEN
    score_scale = HEAD_DIM ** (-0.5)
    hidden_input_rows = inputs.reshape(row_count, D)
    normed_one = low(layer_norm(hidden_input_rows, gain_one, shift_one))
    qkv_all = low_back(low(jnp.dot(normed_one, qkv_mat, precision=highest)))
    qkv_all = qkv_all.reshape(captions, LEN, 3, HEADS, HEAD_DIM)
    queries = qkv_all[:, :, 0]
    keys = qkv_all[:, :, 1]
    values = qkv_all[:, :, 2]
    raw_self = low_back(jnp.einsum('bqhd,bkhd->bhqk', queries, keys, precision=highest) * score_scale)
    causal = lax.broadcasted_iota(jnp.int32, (LEN, LEN), 0) >= lax.broadcasted_iota(jnp.int32, (LEN, LEN), 1)
    probs = softmax_rows(jnp.where(causal, raw_self, -1e+30))
    attended = jnp.einsum('bhqk,bkhd->bqhd', low(probs), values, precision=highest).reshape(row_count, D)
    hidden_one = hidden_input_rows + low_back(jnp.dot(low_back(low(attended)), out_mat, precision=highest))
    normed_two = low(layer_norm(hidden_one, gain_two, shift_two))
    cross_queries = low_back(low(jnp.dot(normed_two, query_mat, precision=highest)))
    cross_queries = cross_queries.reshape(captions, LEN, HEADS, HEAD_DIM)
    keyvals = low_back(low(jnp.dot(pictures.reshape(captions * PATCH, D), keyval_mat, precision=highest)))
    keyvals = keyvals.reshape(captions, PATCH, 2, HEADS, HEAD_DIM)
    valid = lax.broadcasted_iota(jnp.int32, (captions, PATCH), 1) < counts[:, None]
    raw_cross = low_back(jnp.einsum('cqhd,cphd->cqhp', cross_queries, keyvals[:, :, 0], precision=highest) * score_scale)
    cross_probs = softmax_rows(jnp.where(valid[:, None, None, :], raw_cross, -1e+30))
    cross_att = jnp.einsum('cqhp,cphd->cqhd', cross_probs, keyvals[:, :, 1], precision=highest).reshape(row_count, D)
    hidden_two = hidden_one + low_back(jnp.dot(low_back(low(cross_att)), cross_mat, precision=highest))
    normed_three = low(layer_norm(hidden_two, gain_three, shift_three))
    up_pre = low_back(jnp.dot(normed_three, up_mat, precision=highest))
    activated = low(exact_gelu_activation(up_pre))
    result = hidden_two + low_back(jnp.dot(activated, down_mat, precision=highest))
    return result.reshape(captions, LEN, D)

def reference(tokens, images, image_counts, cotangent, norm1_gain, norm1_shift, self_qkv, self_out, norm2_gain, norm2_shift, cross_q, cross_kv, cross_out, norm3_gain, norm3_shift, w_up, w_down):
    params = tuple((item.astype(jnp.float32) for item in (norm1_gain, norm1_shift, self_qkv, self_out, norm2_gain, norm2_shift, cross_q, cross_kv, cross_out, norm3_gain, norm3_shift, w_up, w_down)))
    group_size = math.gcd(CAPS, 64)
    step_count = CAPS // group_size

    def whole(weights, inputs, pictures):

        def run_group(pieces):
            return layer_block(weights, pieces[0], pieces[1], pieces[2])
        outputs = lax.map(jax.checkpoint(run_group), (inputs.reshape(step_count, group_size, LEN, D), pictures.reshape(step_count, group_size, PATCH, D), image_counts.reshape(step_count, group_size)))
        return outputs.reshape(CAPS, LEN, D)
    layer_out, pullback = jax.vjp(whole, params, tokens.astype(jnp.float32), images.astype(jnp.float32))
    grads, tokens_grad, images_grad = pullback(cotangent.astype(jnp.float32))
    return (layer_out.astype(jnp.bfloat16), tokens_grad.astype(jnp.bfloat16), images_grad.astype(jnp.bfloat16), grads[0], grads[1], grads[2], grads[3], grads[4], grads[5], grads[6], grads[7], grads[8], grads[9], grads[10], grads[11], grads[12])
```

```python
import functools
import math

import jax
import jax.numpy as jnp
from jax import lax
from jax.experimental import pallas as pl
from jax.experimental.pallas import tpu as pltpu
from jax.sharding import PartitionSpec as P

HEADS = 12
HEAD_DIM = 64
SHORT = 196
LANES = 256
PACK = LANES // HEAD_DIM
GROUPS = HEADS // PACK
SCALE = HEAD_DIM ** (-0.5)
NEG = -1e30
F32 = jnp.float32
BF16 = jnp.bfloat16
VMEM_LIMIT = 60 * 1024 * 1024


def dot(a, b):
    return jnp.dot(a, b, preferred_element_type=F32)


def dot_nt(a, b):
    return lax.dot_general(a, b, (((1,), (1,)), ((), ())), preferred_element_type=F32)


def dot_tn(a, b):
    return lax.dot_general(a, b, (((0,), (0,)), ((), ())), preferred_element_type=F32)


def normalize(values):
    centered = values - jnp.mean(values, axis=-1, keepdims=True)
    inverse = lax.rsqrt(jnp.mean(centered * centered, axis=-1, keepdims=True) + 1e-05)
    return centered * inverse, inverse


def norm_back(grad, gain, unit, inverse):
    scaled = grad * gain
    mean_one = jnp.mean(scaled, axis=-1, keepdims=True)
    mean_two = jnp.mean(scaled * unit, axis=-1, keepdims=True)
    return (scaled - mean_one - unit * mean_two) * inverse


def iota(shape, dim):
    return lax.broadcasted_iota(jnp.int32, shape, dim)


def same_head():
    shape = (LANES, LANES)
    return (iota(shape, 0) // HEAD_DIM) == (iota(shape, 1) // HEAD_DIM)


def spread(rows, mask):
    stacked = jnp.concatenate([rows] * PACK, axis=0)
    return jnp.where(mask, stacked, jnp.zeros_like(stacked))


def gather_heads(full):
    count = full.shape[0] // PACK
    head = iota((count, LANES), 1) // HEAD_DIM
    out = full[:count]
    for index in range(1, PACK):
        out = jnp.where(head == index, full[index * count : (index + 1) * count], out)
    return out


def split_two(value):
    high = value.astype(BF16)
    return high, (value - high.astype(F32)).astype(BF16)


def lanes_to_rows(row, mask_low):
    shape = (HEAD_DIM, LANES)
    pick = iota(shape, 0) == (iota(shape, 1) % HEAD_DIM)
    high, low = split_two(jnp.where(pick, row, 0.0))
    return dot(high, mask_low) + dot(low, mask_low)


def rows_to_lanes(rows, mask_low):
    high, low = split_two(rows)
    summed = dot(high, mask_low) + dot(low, mask_low)
    shape = (HEAD_DIM, LANES)
    pick = iota(shape, 0) == (iota(shape, 1) % HEAD_DIM)
    return jnp.sum(jnp.where(pick, summed, 0.0), axis=0, keepdims=True)


def lane_slice(group):
    return slice(group * LANES, (group + 1) * LANES)


def causal_mask(length):
    shape = (length, LANES)
    return iota(shape, 0) <= (iota(shape, 1) % HEAD_DIM)


def token_start_body(
    tok_ref, gain_one, shift_one, qkv_mat, out_mat, gain_two, shift_two, query_mat,
    qkv_ref, att_ref, hidden_ref, query_ref, *, length
):
    x = tok_ref[...].astype(F32)
    unit, _ = normalize(x)
    normed = (unit * gain_one[...] + shift_one[...]).astype(BF16)
    width = x.shape[1]
    qkv_ref[...] = dot(normed, qkv_mat[...]).astype(BF16)
    mask = same_head()
    causal = causal_mask(length)
    for cap in range(x.shape[0] // length):
        rows = slice(cap * length, (cap + 1) * length)
        for group in range(GROUPS):
            lo = group * LANES
            query = qkv_ref[rows, lo : lo + LANES] * SCALE
            key = qkv_ref[rows, width + lo : width + lo + LANES]
            value = qkv_ref[rows, 2 * width + lo : 2 * width + lo + LANES]
            scores = jnp.where(causal, dot_nt(key, spread(query, mask)), NEG)
            exponent = jnp.exp(scores - jnp.max(scores, axis=0, keepdims=True))
            probs = exponent / jnp.sum(exponent, axis=0, keepdims=True)
            full = dot_tn(probs.astype(BF16), value)
            att_ref[rows, lo : lo + LANES] = gather_heads(full).astype(BF16)
    hidden = x + dot(att_ref[...], out_mat[...])
    hidden_ref[...] = hidden
    unit, _ = normalize(hidden)
    normed = (unit * gain_two[...] + shift_two[...]).astype(BF16)
    query_ref[...] = (dot(normed, query_mat[...]).astype(BF16).astype(F32) * SCALE).astype(BF16)


def whole(shape):
    zeros = (0,) * len(shape)
    return pl.BlockSpec(shape, lambda *_: zeros)


def token_start(tokens, gain_one, shift_one, qkv_mat, out_mat, gain_two, shift_two, query_mat, length):
    rows, width = tokens.shape
    tile = min(256, rows)
    row_block = lambda cols: pl.BlockSpec((tile, cols), lambda i: (i, 0))
    return pl.pallas_call(
        functools.partial(token_start_body, length=length),
        grid=(rows // tile,),
        in_specs=[
            row_block(width), whole((1, width)), whole((1, width)), whole(qkv_mat.shape),
            whole(out_mat.shape), whole((1, width)), whole((1, width)), whole(query_mat.shape),
        ],
        out_specs=[row_block(3 * width), row_block(width), row_block(width), row_block(width)],
        out_shape=[
            jax.ShapeDtypeStruct((rows, 3 * width), BF16),
            jax.ShapeDtypeStruct((rows, width), BF16),
            jax.ShapeDtypeStruct((rows, width), F32),
            jax.ShapeDtypeStruct((rows, width), BF16),
        ],
        compiler_params=pltpu.CompilerParams(vmem_limit_bytes=VMEM_LIMIT),
        name="token_start",
    )(tokens, gain_one, shift_one, qkv_mat, out_mat, gain_two, shift_two, query_mat)


def cross_start_body(valid_ref, img_ref, kv_mat, query_ref, kv_ref, att_ref, lse_ref, *, short):
    cap = pl.program_id(0)
    valid = valid_ref[cap]
    width = query_ref.shape[2]
    slots = img_ref.shape[1]

    def work(count):
        kv_ref[0, :count] = dot(img_ref[0, :count], kv_mat[...]).astype(BF16)
        mask = same_head()
        inside = iota((count, LANES), 0) < valid
        for group in range(GROUPS):
            lo = group * LANES
            key = kv_ref[0, :count, lo : lo + LANES]
            value = kv_ref[0, :count, width + lo : width + lo + LANES]
            scores = dot_nt(key, spread(query_ref[0, :, lo : lo + LANES], mask))
            scores = jnp.where(inside, scores, NEG)
            peak = jnp.max(scores, axis=0, keepdims=True)
            exponent = jnp.where(inside, jnp.exp(scores - peak), 0.0)
            total = jnp.sum(exponent, axis=0, keepdims=True)
            probs = (exponent * (1.0 / total)).astype(BF16)
            att_ref[0, :, lo : lo + LANES] = gather_heads(dot_tn(probs, value)).astype(BF16)
            lse_ref[0, group : group + 1] = peak + jnp.log(total)

    @pl.when(valid <= 0)
    def _():
        att_ref[...] = jnp.zeros_like(att_ref)
        lse_ref[...] = jnp.full_like(lse_ref, NEG)

    if short < slots:
        pl.when((valid > 0) & (valid <= short))(lambda: work(short))
        pl.when(valid > short)(lambda: work(slots))
    else:
        pl.when(valid > 0)(lambda: work(slots))


def cross_start(valid, images, kv_mat, queries, short):
    caps, slots, width = images.shape
    length = queries.shape[1]
    block = lambda *shape: pl.BlockSpec((1,) + shape, lambda i, *_: (i, 0, 0))
    return pl.pallas_call(
        functools.partial(cross_start_body, short=short),
        grid_spec=pltpu.PrefetchScalarGridSpec(
            num_scalar_prefetch=1,
            grid=(caps,),
            in_specs=[block(slots, width), whole(kv_mat.shape), block(length, width)],
            out_specs=[block(slots, 2 * width), block(length, width), block(GROUPS, LANES)],
        ),
        out_shape=[
            jax.ShapeDtypeStruct((caps, slots, 2 * width), BF16),
            jax.ShapeDtypeStruct((caps, length, width), BF16),
            jax.ShapeDtypeStruct((caps, GROUPS, LANES), F32),
        ],
        compiler_params=pltpu.CompilerParams(vmem_limit_bytes=VMEM_LIMIT),
        name="cross_start",
    )(valid, images, kv_mat, queries)


def feed_body(
    side_ref, att_one, lse_one, att_two, lse_two, hidden_ref, cot_ref, cross_mat, gain_ref,
    shift_ref, up_mat, down_mat,
    out_ref, grad_two_ref, grad_att_ref, lse_ref, delta_ref, up_mine, up_send, down_mine,
    down_send, cross_mine, cross_send, gain_grad, shift_grad,
    att_full, att_low, hidden_two, normed_ref, acc_out, acc_grad, *, length, tile
):
    step = pl.program_id(0)
    steps = pl.num_programs(0)
    side = side_ref[0]
    rows, width = hidden_ref.shape
    captions = rows // length
    tiles = rows // tile
    half = width // 2

    @pl.when(step == 0)
    def _():
        mask_low = same_head().astype(BF16)

        def one_caption(cap, carry):
            span = pl.ds(pl.multiple_of(cap * length, length), length)
            for group in range(GROUPS):
                lo = group * LANES
                first = lse_one[cap, group : group + 1]
                second = lse_two[cap, group : group + 1]
                peak = jnp.maximum(first, second)
                lse = peak + jnp.log(jnp.exp(first - peak) + jnp.exp(second - peak))
                lse_ref[cap, group : group + 1] = lse
                weight_one = lanes_to_rows(jnp.exp(first - lse), mask_low)
                weight_two = lanes_to_rows(jnp.exp(second - lse), mask_low)
                mixed = (
                    weight_one * att_one[span, lo : lo + LANES].astype(F32)
                    + weight_two * att_two[span, lo : lo + LANES].astype(F32)
                )
                att_full[span, lo : lo + LANES] = mixed
                att_low[span, lo : lo + LANES] = mixed.astype(BF16)
            return carry

        lax.fori_loop(0, captions, one_caption, 0)

        def one_tile(index, carry):
            span = pl.ds(pl.multiple_of(index * tile, tile), tile)
            two = hidden_ref[span, :] + dot(att_low[span, :], cross_mat[...])
            hidden_two[span, :] = two
            unit, _ = normalize(two)
            normed_ref[span, :] = (unit * gain_ref[...] + shift_ref[...]).astype(BF16)
            acc_out[span, :] = two
            acc_grad[span, :] = jnp.zeros_like(two)
            return carry

        lax.fori_loop(0, tiles, one_tile, 0)

    pre = dot(normed_ref[...], up_mat[...])
    cdf = 0.5 * (1.0 + lax.erf(pre * 0.7071067811865476))
    act = (pre * cdf).astype(BF16)
    acc_out[...] += dot(act, down_mat[...])
    cot = cot_ref[...]
    density = jnp.exp(-0.5 * pre * pre) * 0.3989422804014327
    grad_up = (dot_nt(cot, down_mat[...]) * (cdf + pre * density)).astype(BF16)
    acc_grad[...] += dot_nt(grad_up, up_mat[...])
    grad_down = dot_tn(act, cot).astype(BF16)
    grad_w = dot_tn(normed_ref[...], grad_up).astype(BF16)
    in_mine = (step >= steps // 2) == (side == 1)

    @pl.when(in_mine)
    def _():
        up_mine[...] = grad_w

    @pl.when(jnp.logical_not(in_mine))
    def _():
        up_send[...] = grad_w

    @pl.when(side == 0)
    def _():
        down_mine[...] = grad_down[:, :half]
        down_send[...] = grad_down[:, half:]

    @pl.when(side == 1)
    def _():
        down_mine[...] = grad_down[:, half:]
        down_send[...] = grad_down[:, :half]

    @pl.when(step == steps - 1)
    def _():
        mask_low = same_head().astype(BF16)
        gain_grad[...] = jnp.zeros_like(gain_grad)
        shift_grad[...] = jnp.zeros_like(shift_grad)

        def one_tile(index, carry):
            span = pl.ds(pl.multiple_of(index * tile, tile), tile)
            out_ref[span, :] = acc_out[span, :].astype(BF16)
            unit, inverse = normalize(hidden_two[span, :])
            grad = acc_grad[span, :]
            gain_grad[...] += jnp.sum(grad * unit, axis=0, keepdims=True)
            shift_grad[...] += jnp.sum(grad, axis=0, keepdims=True)
            two = cot_ref[span, :].astype(F32) + norm_back(grad, gain_ref[...], unit, inverse)
            grad_two_ref[span, :] = two
            low = two.astype(BF16)
            normed_ref[span, :] = low
            grad_att_ref[span, :] = dot_nt(low, cross_mat[...]).astype(BF16)
            return carry

        lax.fori_loop(0, tiles, one_tile, 0)
        grad_cross = dot_tn(att_low[...], normed_ref[...]).astype(BF16)

        @pl.when(side == 0)
        def _():
            cross_mine[...] = grad_cross[:, :half]
            cross_send[...] = grad_cross[:, half:]

        @pl.when(side == 1)
        def _():
            cross_mine[...] = grad_cross[:, half:]
            cross_send[...] = grad_cross[:, :half]

        def one_caption(cap, carry):
            span = pl.ds(pl.multiple_of(cap * length, length), length)
            for group in range(GROUPS):
                lo = group * LANES
                product = grad_att_ref[span, lo : lo + LANES].astype(F32) * att_full[span, lo : lo + LANES]
                delta_ref[cap, group : group + 1] = rows_to_lanes(product, mask_low)
            return carry

        lax.fori_loop(0, captions, one_caption, 0)


def feed(side, att_one, lse_one, att_two, lse_two, hidden, cot, cross_mat, gain, shift, up_mat, down_mat, length):
    rows, width = hidden.shape
    captions = rows // length
    units = up_mat.shape[1]
    chunk = 512
    steps = units // chunk
    middle = steps // 2
    tile = min(256, rows)
    half = width // 2
    stat = (captions, GROUPS, LANES)
    sds = jax.ShapeDtypeStruct
    clip = lambda v: jnp.minimum(jnp.maximum(v, 0), middle - 1)
    mine_map = lambda i, side: (0, clip(i - middle * side[0]))
    send_map = lambda i, side: (0, clip(i - middle * (1 - side[0])))
    return pl.pallas_call(
        functools.partial(feed_body, length=length, tile=tile),
        grid_spec=pltpu.PrefetchScalarGridSpec(
            num_scalar_prefetch=1,
            grid=(steps,),
            in_specs=[
                whole((rows, width)), whole(stat), whole((rows, width)), whole(stat),
                whole((rows, width)), whole((rows, width)), whole((width, width)),
                whole((1, width)), whole((1, width)),
                pl.BlockSpec((width, chunk), lambda i, *_: (0, i)),
                pl.BlockSpec((chunk, width), lambda i, *_: (i, 0)),
            ],
            out_specs=[
                whole((rows, width)), whole((rows, width)), whole((rows, width)), whole(stat),
                whole(stat),
                pl.BlockSpec((width, chunk), mine_map), pl.BlockSpec((width, chunk), send_map),
                pl.BlockSpec((chunk, half), lambda i, *_: (i, 0)),
                pl.BlockSpec((chunk, half), lambda i, *_: (i, 0)),
                whole((width, half)), whole((width, half)),
                whole((1, width)), whole((1, width)),
            ],
            scratch_shapes=[
                pltpu.VMEM((rows, width), F32), pltpu.VMEM((rows, width), BF16),
                pltpu.VMEM((rows, width), F32), pltpu.VMEM((rows, width), BF16),
                pltpu.VMEM((rows, width), F32), pltpu.VMEM((rows, width), F32),
            ],
        ),
        out_shape=[
            sds((rows, width), BF16), sds((rows, width), F32), sds((rows, width), BF16),
            sds(stat, F32), sds(stat, F32),
            sds((width, units // 2), BF16), sds((width, units // 2), BF16),
            sds((units, half), BF16), sds((units, half), BF16),
            sds((width, half), BF16), sds((width, half), BF16),
            sds((1, width), F32), sds((1, width), F32),
        ],
        compiler_params=pltpu.CompilerParams(vmem_limit_bytes=VMEM_LIMIT),
        name="feed",
    )(side, att_one, lse_one, att_two, lse_two, hidden, cot, cross_mat, gain, shift, up_mat, down_mat)


def cross_back_body(
    valid_ref, kv_ref, query_ref, grad_ref, lse_ref, delta_ref, kv_mat,
    grad_query_ref, grad_kv_ref, grad_img_ref, *, short
):
    cap = pl.program_id(0)
    valid = valid_ref[cap]
    width = query_ref.shape[2]
    slots = kv_ref.shape[1]

    def work(count):
        mask = same_head()
        inside = iota((count, LANES), 0) < valid
        for group in range(GROUPS):
            lo = group * LANES
            key = kv_ref[0, :count, lo : lo + LANES]
            value = kv_ref[0, :count, width + lo : width + lo + LANES]
            query = spread(query_ref[0, :, lo : lo + LANES], mask)
            grad = spread(grad_ref[0, :, lo : lo + LANES], mask)
            scores = dot_nt(key, query)
            probs = jnp.where(inside, jnp.exp(scores - lse_ref[0, group : group + 1]), 0.0)
            grad_probs = dot_nt(value, grad)
            grad_scores = (probs * (grad_probs - delta_ref[0, group : group + 1])).astype(BF16)
            back = gather_heads(dot_tn(grad_scores, key)) * SCALE
            grad_query_ref[0, :, lo : lo + LANES] = back.astype(BF16)
            grad_kv_ref[0, :count, lo : lo + LANES] = dot(grad_scores, query).astype(BF16)
            grad_kv_ref[0, :count, width + lo : width + lo + LANES] = dot(
                probs.astype(BF16), grad
            ).astype(BF16)
        grad_img_ref[0, :count] = dot_nt(grad_kv_ref[0, :count], kv_mat[...]).astype(BF16)
        if count < slots:
            grad_kv_ref[0, count:] = jnp.zeros((slots - count, 2 * width), BF16)
            grad_img_ref[0, count:] = jnp.zeros((slots - count, width), BF16)

    @pl.when(valid <= 0)
    def _():
        grad_query_ref[...] = jnp.zeros_like(grad_query_ref)
        grad_kv_ref[...] = jnp.zeros_like(grad_kv_ref)
        grad_img_ref[...] = jnp.zeros_like(grad_img_ref)

    if short < slots:
        pl.when((valid > 0) & (valid <= short))(lambda: work(short))
        pl.when(valid > short)(lambda: work(slots))
    else:
        pl.when(valid > 0)(lambda: work(slots))


def cross_back(valid, kv, queries, grads, lse, delta, kv_mat, short):
    caps, slots, double = kv.shape
    width = double // 2
    length = queries.shape[1]
    block = lambda *shape: pl.BlockSpec((1,) + shape, lambda i, *_: (i, 0, 0))
    sds = jax.ShapeDtypeStruct
    return pl.pallas_call(
        functools.partial(cross_back_body, short=short),
        grid_spec=pltpu.PrefetchScalarGridSpec(
            num_scalar_prefetch=1,
            grid=(caps,),
            in_specs=[
                block(slots, double), block(length, width), block(length, width),
                block(GROUPS, LANES), block(GROUPS, LANES), whole(kv_mat.shape),
            ],
            out_specs=[block(length, width), block(slots, double), block(slots, width)],
        ),
        out_shape=[
            sds((caps, length, width), BF16), sds((caps, slots, double), BF16),
            sds((caps, slots, width), BF16),
        ],
        compiler_params=pltpu.CompilerParams(vmem_limit_bytes=VMEM_LIMIT),
        name="cross_back",
    )(valid, kv, queries, grads, lse, delta, kv_mat)


def image_weight_body(side_ref, img_ref, grad_ref, mine_ref, send_ref, acc_ref):
    step = pl.program_id(0)

    @pl.when(step == 0)
    def _():
        acc_ref[...] = jnp.zeros_like(acc_ref)

    acc_ref[...] += dot_tn(img_ref[...], grad_ref[...])

    @pl.when(step == pl.num_programs(0) - 1)
    def _():
        half = acc_ref.shape[1] // 2
        side = side_ref[0]

        @pl.when(side == 0)
        def _():
            mine_ref[...] = acc_ref[:, :half].astype(BF16)
            send_ref[...] = acc_ref[:, half:].astype(BF16)

        @pl.when(side == 1)
        def _():
            mine_ref[...] = acc_ref[:, half:].astype(BF16)
            send_ref[...] = acc_ref[:, :half].astype(BF16)


def image_weight(side, images, grads):
    rows, width = images.shape
    double = grads.shape[1]
    tile = 512 if rows % 512 == 0 else rows // 4
    sds = jax.ShapeDtypeStruct
    return pl.pallas_call(
        image_weight_body,
        grid_spec=pltpu.PrefetchScalarGridSpec(
            num_scalar_prefetch=1,
            grid=(rows // tile,),
            in_specs=[
                pl.BlockSpec((tile, width), lambda i, *_: (i, 0)),
                pl.BlockSpec((tile, double), lambda i, *_: (i, 0)),
            ],
            out_specs=[whole((width, double // 2)), whole((width, double // 2))],
            scratch_shapes=[pltpu.VMEM((width, double), F32)],
        ),
        out_shape=[sds((width, double // 2), BF16)] * 2,
        compiler_params=pltpu.CompilerParams(vmem_limit_bytes=VMEM_LIMIT),
        name="image_weight",
    )(side, images, grads)


def token_end_body(
    side_ref, back_one, back_two, hidden_ref, grad_two_ref, att_ref, qkv_ref, tok_ref,
    gain_one, shift_one, qkv_mat, out_mat, gain_two, shift_two, query_mat,
    grad_tok_ref, qkv_mine, qkv_send, out_mine, out_send, query_mine, query_send, gains_ref,
    grad_qkv_ref, acc_qkv, acc_out, acc_query, *, length
):
    step = pl.program_id(0)

    @pl.when(step == 0)
    def _():
        acc_qkv[...] = jnp.zeros_like(acc_qkv)
        acc_out[...] = jnp.zeros_like(acc_out)
        acc_query[...] = jnp.zeros_like(acc_query)
        gains_ref[...] = jnp.zeros_like(gains_ref)

    back = (back_one[...].astype(F32) + back_two[...].astype(F32)).astype(BF16)
    unit, inverse = normalize(hidden_ref[...])
    normed = (unit * gain_two[...] + shift_two[...]).astype(BF16)
    acc_query[...] += dot_tn(normed, back)
    grad = dot_nt(back, query_mat[...])
    gains_ref[2:3] += jnp.sum(grad * unit, axis=0, keepdims=True)
    gains_ref[3:4] += jnp.sum(grad, axis=0, keepdims=True)
    grad_one = grad_two_ref[...] + norm_back(grad, gain_two[...], unit, inverse)
    low = grad_one.astype(BF16)
    acc_out[...] += dot_tn(att_ref[...], low)
    grad_att = dot_nt(low, out_mat[...]).astype(BF16)
    rows, width = grad_att.shape
    mask = same_head()
    causal = causal_mask(length)
    for cap in range(rows // length):
        span = slice(cap * length, (cap + 1) * length)
        for group in range(GROUPS):
            lo = group * LANES
            query = spread(qkv_ref[span, lo : lo + LANES] * SCALE, mask)
            key = qkv_ref[span, width + lo : width + lo + LANES]
            value = qkv_ref[span, 2 * width + lo : 2 * width + lo + LANES]
            cot = spread(grad_att[span, lo : lo + LANES], mask)
            scores = jnp.where(causal, dot_nt(key, query), NEG)
            exponent = jnp.exp(scores - jnp.max(scores, axis=0, keepdims=True))
            probs = exponent / jnp.sum(exponent, axis=0, keepdims=True)
            grad_probs = dot_nt(value, cot)
            mean = jnp.sum(probs * grad_probs, axis=0, keepdims=True)
            grad_scores = (probs * (grad_probs - mean)).astype(BF16)
            grad_q = gather_heads(dot_tn(grad_scores, key)) * SCALE
            grad_qkv_ref[span, lo : lo + LANES] = grad_q.astype(BF16)
            grad_qkv_ref[span, width + lo : width + lo + LANES] = dot(grad_scores, query).astype(BF16)
            grad_qkv_ref[span, 2 * width + lo : 2 * width + lo + LANES] = dot(
                probs.astype(BF16), cot
            ).astype(BF16)
    unit, inverse = normalize(tok_ref[...].astype(F32))
    normed = (unit * gain_one[...] + shift_one[...]).astype(BF16)
    acc_qkv[...] += dot_tn(normed, grad_qkv_ref[...])
    grad = dot_nt(grad_qkv_ref[...], qkv_mat[...])
    gains_ref[0:1] += jnp.sum(grad * unit, axis=0, keepdims=True)
    gains_ref[1:2] += jnp.sum(grad, axis=0, keepdims=True)
    grad_tok_ref[...] = (grad_one + norm_back(grad, gain_one[...], unit, inverse)).astype(BF16)

    @pl.when(step == pl.num_programs(0) - 1)
    def _():
        for acc, mine, send in (
            (acc_qkv, qkv_mine, qkv_send),
            (acc_out, out_mine, out_send),
            (acc_query, query_mine, query_send),
        ):
            half = acc.shape[1] // 2

            @pl.when(side_ref[0] == 0)
            def _():
                mine[...] = acc[:, :half].astype(BF16)
                send[...] = acc[:, half:].astype(BF16)

            @pl.when(side_ref[0] == 1)
            def _():
                mine[...] = acc[:, half:].astype(BF16)
                send[...] = acc[:, :half].astype(BF16)


def token_end(
    side, back_one, back_two, hidden, grad_two, att, qkv, tokens,
    gain_one, shift_one, qkv_mat, out_mat, gain_two, shift_two, query_mat, length
):
    rows, width = tokens.shape
    tile = min(256, rows)
    row_block = lambda cols: pl.BlockSpec((tile, cols), lambda i, *_: (i, 0))
    sds = jax.ShapeDtypeStruct
    halves = [(width, 3 * width // 2)] * 2 + [(width, width // 2)] * 4
    return pl.pallas_call(
        functools.partial(token_end_body, length=length),
        grid_spec=pltpu.PrefetchScalarGridSpec(
            num_scalar_prefetch=1,
            grid=(rows // tile,),
            in_specs=[
                row_block(width), row_block(width), row_block(width), row_block(width),
                row_block(width), row_block(3 * width), row_block(width),
                whole((1, width)), whole((1, width)), whole(qkv_mat.shape), whole(out_mat.shape),
                whole((1, width)), whole((1, width)), whole(query_mat.shape),
            ],
            out_specs=[row_block(width)] + [whole(s) for s in halves] + [whole((4, width))],
            scratch_shapes=[
                pltpu.VMEM((tile, 3 * width), BF16), pltpu.VMEM((width, 3 * width), F32),
                pltpu.VMEM((width, width), F32), pltpu.VMEM((width, width), F32),
            ],
        ),
        out_shape=[sds((rows, width), BF16)] + [sds(s, BF16) for s in halves] + [sds((4, width), F32)],
        compiler_params=pltpu.CompilerParams(vmem_limit_bytes=VMEM_LIMIT),
        name="token_end",
    )(
        side, back_one, back_two, hidden, grad_two, att, qkv, tokens,
        gain_one, shift_one, qkv_mat, out_mat, gain_two, shift_two, query_mat,
    )


def add_low(first, second):
    return (first.astype(F32) + second.astype(F32)).astype(BF16)


def exchange(value, axis, bit, size):
    return lax.ppermute(value, axis, [(i, i ^ bit) for i in range(size)])


def reduce_blocks(mine, send, order, me, size):
    total = add_low(mine, exchange(send, "kv", 1, 2))
    bits = size.bit_length() - 1
    rows = total.shape[0] // size
    total = total.reshape((2,) * bits + (rows, total.shape[1]))
    left = list(range(bits))[::-1]
    for bit in order:
        axis = left.index(bit)
        own = (me >> bit) & 1
        keep = lax.dynamic_index_in_dim(total, own, axis, False)
        away = lax.dynamic_index_in_dim(total, 1 - own, axis, False)
        total = add_low(keep, exchange(away, "dp", 1 << bit, size))
        left.remove(bit)
    return total.astype(F32)


def body(
    tokens, images, image_counts, cotangent, norm1_gain, norm1_shift, self_qkv, self_out,
    norm2_gain, norm2_shift, cross_q, cross_kv, cross_out, norm3_gain, norm3_shift, w_up, w_down,
):
    captions, length, width = tokens.shape
    caps, slots, _ = images.shape
    side = lax.axis_index("kv")
    me = lax.axis_index("dp")
    groups = lax.axis_size("dp")
    side_arr = side.reshape(1)
    row = lambda v: v.reshape(1, width)
    tok = tokens.reshape(captions * length, width)
    cot = cotangent.reshape(captions * length, width)
    short = -(-SHORT // 16) * 16
    valid = jnp.clip(image_counts - side * slots, 0, slots)
    swap = lambda v: exchange(v, "kv", 1, 2)

    qkv, att, hidden, query = token_start(
        tok, row(norm1_gain), row(norm1_shift), self_qkv, self_out, row(norm2_gain),
        row(norm2_shift), cross_q, length,
    )

    def both(own):
        other = swap(own)
        first = jnp.where(side == 0, own, other)
        second = jnp.where(side == 0, other, own)
        return jnp.concatenate([first, second], axis=0)

    def own_part(array):
        return lax.dynamic_slice_in_dim(array, side * captions, captions, 0)

    def other_part(array):
        return lax.dynamic_slice_in_dim(array, (1 - side) * captions, captions, 0)

    queries = both(query.reshape(captions, length, width))
    kv, part, lse_part = cross_start(valid, images, cross_kv, queries, short)
    flat = lambda v: v.reshape(captions * length, width)
    (
        layer_out, grad_two, grad_att, lse, delta, up_mine, up_send, down_mine, down_send,
        cross_mine, cross_send, gain3, shift3,
    ) = feed(
        side_arr, flat(own_part(part)), own_part(lse_part), flat(swap(other_part(part))),
        swap(other_part(lse_part)), hidden, cot, cross_out, row(norm3_gain), row(norm3_shift),
        w_up, w_down, length,
    )
    bits = groups.bit_length() - 1
    turn = lambda start: [(start + i) % bits for i in range(bits)]
    w_up_grad = reduce_blocks(up_mine, up_send, turn(0), me, groups)
    down_grad = reduce_blocks(down_mine, down_send, turn(bits // 2), me, groups)
    cross_out_grad = reduce_blocks(cross_mine, cross_send, turn(bits // 4), me, groups)

    grads = both(grad_att.reshape(captions, length, width))
    back, grad_kv, images_grad = cross_back(
        valid, kv, queries, grads, both(lse), both(delta), cross_kv, short
    )
    kv_mine, kv_send = image_weight(
        side_arr, images.reshape(caps * slots, width), grad_kv.reshape(caps * slots, 2 * width)
    )
    cross_kv_grad = reduce_blocks(kv_mine, kv_send, turn(0), me, groups)
    (
        tokens_grad, qkv_mine, qkv_send, out_mine, out_send, query_mine, query_send, gains,
    ) = token_end(
        side_arr, flat(own_part(back)), flat(swap(other_part(back))), hidden, grad_two, att, qkv,
        tok, row(norm1_gain), row(norm1_shift), self_qkv, self_out, row(norm2_gain),
        row(norm2_shift), cross_q, length,
    )
    self_qkv_grad = reduce_blocks(qkv_mine, qkv_send, turn(0), me, groups)
    self_out_grad = reduce_blocks(out_mine, out_send, turn(bits // 2), me, groups)
    cross_q_grad = reduce_blocks(query_mine, query_send, turn(bits // 4), me, groups)
    gains = jnp.concatenate([gains, gain3, shift3], axis=0)
    gains = gains + swap(gains)
    gains = lax.dynamic_slice_in_dim(gains, side * (width // 2), width // 2, 1)
    for bit in range(bits):
        gains = gains + exchange(gains, "dp", 1 << bit, groups)
    return (
        layer_out.reshape(captions, length, width),
        tokens_grad.reshape(captions, length, width),
        images_grad,
        gains[0], gains[1], self_qkv_grad, self_out_grad, gains[2], gains[3], cross_q_grad,
        cross_kv_grad, cross_out_grad, gains[4], gains[5], w_up_grad, down_grad,
    )


def solution(mesh):
    return jax.shard_map(
        body,
        mesh=mesh,
        in_specs=(
            P(("dp", "kv"), None, None), P("dp", "kv", None), P("dp"), P(("dp", "kv"), None, None),
        ) + (P(),) * 13,
        out_specs=(
            P(("dp", "kv"), None, None), P(("dp", "kv"), None, None), P("dp", "kv", None),
            P("kv"), P("kv"), P("dp", "kv"), P("dp", "kv"), P("kv"), P("kv"), P("dp", "kv"),
            P("dp", "kv"), P("dp", "kv"), P("kv"), P("kv"), P("dp", "kv"), P("dp", "kv"),
        ),
        check_vma=False,
    )
```

```python
import functools

import jax
import jax.numpy as jnp
from jax import lax
from jax.experimental import pallas as pl
from jax.experimental.pallas import tpu as pltpu
from jax.sharding import PartitionSpec as P

HEADS = 12
HEAD_DIM = 64
SHORT = 196
LANES = 256
PACK = LANES // HEAD_DIM
GROUPS = HEADS // PACK
SCALE = HEAD_DIM ** (-0.5)
NEG = -1e30
F32 = jnp.float32
BF16 = jnp.bfloat16
VMEM_LIMIT = 60 * 1024 * 1024


def dot(a, b):
    return jnp.dot(a, b, preferred_element_type=F32)


def dot_nt(a, b):
    return lax.dot_general(a, b, (((1,), (1,)), ((), ())), preferred_element_type=F32)


def dot_tn(a, b):
    return lax.dot_general(a, b, (((0,), (0,)), ((), ())), preferred_element_type=F32)


def normalize(values):
    centered = values - jnp.mean(values, axis=-1, keepdims=True)
    inverse = lax.rsqrt(jnp.mean(centered * centered, axis=-1, keepdims=True) + 1e-05)
    return centered * inverse, inverse


def norm_back(grad, gain, unit, inverse):
    scaled = grad * gain
    mean_one = jnp.mean(scaled, axis=-1, keepdims=True)
    mean_two = jnp.mean(scaled * unit, axis=-1, keepdims=True)
    return (scaled - mean_one - unit * mean_two) * inverse


def as_row(ref):
    return ref[...].reshape(1, ref.shape[0])


def iota(shape, dim):
    return lax.broadcasted_iota(jnp.int32, shape, dim)


def same_head():
    shape = (LANES, LANES)
    return (iota(shape, 0) // HEAD_DIM) == (iota(shape, 1) // HEAD_DIM)


def spread(rows, mask):
    stacked = jnp.concatenate([rows] * PACK, axis=0)
    return jnp.where(mask, stacked, jnp.zeros_like(stacked))


def gather_heads(full):
    count = full.shape[0] // PACK
    head = iota((count, LANES), 1) // HEAD_DIM
    out = full[:count]
    for index in range(1, PACK):
        out = jnp.where(head == index, full[index * count : (index + 1) * count], out)
    return out


def split_two(value):
    high = value.astype(BF16)
    return high, (value - high.astype(F32)).astype(BF16)


def lanes_to_rows(row, mask_low):
    shape = (HEAD_DIM, LANES)
    pick = iota(shape, 0) == (iota(shape, 1) % HEAD_DIM)
    high, low = split_two(jnp.where(pick, row, 0.0))
    return dot(high, mask_low) + dot(low, mask_low)


def rows_to_lanes(rows, mask_low):
    high, low = split_two(rows)
    summed = dot(high, mask_low) + dot(low, mask_low)
    shape = (HEAD_DIM, LANES)
    pick = iota(shape, 0) == (iota(shape, 1) % HEAD_DIM)
    return jnp.sum(jnp.where(pick, summed, 0.0), axis=0, keepdims=True)


def lane_slice(group):
    return slice(group * LANES, (group + 1) * LANES)


def causal_mask(length):
    shape = (length, LANES)
    return iota(shape, 0) <= (iota(shape, 1) % HEAD_DIM)


def token_start_body(
    tok_ref, gain_one, shift_one, qkv_mat, out_mat, gain_two, shift_two, query_mat,
    qkv_ref, att_ref, hidden_ref, query_ref, *, length
):
    x = tok_ref[...].astype(F32)
    unit, _ = normalize(x)
    normed = (unit * as_row(gain_one) + as_row(shift_one)).astype(BF16)
    width = x.shape[1]
    qkv_ref[...] = dot(normed, qkv_mat[...]).astype(BF16)
    mask = same_head()
    causal = causal_mask(length)
    for cap in range(x.shape[0] // length):
        rows = slice(cap * length, (cap + 1) * length)
        for group in range(GROUPS):
            lo = group * LANES
            query = qkv_ref[rows, lo : lo + LANES] * SCALE
            key = qkv_ref[rows, width + lo : width + lo + LANES]
            value = qkv_ref[rows, 2 * width + lo : 2 * width + lo + LANES]
            scores = jnp.where(causal, dot_nt(key, spread(query, mask)), NEG)
            exponent = jnp.exp(scores - jnp.max(scores, axis=0, keepdims=True))
            probs = exponent / jnp.sum(exponent, axis=0, keepdims=True)
            full = dot_tn(probs.astype(BF16), value)
            att_ref[rows, lo : lo + LANES] = gather_heads(full).astype(BF16)
    hidden = x + dot(att_ref[...], out_mat[...])
    hidden_ref[...] = hidden
    unit, _ = normalize(hidden)
    normed = (unit * as_row(gain_two) + as_row(shift_two)).astype(BF16)
    query_ref[...] = (dot(normed, query_mat[...]).astype(BF16).astype(F32) * SCALE).astype(BF16)


def whole(shape):
    zeros = (0,) * len(shape)
    return pl.BlockSpec(shape, lambda *_: zeros)


def token_start(tokens, gain_one, shift_one, qkv_mat, out_mat, gain_two, shift_two, query_mat, length):
    rows, width = tokens.shape
    tile = min(256, rows)
    row_block = lambda cols: pl.BlockSpec((tile, cols), lambda i: (i, 0))
    return pl.pallas_call(
        functools.partial(token_start_body, length=length),
        grid=(rows // tile,),
        in_specs=[
            row_block(width), whole((width,)), whole((width,)), whole(qkv_mat.shape),
            whole(out_mat.shape), whole((width,)), whole((width,)), whole(query_mat.shape),
        ],
        out_specs=[row_block(3 * width), row_block(width), row_block(width), row_block(width)],
        out_shape=[
            jax.ShapeDtypeStruct((rows, 3 * width), BF16),
            jax.ShapeDtypeStruct((rows, width), BF16),
            jax.ShapeDtypeStruct((rows, width), F32),
            jax.ShapeDtypeStruct((rows, width), BF16),
        ],
        compiler_params=pltpu.CompilerParams(vmem_limit_bytes=VMEM_LIMIT),
        name="token_start",
    )(tokens, gain_one, shift_one, qkv_mat, out_mat, gain_two, shift_two, query_mat)


def cross_start_body(valid_ref, img_ref, kv_mat, query_ref, kv_ref, att_ref, lse_ref, *, short):
    cap = pl.program_id(0)
    valid = valid_ref[cap]
    width = query_ref.shape[2]
    slots = img_ref.shape[1]

    def work(count):
        kv_ref[0, :count] = dot(img_ref[0, :count], kv_mat[...]).astype(BF16)
        mask = same_head()
        inside = iota((count, LANES), 0) < valid
        for group in range(GROUPS):
            lo = group * LANES
            key = kv_ref[0, :count, lo : lo + LANES]
            value = kv_ref[0, :count, width + lo : width + lo + LANES]
            scores = dot_nt(key, spread(query_ref[0, :, lo : lo + LANES], mask))
            scores = jnp.where(inside, scores, NEG)
            peak = jnp.max(scores, axis=0, keepdims=True)
            exponent = jnp.where(inside, jnp.exp(scores - peak), 0.0)
            total = jnp.sum(exponent, axis=0, keepdims=True)
            probs = (exponent * (1.0 / total)).astype(BF16)
            att_ref[0, :, lo : lo + LANES] = gather_heads(dot_tn(probs, value)).astype(BF16)
            lse_ref[0, group : group + 1] = peak + jnp.log(total)

    @pl.when(valid <= 0)
    def _():
        att_ref[...] = jnp.zeros_like(att_ref)
        lse_ref[...] = jnp.full_like(lse_ref, NEG)

    if short < slots:
        pl.when((valid > 0) & (valid <= short))(lambda: work(short))
        pl.when(valid > short)(lambda: work(slots))
    else:
        pl.when(valid > 0)(lambda: work(slots))


def cross_start(valid, images, kv_mat, queries, short):
    caps, slots, width = images.shape
    length = queries.shape[1]
    block = lambda *shape: pl.BlockSpec((1,) + shape, lambda i, *_: (i, 0, 0))
    return pl.pallas_call(
        functools.partial(cross_start_body, short=short),
        grid_spec=pltpu.PrefetchScalarGridSpec(
            num_scalar_prefetch=1,
            grid=(caps,),
            in_specs=[block(slots, width), whole(kv_mat.shape), block(length, width)],
            out_specs=[block(slots, 2 * width), block(length, width), block(GROUPS, LANES)],
        ),
        out_shape=[
            jax.ShapeDtypeStruct((caps, slots, 2 * width), BF16),
            jax.ShapeDtypeStruct((caps, length, width), BF16),
            jax.ShapeDtypeStruct((caps, GROUPS, LANES), F32),
        ],
        compiler_params=pltpu.CompilerParams(vmem_limit_bytes=VMEM_LIMIT),
        name="cross_start",
    )(valid, images, kv_mat, queries)


def feed_body(
    side_ref, att_one, lse_one, att_two, lse_two, hidden_ref, cot_ref, cross_mat, gain_ref,
    shift_ref, up_mat, down_mat,
    out_ref, grad_two_ref, grad_att_ref, lse_ref, delta_ref, up_mine, up_send, down_mine,
    down_send, cross_mine, cross_send, gain_grad, shift_grad,
    att_full, att_low, hidden_two, normed_ref, acc_out, acc_grad, *, length, tile
):
    step = pl.program_id(0)
    steps = pl.num_programs(0)
    side = side_ref[0]
    rows, width = hidden_ref.shape
    captions = rows // length
    tiles = rows // tile
    half = width // 2

    @pl.when(step == 0)
    def _():
        mask_low = same_head().astype(BF16)

        def one_caption(cap, carry):
            span = pl.ds(pl.multiple_of(cap * length, length), length)
            for group in range(GROUPS):
                lo = group * LANES
                first = lse_one[cap, group : group + 1]
                second = lse_two[cap, group : group + 1]
                peak = jnp.maximum(first, second)
                lse = peak + jnp.log(jnp.exp(first - peak) + jnp.exp(second - peak))
                lse_ref[cap, group : group + 1] = lse
                weight_one = lanes_to_rows(jnp.exp(first - lse), mask_low)
                weight_two = lanes_to_rows(jnp.exp(second - lse), mask_low)
                mixed = (
                    weight_one * att_one[span, lo : lo + LANES].astype(F32)
                    + weight_two * att_two[span, lo : lo + LANES].astype(F32)
                )
                att_full[span, lo : lo + LANES] = mixed
                att_low[span, lo : lo + LANES] = mixed.astype(BF16)
            return carry

        lax.fori_loop(0, captions, one_caption, 0)

        def one_tile(index, carry):
            span = pl.ds(pl.multiple_of(index * tile, tile), tile)
            two = hidden_ref[span, :] + dot(att_low[span, :], cross_mat[...])
            hidden_two[span, :] = two
            unit, _ = normalize(two)
            normed_ref[span, :] = (unit * as_row(gain_ref) + as_row(shift_ref)).astype(BF16)
            acc_out[span, :] = two
            acc_grad[span, :] = jnp.zeros_like(two)
            return carry

        lax.fori_loop(0, tiles, one_tile, 0)

    pre = dot(normed_ref[...], up_mat[...])
    cdf = 0.5 * (1.0 + lax.erf(pre * 0.7071067811865476))
    act = (pre * cdf).astype(BF16)
    acc_out[...] += dot(act, down_mat[...])
    cot = cot_ref[...]
    density = jnp.exp(-0.5 * pre * pre) * 0.3989422804014327
    grad_up = (dot_nt(cot, down_mat[...]) * (cdf + pre * density)).astype(BF16)
    acc_grad[...] += dot_nt(grad_up, up_mat[...])
    grad_down = dot_tn(act, cot).astype(BF16)
    grad_w = dot_tn(normed_ref[...], grad_up).astype(BF16)
    in_mine = (step >= steps // 2) == (side == 1)

    @pl.when(in_mine)
    def _():
        up_mine[...] = grad_w

    @pl.when(jnp.logical_not(in_mine))
    def _():
        up_send[...] = grad_w

    @pl.when(side == 0)
    def _():
        down_mine[...] = grad_down[:, :half]
        down_send[...] = grad_down[:, half:]

    @pl.when(side == 1)
    def _():
        down_mine[...] = grad_down[:, half:]
        down_send[...] = grad_down[:, :half]

    @pl.when(step == steps - 1)
    def _():
        mask_low = same_head().astype(BF16)
        gain_grad[...] = jnp.zeros_like(gain_grad)
        shift_grad[...] = jnp.zeros_like(shift_grad)

        def one_tile(index, carry):
            span = pl.ds(pl.multiple_of(index * tile, tile), tile)
            out_ref[span, :] = acc_out[span, :].astype(BF16)
            unit, inverse = normalize(hidden_two[span, :])
            grad = acc_grad[span, :]
            gain_grad[...] += jnp.sum(grad * unit, axis=0, keepdims=True)
            shift_grad[...] += jnp.sum(grad, axis=0, keepdims=True)
            two = cot_ref[span, :].astype(F32) + norm_back(grad, as_row(gain_ref), unit, inverse)
            grad_two_ref[span, :] = two
            low = two.astype(BF16)
            normed_ref[span, :] = low
            grad_att_ref[span, :] = dot_nt(low, cross_mat[...]).astype(BF16)
            return carry

        lax.fori_loop(0, tiles, one_tile, 0)
        grad_cross = dot_tn(att_low[...], normed_ref[...]).astype(BF16)

        @pl.when(side == 0)
        def _():
            cross_mine[...] = grad_cross[:, :half]
            cross_send[...] = grad_cross[:, half:]

        @pl.when(side == 1)
        def _():
            cross_mine[...] = grad_cross[:, half:]
            cross_send[...] = grad_cross[:, :half]

        def one_caption(cap, carry):
            span = pl.ds(pl.multiple_of(cap * length, length), length)
            for group in range(GROUPS):
                lo = group * LANES
                product = grad_att_ref[span, lo : lo + LANES].astype(F32) * att_full[span, lo : lo + LANES]
                delta_ref[cap, group : group + 1] = rows_to_lanes(product, mask_low)
            return carry

        lax.fori_loop(0, captions, one_caption, 0)


def feed(side, att_one, lse_one, att_two, lse_two, hidden, cot, cross_mat, gain, shift, up_mat, down_mat, length):
    rows, width = hidden.shape
    captions = rows // length
    units = up_mat.shape[1]
    chunk = 512
    steps = units // chunk
    middle = steps // 2
    tile = min(256, rows)
    half = width // 2
    stat = (captions, GROUPS, LANES)
    sds = jax.ShapeDtypeStruct
    clip = lambda v: jnp.minimum(jnp.maximum(v, 0), middle - 1)
    mine_map = lambda i, side: (0, clip(i - middle * side[0]))
    send_map = lambda i, side: (0, clip(i - middle * (1 - side[0])))
    return pl.pallas_call(
        functools.partial(feed_body, length=length, tile=tile),
        grid_spec=pltpu.PrefetchScalarGridSpec(
            num_scalar_prefetch=1,
            grid=(steps,),
            in_specs=[
                whole((rows, width)), whole(stat), whole((rows, width)), whole(stat),
                whole((rows, width)), whole((rows, width)), whole((width, width)),
                whole((width,)), whole((width,)),
                pl.BlockSpec((width, chunk), lambda i, *_: (0, i)),
                pl.BlockSpec((chunk, width), lambda i, *_: (i, 0)),
            ],
            out_specs=[
                whole((rows, width)), whole((rows, width)), whole((rows, width)), whole(stat),
                whole(stat),
                pl.BlockSpec((width, chunk), mine_map), pl.BlockSpec((width, chunk), send_map),
                pl.BlockSpec((chunk, half), lambda i, *_: (i, 0)),
                pl.BlockSpec((chunk, half), lambda i, *_: (i, 0)),
                whole((width, half)), whole((width, half)),
                whole((1, width)), whole((1, width)),
            ],
            scratch_shapes=[
                pltpu.VMEM((rows, width), F32), pltpu.VMEM((rows, width), BF16),
                pltpu.VMEM((rows, width), F32), pltpu.VMEM((rows, width), BF16),
                pltpu.VMEM((rows, width), F32), pltpu.VMEM((rows, width), F32),
            ],
        ),
        out_shape=[
            sds((rows, width), BF16), sds((rows, width), F32), sds((rows, width), BF16),
            sds(stat, F32), sds(stat, F32),
            sds((width, units // 2), BF16), sds((width, units // 2), BF16),
            sds((units, half), BF16), sds((units, half), BF16),
            sds((width, half), BF16), sds((width, half), BF16),
            sds((1, width), F32), sds((1, width), F32),
        ],
        compiler_params=pltpu.CompilerParams(vmem_limit_bytes=VMEM_LIMIT),
        name="feed",
    )(side, att_one, lse_one, att_two, lse_two, hidden, cot, cross_mat, gain, shift, up_mat, down_mat)


def cross_back_body(
    valid_ref, kv_ref, query_ref, grad_ref, lse_ref, delta_ref, kv_mat,
    grad_query_ref, grad_kv_ref, grad_img_ref, *, short
):
    cap = pl.program_id(0)
    valid = valid_ref[cap]
    width = query_ref.shape[2]
    slots = kv_ref.shape[1]

    def work(count):
        mask = same_head()
        inside = iota((count, LANES), 0) < valid
        for group in range(GROUPS):
            lo = group * LANES
            key = kv_ref[0, :count, lo : lo + LANES]
            value = kv_ref[0, :count, width + lo : width + lo + LANES]
            query = spread(query_ref[0, :, lo : lo + LANES], mask)
            grad = spread(grad_ref[0, :, lo : lo + LANES], mask)
            scores = dot_nt(key, query)
            probs = jnp.where(inside, jnp.exp(scores - lse_ref[0, group : group + 1]), 0.0)
            grad_probs = dot_nt(value, grad)
            grad_scores = (probs * (grad_probs - delta_ref[0, group : group + 1])).astype(BF16)
            back = gather_heads(dot_tn(grad_scores, key)) * SCALE
            grad_query_ref[0, :, lo : lo + LANES] = back.astype(BF16)
            grad_kv_ref[0, :count, lo : lo + LANES] = dot(grad_scores, query).astype(BF16)
            grad_kv_ref[0, :count, width + lo : width + lo + LANES] = dot(
                probs.astype(BF16), grad
            ).astype(BF16)
        grad_img_ref[0, :count] = dot_nt(grad_kv_ref[0, :count], kv_mat[...]).astype(BF16)
        if count < slots:
            grad_kv_ref[0, count:] = jnp.zeros((slots - count, 2 * width), BF16)
            grad_img_ref[0, count:] = jnp.zeros((slots - count, width), BF16)

    @pl.when(valid <= 0)
    def _():
        grad_query_ref[...] = jnp.zeros_like(grad_query_ref)
        grad_kv_ref[...] = jnp.zeros_like(grad_kv_ref)
        grad_img_ref[...] = jnp.zeros_like(grad_img_ref)

    if short < slots:
        pl.when((valid > 0) & (valid <= short))(lambda: work(short))
        pl.when(valid > short)(lambda: work(slots))
    else:
        pl.when(valid > 0)(lambda: work(slots))


def cross_back(valid, kv, queries, grads, lse, delta, kv_mat, short):
    caps, slots, double = kv.shape
    width = double // 2
    length = queries.shape[1]
    block = lambda *shape: pl.BlockSpec((1,) + shape, lambda i, *_: (i, 0, 0))
    sds = jax.ShapeDtypeStruct
    return pl.pallas_call(
        functools.partial(cross_back_body, short=short),
        grid_spec=pltpu.PrefetchScalarGridSpec(
            num_scalar_prefetch=1,
            grid=(caps,),
            in_specs=[
                block(slots, double), block(length, width), block(length, width),
                block(GROUPS, LANES), block(GROUPS, LANES), whole(kv_mat.shape),
            ],
            out_specs=[block(length, width), block(slots, double), block(slots, width)],
        ),
        out_shape=[
            sds((caps, length, width), BF16), sds((caps, slots, double), BF16),
            sds((caps, slots, width), BF16),
        ],
        compiler_params=pltpu.CompilerParams(vmem_limit_bytes=VMEM_LIMIT),
        name="cross_back",
    )(valid, kv, queries, grads, lse, delta, kv_mat)


def token_end_body(
    side_ref, back_one, back_two, hidden_ref, grad_two_ref, att_ref, qkv_ref, tok_ref,
    gain_one, shift_one, qkv_mat, out_mat, gain_two, shift_two, query_mat,
    grad_tok_ref, qkv_mine, qkv_send, out_mine, out_send, query_mine, query_send, gains_ref,
    grad_qkv_ref, acc_qkv, acc_out, acc_query, *, length
):
    step = pl.program_id(0)

    @pl.when(step == 0)
    def _():
        acc_qkv[...] = jnp.zeros_like(acc_qkv)
        acc_out[...] = jnp.zeros_like(acc_out)
        acc_query[...] = jnp.zeros_like(acc_query)
        gains_ref[...] = jnp.zeros_like(gains_ref)

    back = (back_one[...].astype(F32) + back_two[...].astype(F32)).astype(BF16)
    unit, inverse = normalize(hidden_ref[...])
    normed = (unit * as_row(gain_two) + as_row(shift_two)).astype(BF16)
    acc_query[...] += dot_tn(normed, back)
    grad = dot_nt(back, query_mat[...])
    gains_ref[2:3] += jnp.sum(grad * unit, axis=0, keepdims=True)
    gains_ref[3:4] += jnp.sum(grad, axis=0, keepdims=True)
    grad_one = grad_two_ref[...] + norm_back(grad, as_row(gain_two), unit, inverse)
    low = grad_one.astype(BF16)
    acc_out[...] += dot_tn(att_ref[...], low)
    grad_att = dot_nt(low, out_mat[...]).astype(BF16)
    rows, width = grad_att.shape
    mask = same_head()
    causal = causal_mask(length)
    for cap in range(rows // length):
        span = slice(cap * length, (cap + 1) * length)
        for group in range(GROUPS):
            lo = group * LANES
            query = spread(qkv_ref[span, lo : lo + LANES] * SCALE, mask)
            key = qkv_ref[span, width + lo : width + lo + LANES]
            value = qkv_ref[span, 2 * width + lo : 2 * width + lo + LANES]
            cot = spread(grad_att[span, lo : lo + LANES], mask)
            scores = jnp.where(causal, dot_nt(key, query), NEG)
            exponent = jnp.exp(scores - jnp.max(scores, axis=0, keepdims=True))
            probs = exponent / jnp.sum(exponent, axis=0, keepdims=True)
            grad_probs = dot_nt(value, cot)
            mean = jnp.sum(probs * grad_probs, axis=0, keepdims=True)
            grad_scores = (probs * (grad_probs - mean)).astype(BF16)
            grad_q = gather_heads(dot_tn(grad_scores, key)) * SCALE
            grad_qkv_ref[span, lo : lo + LANES] = grad_q.astype(BF16)
            grad_qkv_ref[span, width + lo : width + lo + LANES] = dot(grad_scores, query).astype(BF16)
            grad_qkv_ref[span, 2 * width + lo : 2 * width + lo + LANES] = dot(
                probs.astype(BF16), cot
            ).astype(BF16)
    unit, inverse = normalize(tok_ref[...].astype(F32))
    normed = (unit * as_row(gain_one) + as_row(shift_one)).astype(BF16)
    acc_qkv[...] += dot_tn(normed, grad_qkv_ref[...])
    grad = dot_nt(grad_qkv_ref[...], qkv_mat[...])
    gains_ref[0:1] += jnp.sum(grad * unit, axis=0, keepdims=True)
    gains_ref[1:2] += jnp.sum(grad, axis=0, keepdims=True)
    grad_tok_ref[...] = (grad_one + norm_back(grad, as_row(gain_one), unit, inverse)).astype(BF16)

    @pl.when(step == pl.num_programs(0) - 1)
    def _():
        for acc, mine, send in (
            (acc_qkv, qkv_mine, qkv_send),
            (acc_out, out_mine, out_send),
            (acc_query, query_mine, query_send),
        ):
            half = acc.shape[1] // 2

            @pl.when(side_ref[0] == 0)
            def _():
                mine[...] = acc[:, :half].astype(BF16)
                send[...] = acc[:, half:].astype(BF16)

            @pl.when(side_ref[0] == 1)
            def _():
                mine[...] = acc[:, half:].astype(BF16)
                send[...] = acc[:, :half].astype(BF16)


def token_end(
    side, back_one, back_two, hidden, grad_two, att, qkv, tokens,
    gain_one, shift_one, qkv_mat, out_mat, gain_two, shift_two, query_mat, length
):
    rows, width = tokens.shape
    tile = min(256, rows)
    row_block = lambda cols: pl.BlockSpec((tile, cols), lambda i, *_: (i, 0))
    sds = jax.ShapeDtypeStruct
    halves = [(width, 3 * width // 2)] * 2 + [(width, width // 2)] * 4
    return pl.pallas_call(
        functools.partial(token_end_body, length=length),
        grid_spec=pltpu.PrefetchScalarGridSpec(
            num_scalar_prefetch=1,
            grid=(rows // tile,),
            in_specs=[
                row_block(width), row_block(width), row_block(width), row_block(width),
                row_block(width), row_block(3 * width), row_block(width),
                whole((width,)), whole((width,)), whole(qkv_mat.shape), whole(out_mat.shape),
                whole((width,)), whole((width,)), whole(query_mat.shape),
            ],
            out_specs=[row_block(width)] + [whole(s) for s in halves] + [whole((4, width))],
            scratch_shapes=[
                pltpu.VMEM((tile, 3 * width), BF16), pltpu.VMEM((width, 3 * width), F32),
                pltpu.VMEM((width, width), F32), pltpu.VMEM((width, width), F32),
            ],
        ),
        out_shape=[sds((rows, width), BF16)] + [sds(s, BF16) for s in halves] + [sds((4, width), F32)],
        compiler_params=pltpu.CompilerParams(vmem_limit_bytes=VMEM_LIMIT),
        name="token_end",
    )(
        side, back_one, back_two, hidden, grad_two, att, qkv, tokens,
        gain_one, shift_one, qkv_mat, out_mat, gain_two, shift_two, query_mat,
    )


def add_low(first, second):
    return (first.astype(F32) + second.astype(F32)).astype(BF16)


class Piece:
    def __init__(self, acc, recvs, out, col, bits, order, source=None, mine=None, send=None, kv_recv=None):
        self.acc, self.recvs, self.out, self.col = acc, recvs, out, col
        self.bits, self.order, self.source = bits, order, source
        self.mine, self.send, self.kv_recv = mine, send, kv_recv
        self.copies = 1 + len(order)
        self.done = []

    def columns(self, ref):
        width = self.acc.shape[-1]
        return (slice(None), pl.ds(self.col, width)) if ref.shape[-1] != width else (slice(None), slice(None))


class Sums:
    def __init__(self, send_sem, recv_sem, size):
        self.send_sem, self.recv_sem, self.count, self.size = send_sem, recv_sem, 0, size
        self.me, self.side = lax.axis_index("dp"), lax.axis_index("kv")

    def own(self, bit):
        return (self.me // (1 << bit)) % 2

    def partner(self, bit):
        return {"dp": self.me + (1 - 2 * self.own(bit)) * (1 << bit)}

    def copy(self, src, dst, device):
        index = self.count
        self.count += 1
        return pltpu.make_async_remote_copy(
            src_ref=src, dst_ref=dst, send_sem=self.send_sem.at[index], recv_sem=self.recv_sem.at[index],
            device_id=device, device_id_type=pl.DeviceIdType.MESH,
        )

    def greet(self, bits):
        barrier = pltpu.get_barrier_semaphore()
        for device in [{"kv": 1 - self.side}] + [self.partner(bit) for bit in bits]:
            pl.semaphore_signal(barrier, inc=1, device_id=device, device_id_type=pl.DeviceIdType.MESH)
        pl.semaphore_wait(barrier, 1 + len(bits))

    def place(self, piece, now, value):
        index = []
        for bit in piece.bits:
            if bit in piece.order[:now]:
                index.append(self.own(bit))
            elif bit == piece.order[now]:
                index.append(value)
            else:
                index.append(slice(None))
        return tuple(index)

    def start_kv(self, piece):
        piece.pending = self.copy(
            piece.send.at[(slice(None),) * len(piece.bits) + piece.columns(piece.send)],
            piece.kv_recv, {"kv": 1 - self.side},
        )
        piece.pending.start()

    def end_kv(self, piece):
        piece.pending.wait()
        count = len(piece.bits)
        cols = piece.columns(piece.mine)

        def one(i, carry):
            lead = tuple((i // (1 << (count - 1 - d))) % 2 for d in range(count))
            piece.acc[lead] = add_low(piece.mine[lead + cols], piece.kv_recv[lead])
            return carry

        lax.fori_loop(0, 1 << count, one, 0)
        piece.source = None

    def start(self, piece, now):
        bit = piece.order[now]
        ref = piece.acc if piece.source is None else piece.source
        lead = self.place(piece, now, 1 - self.own(bit))
        piece.pending = self.copy(ref.at[lead + piece.columns(ref)], piece.recvs[now], self.partner(bit))
        piece.pending.start()

    def end(self, piece, now):
        piece.pending.wait()
        ref = piece.acc if piece.source is None else piece.source
        cols = piece.columns(ref)
        bit = piece.order[now]
        left = [b for b in piece.bits if b not in piece.order[: now + 1]]
        recv = piece.recvs[now]
        if not left:
            lead = self.place(piece, now, self.own(bit))
            width = piece.acc.shape[-1]
            piece.out[:, piece.col : piece.col + width] = ref[lead + cols].astype(F32) + recv[...].astype(F32)
            return

        def one(i, carry):
            inner = {b: (i // (1 << (len(left) - 1 - d))) % 2 for d, b in enumerate(left)}
            lead = tuple(inner[b] if b in inner else self.own(b) for b in piece.bits)
            piece.acc[lead] = add_low(ref[lead + cols], recv[tuple(inner[b] for b in left)])
            return carry

        lax.fori_loop(0, 1 << len(left), one, 0)
        piece.source = None


def finish_body(
    img_hbm, grad_hbm, up_ref, down_ref, cross_ref, qkv_mine, out_mine, query_mine,
    qkv_send, out_send, query_send, gains_ref,
    up_out, down_out, cross_out, qkv_out, out_out, query_out, kv_out, gains_out,
    *scratch, plan, tile, size
):
    scratch = list(scratch)
    send_sem, recv_sem, load_sem, img_buf, grad_buf, acc_kv, kv_mine, kv_send = scratch[:8]
    gain_buf, gain_recv = scratch[8:10]
    rest = scratch[10:]
    sums = Sums(send_sem, recv_sem, size)
    bits = list(range(size.bit_length() - 1))
    named = dict(
        up=(up_ref, None, None, up_out), down=(down_ref, None, None, down_out),
        cross=(cross_ref, None, None, cross_out), qkv=(None, qkv_mine, qkv_send, qkv_out),
        out=(None, out_mine, out_send, out_out), query=(None, query_mine, query_send, query_out),
        kv=(None, kv_mine, kv_send, kv_out),
    )
    pieces = []
    for name, col, width, piece_bits, order, kv in plan:
        source, mine, send, out = named[name]
        acc = rest.pop(0)
        kv_recv = rest.pop(0) if kv else None
        recvs = [rest.pop(0) for _ in order]
        pieces.append((name, Piece(acc, recvs, out, col, piece_bits, order, source, mine, send, kv_recv)))
    early = [p for n, p in pieces if n in ("up", "down", "cross")]
    late = [p for n, p in pieces if n in ("qkv", "out", "query")]
    image = [p for n, p in pieces if n == "kv"]

    steps = img_hbm.shape[0] // tile

    def load(step, slot):
        rows = pl.ds(pl.multiple_of(step * tile, tile), tile)
        return (
            pltpu.make_async_copy(img_hbm.at[rows], img_buf.at[slot], load_sem.at[0, slot]),
            pltpu.make_async_copy(grad_hbm.at[rows], grad_buf.at[slot], load_sem.at[1, slot]),
        )

    for copy in load(0, 0):
        copy.start()
    sums.greet(bits)
    for piece in late:
        sums.start_kv(piece)
    for piece in early:
        sums.start(piece, 0)
    half = gains_ref.shape[1] // 2
    gains_kv = sums.copy(gains_ref, gain_recv.at[0], {"kv": 1 - sums.side})
    gains_kv.start()
    acc_kv[...] = jnp.zeros_like(acc_kv)

    def multiply(first, last):
        def one(step, carry):
            slot = step % 2

            @pl.when(step + 1 < steps)
            def _():
                for copy in load(step + 1, 1 - slot):
                    copy.start()

            for copy in load(step, slot):
                copy.wait()
            acc_kv[...] += dot_tn(img_buf[slot], grad_buf[slot])
            return carry

        lax.fori_loop(first, last, one, 0)

    multiply(0, min(3, steps))
    for piece in late:
        sums.end_kv(piece)
        sums.start(piece, 0)
    multiply(min(3, steps), steps)
    gains_kv.wait()
    total = gains_ref[...] + gain_recv[0]

    @pl.when(sums.side == 0)
    def _():
        gain_buf[0] = total[:, :half]

    @pl.when(sums.side == 1)
    def _():
        gain_buf[0] = total[:, half:]

    def gain_start(now):
        copy = sums.copy(gain_buf.at[now], gain_recv.at[now + 1, :, pl.ds(0, half)], sums.partner(bits[now]))
        copy.start()
        return copy

    def gain_end(now, copy):
        copy.wait()
        gain_buf[now + 1] = gain_buf[now] + gain_recv[now + 1, :, :half]

    gain_copy = gain_start(0)

    def store_kv(ref, second):
        count = len(bits)
        rows = ref.shape[-2]
        width = ref.shape[-1]

        def one(i, carry):
            lead = tuple((i // (1 << (count - 1 - d))) % 2 for d in range(count))
            span = pl.ds(i * rows, rows)
            ref[lead] = acc_kv[span, second * width : (second + 1) * width].astype(BF16)
            return carry

        if rows % 8 == 0:
            lax.fori_loop(0, 1 << count, one, 0)
        else:
            for i in range(1 << count):
                one(i, 0)

    @pl.when(sums.side == 0)
    def _():
        store_kv(kv_mine, 0)
        store_kv(kv_send, 1)

    @pl.when(sums.side == 1)
    def _():
        store_kv(kv_mine, 1)
        store_kv(kv_send, 0)

    for piece in image:
        sums.start_kv(piece)
    for now in range(len(bits)):
        for piece in early:
            if now < len(piece.order):
                sums.end(piece, now)
                if now + 1 < len(piece.order):
                    sums.start(piece, now + 1)
        for piece in image:
            if now == 0:
                sums.end_kv(piece)
            else:
                sums.end(piece, now - 1)
            sums.start(piece, now)
        gain_end(now, gain_copy)
        if now + 1 < len(bits):
            gain_copy = gain_start(now + 1)
        for piece in late:
            sums.end(piece, now)
            if now + 1 < len(bits):
                sums.start(piece, now + 1)
    for piece in image:
        sums.end(piece, len(bits) - 1)
    gains_out[...] = gain_buf[len(bits)]


def hand_over_body(*refs):
    count = len(refs) // 2
    for source, target in zip(refs[:count], refs[count:]):
        target[...] = source[...]


def hand_over(*arrays):
    vmem = pl.BlockSpec(memory_space=pltpu.VMEM)
    return pl.pallas_call(
        hand_over_body,
        in_specs=[vmem] * len(arrays),
        out_specs=[vmem] * len(arrays),
        out_shape=[jax.ShapeDtypeStruct(v.shape, v.dtype) for v in arrays],
        name="hand_over",
    )(*arrays)


def finish(images, grads, early, mines, sends, gains, size):
    bits = list(range(size.bit_length() - 1))
    down_bits = bits[::-1]
    left = bits[-2:]
    left_down = left[::-1]
    forward = bits
    turned = bits[1:2] + bits[0:1] + bits[2:]
    rows, width = images.shape
    double = grads.shape[1]
    tile = 512 if rows % 512 == 0 else rows // 4
    up, down, cross = early
    qkv, out, query = mines
    split = (qkv.shape[-1] // 256 + 1) * 128
    plan = [
        ("up", 0, up.shape[-1], left_down, left, False),
        ("down", 0, down.shape[-1], left_down, left, False),
        ("cross", 0, cross.shape[-1], left_down, left, False),
        ("qkv", 0, split, down_bits, forward, True),
        ("qkv", split, qkv.shape[-1] - split, down_bits, turned, True),
        ("out", 0, out.shape[-1], down_bits, forward, True),
        ("query", 0, query.shape[-1], down_bits, turned, True),
        ("kv", 0, double // 4, down_bits, forward, True),
        ("kv", double // 4, double // 4, down_bits, turned, True),
    ]
    shapes = dict(up=up, down=down, cross=cross, qkv=qkv, out=out, query=query)
    lead = (2,) * len(bits)
    kv_shape = lead + (width // size, double // 2)
    buffers = []
    copies = 1 + len(bits)
    for name, col, cols, piece_bits, order, kv in plan:
        block = (kv_shape if name == "kv" else shapes[name].shape)[-2]
        full = (2,) * len(piece_bits) + (block, cols)
        buffers.append(pltpu.VMEM(full, BF16))
        if kv:
            buffers.append(pltpu.VMEM(full, BF16))
            copies += 1
        for now in range(len(order)):
            buffers.append(pltpu.VMEM((2,) * (len(piece_bits) - now - 1) + (block, cols), BF16))
            copies += 1
    vmem = pl.BlockSpec(memory_space=pltpu.VMEM)
    hbm = pl.BlockSpec(memory_space=pl.ANY)
    sds = jax.ShapeDtypeStruct
    outs = [sds(v.shape[-2:], F32) for v in (up, down, cross, qkv, out, query)]
    outs += [sds(kv_shape[-2:], F32), sds((gains.shape[0], width // 2), F32)]
    return pl.pallas_call(
        functools.partial(finish_body, plan=plan, tile=tile, size=size),
        in_specs=[hbm, hbm] + [vmem] * 6 + [hbm] * 3 + [vmem],
        out_specs=[vmem] * len(outs),
        out_shape=outs,
        scratch_shapes=[
            pltpu.SemaphoreType.DMA((copies,)), pltpu.SemaphoreType.DMA((copies,)),
            pltpu.SemaphoreType.DMA((2, 2)),
            pltpu.VMEM((2, tile, width), BF16), pltpu.VMEM((2, tile, double), BF16),
            pltpu.VMEM((width, double), F32), pltpu.VMEM(kv_shape, BF16), pltpu.VMEM(kv_shape, BF16),
            pltpu.VMEM((len(bits) + 1, gains.shape[0], width // 2), F32),
            pltpu.VMEM((len(bits) + 1, gains.shape[0], width), F32),
        ] + buffers,
        compiler_params=pltpu.CompilerParams(
            vmem_limit_bytes=VMEM_LIMIT, collective_id=0, has_side_effects=True
        ),
        name="finish",
    )(images, grads, up, down, cross, qkv, out, query, *sends, gains)


def exchange(value, axis, bit, size):
    return lax.ppermute(value, axis, [(i, i ^ bit) for i in range(size)])


def split_rows(array, size):
    bits = size.bit_length() - 1
    return array.reshape((2,) * bits + (array.shape[0] // size, array.shape[1]))


def reduce_some(mine, send, order, me, size):
    total = add_low(mine, exchange(send, "kv", 1, 2))
    left = list(range(size.bit_length() - 1))[::-1]
    total = split_rows(total, size)
    for bit in order:
        axis = left.index(bit)
        own = (me >> bit) & 1
        keep = lax.dynamic_index_in_dim(total, own, axis, False)
        away = lax.dynamic_index_in_dim(total, 1 - own, axis, False)
        total = add_low(keep, exchange(away, "dp", 1 << bit, size))
        left.remove(bit)
    return total


def body(
    tokens, images, image_counts, cotangent, norm1_gain, norm1_shift, self_qkv, self_out,
    norm2_gain, norm2_shift, cross_q, cross_kv, cross_out, norm3_gain, norm3_shift, w_up, w_down,
):
    captions, length, width = tokens.shape
    caps, slots, _ = images.shape
    side = lax.axis_index("kv")
    me = lax.axis_index("dp")
    groups = lax.axis_size("dp")
    side_arr = side.reshape(1)
    row = lambda v: v
    tok = tokens.reshape(captions * length, width)
    cot = cotangent.reshape(captions * length, width)
    short = -(-SHORT // 16) * 16
    valid = jnp.clip(image_counts - side * slots, 0, slots)
    swap = lambda v: exchange(v, "kv", 1, 2)

    qkv, att, hidden, query = token_start(
        tok, row(norm1_gain), row(norm1_shift), self_qkv, self_out, row(norm2_gain),
        row(norm2_shift), cross_q, length,
    )

    def both(own):
        other = swap(own)
        first = jnp.where(side == 0, own, other)
        second = jnp.where(side == 0, other, own)
        return jnp.concatenate([first, second], axis=0)

    def own_part(array):
        return lax.dynamic_slice_in_dim(array, side * captions, captions, 0)

    def other_part(array):
        return lax.dynamic_slice_in_dim(array, (1 - side) * captions, captions, 0)

    queries = both(query.reshape(captions, length, width))
    kv, part, lse_part = cross_start(valid, images, cross_kv, queries, short)
    flat = lambda v: v.reshape(captions * length, width)
    (
        layer_out, grad_two, grad_att, lse, delta, up_mine, up_send, down_mine, down_send,
        cross_mine, cross_send, gain3, shift3,
    ) = feed(
        side_arr, flat(own_part(part)), own_part(lse_part), flat(swap(other_part(part))),
        swap(other_part(lse_part)), hidden, cot, cross_out, row(norm3_gain), row(norm3_shift),
        w_up, w_down, length,
    )
    first_bits = list(range(groups.bit_length() - 1))[:-2]
    turned = first_bits[1:] + first_bits[:1]
    early = [
        reduce_some(up_mine, up_send, first_bits, me, groups),
        reduce_some(down_mine, down_send, turned, me, groups),
        reduce_some(cross_mine, cross_send, turned, me, groups),
    ]

    grads = both(grad_att.reshape(captions, length, width))
    back, grad_kv, images_grad = cross_back(
        valid, kv, queries, grads, both(lse), both(delta), cross_kv, short
    )
    (
        tokens_grad, qkv_mine, qkv_send, out_mine, out_send, query_mine, query_send, gains,
    ) = token_end(
        side_arr, flat(own_part(back)), flat(swap(other_part(back))), hidden, grad_two, att, qkv,
        tok, row(norm1_gain), row(norm1_shift), self_qkv, self_out, row(norm2_gain),
        row(norm2_shift), cross_q, length,
    )
    gains = jnp.concatenate([gains, gain3, shift3, jnp.zeros((2, width), F32)], axis=0)
    cut = lambda v: split_rows(v, groups)
    (
        w_up_grad, down_grad, cross_out_grad, self_qkv_grad, self_out_grad, cross_q_grad,
        cross_kv_grad, gains,
    ) = hand_over(*finish(
        images.reshape(caps * slots, width), grad_kv.reshape(caps * slots, 2 * width), early,
        [cut(qkv_mine), cut(out_mine), cut(query_mine)],
        [cut(qkv_send), cut(out_send), cut(query_send)], gains, groups,
    ))
    return (
        layer_out.reshape(captions, length, width),
        tokens_grad.reshape(captions, length, width),
        images_grad,
        gains[0], gains[1], self_qkv_grad, self_out_grad, gains[2], gains[3], cross_q_grad,
        cross_kv_grad, cross_out_grad, gains[4], gains[5], w_up_grad, down_grad,
    )


def solution(mesh):
    return jax.shard_map(
        body,
        mesh=mesh,
        in_specs=(
            P(("dp", "kv"), None, None), P("dp", "kv", None), P("dp"), P(("dp", "kv"), None, None),
        ) + (P(),) * 13,
        out_specs=(
            P(("dp", "kv"), None, None), P(("dp", "kv"), None, None), P("dp", "kv", None),
            P("kv"), P("kv"), P("dp", "kv"), P("dp", "kv"), P("kv"), P("kv"), P("dp", "kv"),
            P("dp", "kv"), P("dp", "kv"), P("kv"), P("kv"), P("dp", "kv"), P("dp", "kv"),
        ),
        check_vma=False,
    )
```

```python
import functools

import jax
import jax.numpy as jnp
from jax import lax
from jax.experimental import pallas as pl
from jax.experimental.pallas import tpu as pltpu
from jax.sharding import PartitionSpec as P

HEADS = 12
HEAD_DIM = 64
SHORT = 196
LANES = 256
PACK = LANES // HEAD_DIM
GROUPS = HEADS // PACK
SCALE = HEAD_DIM ** (-0.5)
NEG = -1e30
F32 = jnp.float32
BF16 = jnp.bfloat16
VMEM_LIMIT = 60 * 1024 * 1024
VMEM_MOST = 67043328


def dot(a, b):
    return jnp.dot(a, b, preferred_element_type=F32)


def dot_nt(a, b):
    return lax.dot_general(a, b, (((1,), (1,)), ((), ())), preferred_element_type=F32)


def dot_tn(a, b):
    return lax.dot_general(a, b, (((0,), (0,)), ((), ())), preferred_element_type=F32)


def normalize(values):
    centered = values - jnp.mean(values, axis=-1, keepdims=True)
    inverse = lax.rsqrt(jnp.mean(centered * centered, axis=-1, keepdims=True) + 1e-05)
    return centered * inverse, inverse


def norm_back(grad, gain, unit, inverse):
    scaled = grad * gain
    mean_one = jnp.mean(scaled, axis=-1, keepdims=True)
    mean_two = jnp.mean(scaled * unit, axis=-1, keepdims=True)
    return (scaled - mean_one - unit * mean_two) * inverse


def as_row(ref):
    return ref[...].reshape(1, ref.shape[0])


def iota(shape, dim):
    return lax.broadcasted_iota(jnp.int32, shape, dim)


def same_head():
    shape = (LANES, LANES)
    return (iota(shape, 0) // HEAD_DIM) == (iota(shape, 1) // HEAD_DIM)


def spread(rows, mask):
    stacked = jnp.concatenate([rows] * PACK, axis=0)
    return jnp.where(mask, stacked, jnp.zeros_like(stacked))


def gather_heads(full):
    count = full.shape[0] // PACK
    head = iota((count, LANES), 1) // HEAD_DIM
    out = full[:count]
    for index in range(1, PACK):
        out = jnp.where(head == index, full[index * count : (index + 1) * count], out)
    return out


def split_two(value):
    high = value.astype(BF16)
    return high, (value - high.astype(F32)).astype(BF16)


def lanes_to_rows(row, mask_low):
    shape = (HEAD_DIM, LANES)
    pick = iota(shape, 0) == (iota(shape, 1) % HEAD_DIM)
    high, low = split_two(jnp.where(pick, row, 0.0))
    return dot(high, mask_low) + dot(low, mask_low)


def rows_to_lanes(rows, mask_low):
    high, low = split_two(rows)
    summed = dot(high, mask_low) + dot(low, mask_low)
    shape = (HEAD_DIM, LANES)
    pick = iota(shape, 0) == (iota(shape, 1) % HEAD_DIM)
    return jnp.sum(jnp.where(pick, summed, 0.0), axis=0, keepdims=True)


def lane_slice(group):
    return slice(group * LANES, (group + 1) * LANES)


def causal_mask(length):
    shape = (length, LANES)
    return iota(shape, 0) <= (iota(shape, 1) % HEAD_DIM)


def token_start_body(
    tok_ref, gain_one, shift_one, qkv_mat, out_mat, gain_two, shift_two, query_mat,
    qkv_ref, att_ref, hidden_ref, query_ref, *, length
):
    x = tok_ref[...].astype(F32)
    unit, _ = normalize(x)
    normed = (unit * as_row(gain_one) + as_row(shift_one)).astype(BF16)
    width = x.shape[1]
    qkv_ref[...] = dot(normed, qkv_mat[...]).astype(BF16)
    mask = same_head()
    causal = causal_mask(length)
    for cap in range(x.shape[0] // length):
        rows = slice(cap * length, (cap + 1) * length)
        for group in range(GROUPS):
            lo = group * LANES
            query = qkv_ref[rows, lo : lo + LANES] * SCALE
            key = qkv_ref[rows, width + lo : width + lo + LANES]
            value = qkv_ref[rows, 2 * width + lo : 2 * width + lo + LANES]
            scores = jnp.where(causal, dot_nt(key, spread(query, mask)), NEG)
            exponent = jnp.exp(scores - jnp.max(scores, axis=0, keepdims=True))
            probs = exponent / jnp.sum(exponent, axis=0, keepdims=True)
            full = dot_tn(probs.astype(BF16), value)
            att_ref[rows, lo : lo + LANES] = gather_heads(full).astype(BF16)
    hidden = x + dot(att_ref[...], out_mat[...])
    hidden_ref[...] = hidden
    unit, _ = normalize(hidden)
    normed = (unit * as_row(gain_two) + as_row(shift_two)).astype(BF16)
    query_ref[...] = (dot(normed, query_mat[...]).astype(BF16).astype(F32) * SCALE).astype(BF16)


def whole(shape):
    zeros = (0,) * len(shape)
    return pl.BlockSpec(shape, lambda *_: zeros)


def token_start(tokens, gain_one, shift_one, qkv_mat, out_mat, gain_two, shift_two, query_mat, length):
    rows, width = tokens.shape
    tile = min(256, rows)
    row_block = lambda cols: pl.BlockSpec((tile, cols), lambda i: (i, 0))
    return pl.pallas_call(
        functools.partial(token_start_body, length=length),
        grid=(rows // tile,),
        in_specs=[
            row_block(width), whole((width,)), whole((width,)), whole(qkv_mat.shape),
            whole(out_mat.shape), whole((width,)), whole((width,)), whole(query_mat.shape),
        ],
        out_specs=[row_block(3 * width), row_block(width), row_block(width), row_block(width)],
        out_shape=[
            jax.ShapeDtypeStruct((rows, 3 * width), BF16),
            jax.ShapeDtypeStruct((rows, width), BF16),
            jax.ShapeDtypeStruct((rows, width), F32),
            jax.ShapeDtypeStruct((rows, width), BF16),
        ],
        compiler_params=pltpu.CompilerParams(vmem_limit_bytes=VMEM_LIMIT),
        name="token_start",
    )(tokens, gain_one, shift_one, qkv_mat, out_mat, gain_two, shift_two, query_mat)


def cross_start_body(valid_ref, img_ref, kv_mat, query_ref, kv_ref, att_ref, lse_ref, *, short):
    cap = pl.program_id(0)
    valid = valid_ref[cap]
    width = query_ref.shape[2]
    slots = img_ref.shape[1]

    def work(count):
        kv_ref[0, :count] = dot(img_ref[0, :count], kv_mat[...]).astype(BF16)
        mask = same_head()
        inside = iota((count, LANES), 0) < valid
        for group in range(GROUPS):
            lo = group * LANES
            key = kv_ref[0, :count, lo : lo + LANES]
            value = kv_ref[0, :count, width + lo : width + lo + LANES]
            scores = dot_nt(key, spread(query_ref[0, :, lo : lo + LANES], mask))
            scores = jnp.where(inside, scores, NEG)
            peak = jnp.max(scores, axis=0, keepdims=True)
            exponent = jnp.where(inside, jnp.exp(scores - peak), 0.0)
            total = jnp.sum(exponent, axis=0, keepdims=True)
            probs = (exponent * (1.0 / total)).astype(BF16)
            att_ref[0, :, lo : lo + LANES] = gather_heads(dot_tn(probs, value)).astype(BF16)
            lse_ref[0, group : group + 1] = peak + jnp.log(total)

    @pl.when(valid <= 0)
    def _():
        att_ref[...] = jnp.zeros_like(att_ref)
        lse_ref[...] = jnp.full_like(lse_ref, NEG)

    if short < slots:
        pl.when((valid > 0) & (valid <= short))(lambda: work(short))
        pl.when(valid > short)(lambda: work(slots))
    else:
        pl.when(valid > 0)(lambda: work(slots))


def cross_start(valid, images, kv_mat, queries, short):
    caps, slots, width = images.shape
    length = queries.shape[1]
    block = lambda *shape: pl.BlockSpec((1,) + shape, lambda i, *_: (i, 0, 0))
    return pl.pallas_call(
        functools.partial(cross_start_body, short=short),
        grid_spec=pltpu.PrefetchScalarGridSpec(
            num_scalar_prefetch=1,
            grid=(caps,),
            in_specs=[block(slots, width), whole(kv_mat.shape), block(length, width)],
            out_specs=[block(slots, 2 * width), block(length, width), block(GROUPS, LANES)],
        ),
        out_shape=[
            jax.ShapeDtypeStruct((caps, slots, 2 * width), BF16),
            jax.ShapeDtypeStruct((caps, length, width), BF16),
            jax.ShapeDtypeStruct((caps, GROUPS, LANES), F32),
        ],
        compiler_params=pltpu.CompilerParams(vmem_limit_bytes=VMEM_LIMIT),
        name="cross_start",
    )(valid, images, kv_mat, queries)


def feed_body(
    side_ref, att_one, lse_one, att_two, lse_two, hidden_ref, cot_ref, cross_mat, gain_ref,
    shift_ref, up_mat, down_mat,
    out_ref, grad_two_ref, grad_att_ref, lse_ref, delta_ref, up_mine, up_send, down_mine,
    down_send, cross_mine, cross_send, gain_grad, shift_grad,
    att_full, att_low, hidden_two, normed_ref, acc_out, acc_grad, *, length, tile
):
    step = pl.program_id(0)
    steps = pl.num_programs(0)
    side = side_ref[0]
    rows, width = hidden_ref.shape
    captions = rows // length
    tiles = rows // tile
    half = width // 2

    @pl.when(step == 0)
    def _():
        mask_low = same_head().astype(BF16)

        def one_caption(cap, carry):
            span = pl.ds(pl.multiple_of(cap * length, length), length)
            for group in range(GROUPS):
                lo = group * LANES
                first = lse_one[cap, group : group + 1]
                second = lse_two[cap, group : group + 1]
                peak = jnp.maximum(first, second)
                lse = peak + jnp.log(jnp.exp(first - peak) + jnp.exp(second - peak))
                lse_ref[cap, group : group + 1] = lse
                weight_one = lanes_to_rows(jnp.exp(first - lse), mask_low)
                weight_two = lanes_to_rows(jnp.exp(second - lse), mask_low)
                mixed = (
                    weight_one * att_one[span, lo : lo + LANES].astype(F32)
                    + weight_two * att_two[span, lo : lo + LANES].astype(F32)
                )
                att_full[span, lo : lo + LANES] = mixed
                att_low[span, lo : lo + LANES] = mixed.astype(BF16)
            return carry

        lax.fori_loop(0, captions, one_caption, 0)

        def one_tile(index, carry):
            span = pl.ds(pl.multiple_of(index * tile, tile), tile)
            two = hidden_ref[span, :] + dot(att_low[span, :], cross_mat[...])
            hidden_two[span, :] = two
            unit, _ = normalize(two)
            normed_ref[span, :] = (unit * as_row(gain_ref) + as_row(shift_ref)).astype(BF16)
            acc_out[span, :] = two
            acc_grad[span, :] = jnp.zeros_like(two)
            return carry

        lax.fori_loop(0, tiles, one_tile, 0)

    pre = dot(normed_ref[...], up_mat[...])
    cdf = 0.5 * (1.0 + lax.erf(pre * 0.7071067811865476))
    act = (pre * cdf).astype(BF16)
    acc_out[...] += dot(act, down_mat[...])
    cot = cot_ref[...]
    density = jnp.exp(-0.5 * pre * pre) * 0.3989422804014327
    grad_up = (dot_nt(cot, down_mat[...]) * (cdf + pre * density)).astype(BF16)
    acc_grad[...] += dot_nt(grad_up, up_mat[...])
    grad_down = dot_tn(act, cot).astype(BF16)
    grad_w = dot_tn(normed_ref[...], grad_up).astype(BF16)
    in_mine = (step >= steps // 2) == (side == 1)

    @pl.when(in_mine)
    def _():
        up_mine[...] = grad_w

    @pl.when(jnp.logical_not(in_mine))
    def _():
        up_send[...] = grad_w

    @pl.when(side == 0)
    def _():
        down_mine[...] = grad_down[:, :half]
        down_send[...] = grad_down[:, half:]

    @pl.when(side == 1)
    def _():
        down_mine[...] = grad_down[:, half:]
        down_send[...] = grad_down[:, :half]

    @pl.when(step == steps - 1)
    def _():
        mask_low = same_head().astype(BF16)
        gain_grad[...] = jnp.zeros_like(gain_grad)
        shift_grad[...] = jnp.zeros_like(shift_grad)

        def one_tile(index, carry):
            span = pl.ds(pl.multiple_of(index * tile, tile), tile)
            out_ref[span, :] = acc_out[span, :].astype(BF16)
            unit, inverse = normalize(hidden_two[span, :])
            grad = acc_grad[span, :]
            gain_grad[...] += jnp.sum(grad * unit, axis=0, keepdims=True)
            shift_grad[...] += jnp.sum(grad, axis=0, keepdims=True)
            two = cot_ref[span, :].astype(F32) + norm_back(grad, as_row(gain_ref), unit, inverse)
            grad_two_ref[span, :] = two
            low = two.astype(BF16)
            normed_ref[span, :] = low
            grad_att_ref[span, :] = dot_nt(low, cross_mat[...]).astype(BF16)
            return carry

        lax.fori_loop(0, tiles, one_tile, 0)
        grad_cross = dot_tn(att_low[...], normed_ref[...]).astype(BF16)

        @pl.when(side == 0)
        def _():
            cross_mine[...] = grad_cross[:, :half]
            cross_send[...] = grad_cross[:, half:]

        @pl.when(side == 1)
        def _():
            cross_mine[...] = grad_cross[:, half:]
            cross_send[...] = grad_cross[:, :half]

        def one_caption(cap, carry):
            span = pl.ds(pl.multiple_of(cap * length, length), length)
            for group in range(GROUPS):
                lo = group * LANES
                product = grad_att_ref[span, lo : lo + LANES].astype(F32) * att_full[span, lo : lo + LANES]
                delta_ref[cap, group : group + 1] = rows_to_lanes(product, mask_low)
            return carry

        lax.fori_loop(0, captions, one_caption, 0)


def feed(side, att_one, lse_one, att_two, lse_two, hidden, cot, cross_mat, gain, shift, up_mat, down_mat, length):
    rows, width = hidden.shape
    captions = rows // length
    units = up_mat.shape[1]
    chunk = 512
    steps = units // chunk
    middle = steps // 2
    tile = min(256, rows)
    half = width // 2
    stat = (captions, GROUPS, LANES)
    sds = jax.ShapeDtypeStruct
    clip = lambda v: jnp.minimum(jnp.maximum(v, 0), middle - 1)
    mine_map = lambda i, side: (0, clip(i - middle * side[0]))
    send_map = lambda i, side: (0, clip(i - middle * (1 - side[0])))
    return pl.pallas_call(
        functools.partial(feed_body, length=length, tile=tile),
        grid_spec=pltpu.PrefetchScalarGridSpec(
            num_scalar_prefetch=1,
            grid=(steps,),
            in_specs=[
                whole((rows, width)), whole(stat), whole((rows, width)), whole(stat),
                whole((rows, width)), whole((rows, width)), whole((width, width)),
                whole((width,)), whole((width,)),
                pl.BlockSpec((width, chunk), lambda i, *_: (0, i)),
                pl.BlockSpec((chunk, width), lambda i, *_: (i, 0)),
            ],
            out_specs=[
                whole((rows, width)), whole((rows, width)), whole((rows, width)), whole(stat),
                whole(stat),
                pl.BlockSpec((width, chunk), mine_map), pl.BlockSpec((width, chunk), send_map),
                pl.BlockSpec((chunk, half), lambda i, *_: (i, 0)),
                pl.BlockSpec((chunk, half), lambda i, *_: (i, 0)),
                whole((width, half)), whole((width, half)),
                whole((1, width)), whole((1, width)),
            ],
            scratch_shapes=[
                pltpu.VMEM((rows, width), F32), pltpu.VMEM((rows, width), BF16),
                pltpu.VMEM((rows, width), F32), pltpu.VMEM((rows, width), BF16),
                pltpu.VMEM((rows, width), F32), pltpu.VMEM((rows, width), F32),
            ],
        ),
        out_shape=[
            sds((rows, width), BF16), sds((rows, width), F32), sds((rows, width), BF16),
            sds(stat, F32), sds(stat, F32),
            sds((width, units // 2), BF16), sds((width, units // 2), BF16),
            sds((units, half), BF16), sds((units, half), BF16),
            sds((width, half), BF16), sds((width, half), BF16),
            sds((1, width), F32), sds((1, width), F32),
        ],
        compiler_params=pltpu.CompilerParams(vmem_limit_bytes=VMEM_LIMIT),
        name="feed",
    )(side, att_one, lse_one, att_two, lse_two, hidden, cot, cross_mat, gain, shift, up_mat, down_mat)


def cross_back_body(
    valid_ref, side_ref, kv_ref, query_ref, grad_ref, lse_ref, delta_ref, kv_mat, img_ref,
    grad_query_ref, grad_img_ref, mine_ref, send_ref, grad_kv_ref, acc_ref, *, short
):
    cap = pl.program_id(0)
    valid = valid_ref[cap]
    width = query_ref.shape[2]
    slots = kv_ref.shape[1]
    batch = img_ref.shape[0]
    place = cap % batch

    @pl.when(cap == 0)
    def _():
        acc_ref[...] = jnp.zeros_like(acc_ref)

    def work(count):
        mask = same_head()
        inside = iota((count, LANES), 0) < valid
        for group in range(GROUPS):
            lo = group * LANES
            key = kv_ref[0, :count, lo : lo + LANES]
            value = kv_ref[0, :count, width + lo : width + lo + LANES]
            query = spread(query_ref[0, :, lo : lo + LANES], mask)
            grad = spread(grad_ref[0, :, lo : lo + LANES], mask)
            scores = dot_nt(key, query)
            probs = jnp.where(inside, jnp.exp(scores - lse_ref[0, group : group + 1]), 0.0)
            grad_probs = dot_nt(value, grad)
            grad_scores = (probs * (grad_probs - delta_ref[0, group : group + 1])).astype(BF16)
            back = gather_heads(dot_tn(grad_scores, key)) * SCALE
            grad_query_ref[0, :, lo : lo + LANES] = back.astype(BF16)
            grad_kv_ref[place, :count, lo : lo + LANES] = dot(grad_scores, query).astype(BF16)
            grad_kv_ref[place, :count, width + lo : width + lo + LANES] = dot(
                probs.astype(BF16), grad
            ).astype(BF16)
        grad_img_ref[0, :count] = dot_nt(grad_kv_ref[place, :count], kv_mat[...]).astype(BF16)
        if count < slots:
            grad_kv_ref[place, count:] = jnp.zeros((slots - count, 2 * width), BF16)
            grad_img_ref[0, count:] = jnp.zeros((slots - count, width), BF16)

    @pl.when(valid <= 0)
    def _():
        grad_query_ref[...] = jnp.zeros_like(grad_query_ref)
        grad_kv_ref[place] = jnp.zeros((slots, 2 * width), BF16)
        grad_img_ref[...] = jnp.zeros_like(grad_img_ref)

    if short < slots:
        pl.when((valid > 0) & (valid <= short))(lambda: work(short))
        pl.when(valid > short)(lambda: work(slots))
    else:
        pl.when(valid > 0)(lambda: work(slots))

    @pl.when(place == batch - 1)
    def _():
        left = img_ref[...].reshape(batch * slots, width)
        right = grad_kv_ref[...].reshape(batch * slots, 2 * width)
        acc_ref[...] += dot_tn(left, right)

    @pl.when(cap == pl.num_programs(0) - 1)
    def _():
        side = side_ref[0]
        own = pl.ds(pl.multiple_of(side * width, width), width)
        other = pl.ds(pl.multiple_of((1 - side) * width, width), width)
        mine_ref[...] = acc_ref[:, own].astype(BF16)
        send_ref[...] = acc_ref[:, other].astype(BF16)


def cross_back(valid, side, kv, queries, grads, lse, delta, kv_mat, images, short):
    caps, slots, double = kv.shape
    width = double // 2
    length = queries.shape[1]
    batch = 4 if caps % 4 == 0 else 1
    block = lambda *shape: pl.BlockSpec((1,) + shape, lambda i, *_: (i, 0, 0))
    sds = jax.ShapeDtypeStruct
    return pl.pallas_call(
        functools.partial(cross_back_body, short=short),
        grid_spec=pltpu.PrefetchScalarGridSpec(
            num_scalar_prefetch=2,
            grid=(caps,),
            in_specs=[
                block(slots, double), block(length, width), block(length, width),
                block(GROUPS, LANES), block(GROUPS, LANES), whole(kv_mat.shape),
                pl.BlockSpec((batch, slots, width), lambda i, *_: (i // batch, 0, 0)),
            ],
            out_specs=[
                block(length, width), block(slots, width), whole((width, width)), whole((width, width)),
            ],
            scratch_shapes=[
                pltpu.VMEM((batch, slots, double), BF16), pltpu.VMEM((width, double), F32),
            ],
        ),
        out_shape=[
            sds((caps, length, width), BF16), sds((caps, slots, width), BF16),
            sds((width, width), BF16), sds((width, width), BF16),
        ],
        compiler_params=pltpu.CompilerParams(vmem_limit_bytes=VMEM_LIMIT),
        name="cross_back",
    )(valid, side, kv, queries, grads, lse, delta, kv_mat, images)


def add_low(first, second):
    return (first.astype(F32) + second.astype(F32)).astype(BF16)


class Piece:
    def __init__(self, sums, source, out, col, width, bits, order, recvs, mine=None, send=None, kv_recv=None):
        self.sums, self.out, self.col, self.width = sums, out, col, width
        self.bits, self.order, self.recvs = list(bits), list(order), recvs
        self.mine, self.send, self.kv_recv = mine, send, kv_recv
        self.now, self.holds, self.pending = 0, source, None

    def columns(self, ref):
        return (slice(None), pl.ds(self.col, self.width) if ref.shape[-1] != self.width else slice(None))

    def start_kv(self):
        whole_lead = (slice(None),) * len(self.bits)
        self.pending = self.sums.copy(
            self.send.at[whole_lead + self.columns(self.send)], self.kv_recv, {"kv": 1 - self.sums.side}
        )
        self.pending.start()

    def start(self):
        bit = self.order[self.now]
        lead = tuple(1 - self.sums.own(bit) if b == bit else slice(None) for b in self.bits)
        self.pending = self.sums.copy(
            self.holds.at[lead + self.columns(self.holds)], self.recvs[self.now], self.sums.partner(bit)
        )
        self.pending.start()

    def add(self, kept, arrived, cols, left, fixed):
        def one(i, carry):
            inner = {b: (i // (1 << (len(left) - 1 - d))) % 2 for d, b in enumerate(left)}
            lead = tuple(inner[b] if b in inner else fixed[b] for b in self.bits)
            into = tuple(inner[b] for b in left)
            arrived[into] = add_low(kept[lead + cols], arrived[into])
            return carry

        lax.fori_loop(0, 1 << len(left), one, 0)

    def advance(self):
        if self.pending is None:
            return True
        self.pending.wait()
        self.pending = None
        if self.holds is None:
            self.add(self.mine, self.kv_recv, self.columns(self.mine), self.bits, {})
            self.holds = self.kv_recv
            self.start()
            return False
        bit = self.order[self.now]
        arrived, cols = self.recvs[self.now], self.columns(self.holds)
        left = [b for b in self.bits if b != bit]
        if not left:
            total = self.holds[(self.sums.own(bit),) + cols].astype(F32) + arrived[...].astype(F32)
            self.out[:, self.col : self.col + self.width] = total
            return True
        self.add(self.holds, arrived, cols, left, {bit: self.sums.own(bit)})
        self.bits, self.holds, self.now = left, arrived, self.now + 1
        self.start()
        return False


class Sums:
    def __init__(self, send_sem, recv_sem):
        self.send_sem, self.recv_sem, self.count = send_sem, recv_sem, 0
        self.me, self.side = lax.axis_index("dp"), lax.axis_index("kv")

    def own(self, bit):
        return (self.me // (1 << bit)) % 2

    def partner(self, bit):
        return {"dp": self.me + (1 - 2 * self.own(bit)) * (1 << bit)}

    def copy(self, src, dst, device):
        index = self.count
        self.count += 1
        return pltpu.make_async_remote_copy(
            src_ref=src, dst_ref=dst, send_sem=self.send_sem.at[index], recv_sem=self.recv_sem.at[index],
            device_id=device, device_id_type=pl.DeviceIdType.MESH,
        )

    def greet(self, bits):
        barrier = pltpu.get_barrier_semaphore()
        for device in [{"kv": 1 - self.side}] + [self.partner(bit) for bit in bits]:
            pl.semaphore_signal(barrier, inc=1, device_id=device, device_id_type=pl.DeviceIdType.MESH)
        pl.semaphore_wait(barrier, 1 + len(bits))


def turned(bits, by):
    first = bits[:-1]
    by %= len(first)
    return first[by:] + first[:by] + bits[-1:]


def end_body(
    back_hbm, hidden_hbm, grad_two_hbm, att_hbm, qkv_hbm, tok_hbm, qkv_mat_hbm, out_mat_hbm, query_mat_hbm,
    gain_one, shift_one, gain_two, shift_two, gain_three, shift_three,
    up_ref, down_ref, cross_ref, kv_mine, kv_send,
    grad_tok, up_out, down_out, cross_out, qkv_out, out_out, query_out, kv_out, gains_out,
    *scratch, plan, bits, length, tile
):
    scratch = list(scratch)
    (
        send_sem, recv_sem, load_sem, back_one, back_two, hidden, grad_two, att, qkv, tok, qkv_mat,
        out_mat, query_mat, back_sum, normed, low, grad_att, grad_qkv, acc, gains_all, gain_kv,
        gain_buf, gain_recv, qkv_mine, qkv_send, out_mine, out_send, query_mine, query_send,
    ) = scratch[:29]
    rest = scratch[29:]
    sums = Sums(send_sem, recv_sem)
    side = sums.side
    captions = back_one.shape[0]
    rows, width = hidden.shape
    half = width // 2
    named = dict(
        up=(up_ref, None, None, up_out), down=(down_ref, None, None, down_out),
        cross=(cross_ref, None, None, cross_out), qkv=(None, qkv_mine, qkv_send, qkv_out),
        out=(None, out_mine, out_send, out_out), query=(None, query_mine, query_send, query_out),
        kv=(None, kv_mine, kv_send, kv_out),
    )
    pieces = {}
    for name, col, cols, axes, order, kv in plan:
        source, mine, send, out = named[name]
        kv_recv = rest.pop(0) if kv else None
        recvs = [rest.pop(0) for _ in order]
        pieces.setdefault(name, []).append(
            Piece(sums, source, out, col, cols, axes, order, recvs, mine, send, kv_recv)
        )
    early = pieces["up"] + pieces["down"] + pieces["cross"]
    image = pieces["kv"]
    middle = pieces["query"] + pieces["out"]
    late = pieces["qkv"]

    own_caps = pl.ds(pl.multiple_of(side * captions, captions), captions)
    other_caps = pl.ds(pl.multiple_of((1 - side) * captions, captions), captions)
    pairs = [
        (back_hbm.at[own_caps], back_one), (hidden_hbm, hidden), (query_mat_hbm, query_mat),
        (grad_two_hbm, grad_two), (out_mat_hbm, out_mat), (att_hbm, att), (qkv_hbm, qkv),
        (tok_hbm, tok), (qkv_mat_hbm, qkv_mat),
    ]
    loads = [pltpu.make_async_copy(src, dst, load_sem.at[i]) for i, (src, dst) in enumerate(pairs)]
    for load in loads:
        load.start()
    sums.greet(bits)
    swap = sums.copy(back_hbm.at[other_caps], back_two, {"kv": 1 - side})
    swap.start()
    for piece in image:
        piece.start_kv()
    for piece in early:
        piece.start()
    gains_all[...] = jnp.zeros_like(gains_all)
    gains_all[4:5] = gain_three[...]
    gains_all[5:6] = shift_three[...]
    for load in loads[:5]:
        load.wait()
    swap.wait()

    def rows_at(index):
        return pl.ds(pl.multiple_of(index * tile, tile), tile)

    def query_back(index, carry):
        span = rows_at(index)
        caps = pl.ds(index * (tile // length), tile // length)
        back = add_low(back_one[caps], back_two[caps]).reshape(tile, width)
        back_sum[span, :] = back
        unit, inverse = normalize(hidden[span, :])
        normed[span, :] = (unit * as_row(gain_two) + as_row(shift_two)).astype(BF16)
        grad = dot_nt(back, query_mat[...])
        gains_all[2:3] += jnp.sum(grad * unit, axis=0, keepdims=True)
        gains_all[3:4] += jnp.sum(grad, axis=0, keepdims=True)
        grad_one = grad_two[span, :] + norm_back(grad, as_row(gain_two), unit, inverse)
        grad_two[span, :] = grad_one
        low[span, :] = grad_one.astype(BF16)
        grad_att[span, :] = dot_nt(grad_one.astype(BF16), out_mat[...]).astype(BF16)
        return carry

    lax.fori_loop(0, rows // tile, query_back, 0)
    for piece in image:
        piece.advance()

    def weight(left, right, target, which):
        cols = target.shape[-1]
        block = target.shape[-2]
        start = pl.multiple_of(which * cols, 128)
        acc[:, :cols] = dot_tn(left[...], right[:, pl.ds(start, cols)])

        def one(i, carry):
            lead = tuple((i // (1 << (len(bits) - 1 - d))) % 2 for d in range(len(bits)))
            span = pl.ds(i * block, block) if isinstance(i, int) else pl.ds(pl.multiple_of(i * block, 8), block)
            target[lead] = acc[span, :cols].astype(BF16)
            return carry

        if block % 8 == 0:
            lax.fori_loop(0, 1 << len(bits), one, 0)
        else:
            for i in range(1 << len(bits)):
                one(i, 0)

    def weights(left, right, mine, send, group):
        weight(left, right, send, 1 - side)
        for piece in group:
            piece.start_kv()
        weight(left, right, mine, side)

    weights(normed, back_sum, query_mine, query_send, pieces["query"])
    loads[5].wait()
    loads[6].wait()
    weights(att, low, out_mine, out_send, pieces["out"])
    for piece in middle:
        piece.advance()

    mask = same_head()
    causal = causal_mask(length)

    def attend(cap, carry):
        span = pl.ds(pl.multiple_of(cap * length, length), length)
        for group in range(GROUPS):
            lo = group * LANES
            query = spread(qkv[span, lo : lo + LANES] * SCALE, mask)
            key = qkv[span, width + lo : width + lo + LANES]
            value = qkv[span, 2 * width + lo : 2 * width + lo + LANES]
            cot = spread(grad_att[span, lo : lo + LANES], mask)
            scores = jnp.where(causal, dot_nt(key, query), NEG)
            exponent = jnp.exp(scores - jnp.max(scores, axis=0, keepdims=True))
            probs = exponent / jnp.sum(exponent, axis=0, keepdims=True)
            grad_probs = dot_nt(value, cot)
            mean = jnp.sum(probs * grad_probs, axis=0, keepdims=True)
            grad_scores = (probs * (grad_probs - mean)).astype(BF16)
            grad_q = gather_heads(dot_tn(grad_scores, key)) * SCALE
            grad_qkv[span, lo : lo + LANES] = grad_q.astype(BF16)
            grad_qkv[span, width + lo : width + lo + LANES] = dot(grad_scores, query).astype(BF16)
            grad_qkv[span, 2 * width + lo : 2 * width + lo + LANES] = dot(
                probs.astype(BF16), cot
            ).astype(BF16)
        return carry

    lax.fori_loop(0, captions // 2, attend, 0)
    lax.fori_loop(captions // 2, captions, attend, 0)
    for piece in early:
        piece.advance()
    loads[7].wait()
    loads[8].wait()

    def token_norm(index, carry):
        span = rows_at(index)
        unit, _ = normalize(tok[span, :].astype(F32))
        normed[span, :] = (unit * as_row(gain_one) + as_row(shift_one)).astype(BF16)
        return carry

    lax.fori_loop(0, rows // tile, token_norm, 0)
    weights(normed, grad_qkv, qkv_mine, qkv_send, late)
    for piece in late + image:
        piece.advance()

    def token_back(index, carry):
        span = rows_at(index)
        unit, inverse = normalize(tok[span, :].astype(F32))
        grad = dot_nt(grad_qkv[span, :], qkv_mat[...])
        gains_all[0:1] += jnp.sum(grad * unit, axis=0, keepdims=True)
        gains_all[1:2] += jnp.sum(grad, axis=0, keepdims=True)
        back = grad_two[span, :] + norm_back(grad, as_row(gain_one), unit, inverse)
        grad_tok[span, :] = back.astype(BF16)
        return carry

    lax.fori_loop(0, rows // tile, token_back, 0)
    own_cols = pl.ds(pl.multiple_of(side * half, 128), half)
    other_cols = pl.ds(pl.multiple_of((1 - side) * half, 128), half)
    gain_copy = sums.copy(gains_all.at[:, other_cols], gain_kv, {"kv": 1 - side})
    gain_copy.start()
    stage = -1
    everything = early + image + middle + late
    while stage < len(bits) or not all(piece.pending is None for piece in everything):
        if stage < len(bits):
            gain_copy.wait()
            if stage < 0:
                gain_buf[0] = gains_all[:, own_cols] + gain_kv[...]
            else:
                gain_buf[stage + 1] = gain_buf[stage] + gain_recv[stage]
            stage += 1
            if stage < len(bits):
                gain_copy = sums.copy(gain_buf.at[stage], gain_recv.at[stage], sums.partner(bits[stage]))
                gain_copy.start()
            else:
                gains_out[...] = gain_buf[stage]
        for piece in everything:
            piece.advance()


def end(
    back, hidden, grad_two, att, qkv, tokens, qkv_mat, out_mat, query_mat, gain_one, shift_one,
    gain_two, shift_two, gain_three, shift_three, early, kv_mine, kv_send, length, size
):
    bits = list(range(size.bit_length() - 1))
    axes = bits[::-1]
    rows, width = hidden.shape
    captions = rows // length
    tile = min(256, rows)
    block = width // size
    lead = (2,) * len(bits)
    up, down, cross = early
    cut_up = up.shape[-1] // 384 * 256
    cut_down = down.shape[-1] // 384 * 256
    third = width // 3
    early_order = lambda by, array: [b for b in turned(bits, by) if b in bits[len(bits) + 2 - array.ndim :]]
    early_axes = lambda array: axes[: array.ndim - 2]
    plan = []
    for name, array, cuts in (
        ("up", up, ((0, cut_up, 0), (cut_up, up.shape[-1] - cut_up, 2))),
        ("down", down, ((0, cut_down, 1), (cut_down, down.shape[-1] - cut_down, 2))),
        ("cross", cross, ((0, cross.shape[-1], 1),)),
    ):
        for col, cols, by in cuts:
            plan.append((name, col, cols, early_axes(array), early_order(by, array), False))
    plan.append(("query", 0, width // 2, axes, turned(bits, 0), True))
    plan.append(("out", 0, width // 2, axes, turned(bits, 1), True))
    for by in range(3):
        plan.append(("kv", by * third, third, axes, turned(bits, by), True))
        plan.append(("qkv", by * (width // 2), width // 2, axes, turned(bits, by), True))
    heights = dict(up=up.shape[-2], down=down.shape[-2], cross=cross.shape[-2])
    buffers = []
    copies = 2 + len(bits)
    for name, col, cols, piece_axes, order, kv in plan:
        shape = (heights.get(name, block), cols)
        for count in range(len(order) if kv else len(order) - 1, -1, -1):
            buffers.append(pltpu.VMEM((2,) * count + shape, BF16))
            copies += 1
    vmem = pl.BlockSpec(memory_space=pltpu.VMEM)
    hbm = pl.BlockSpec(memory_space=pl.ANY)
    sds = jax.ShapeDtypeStruct
    cut = lambda cols: pltpu.VMEM(lead + (block, cols), BF16)
    outs = [sds((rows, width), BF16)]
    outs += [sds(v.shape[-2:], F32) for v in (up, down, cross)]
    outs += [sds((block, cols), F32) for cols in (3 * width // 2, width // 2, width // 2, width)]
    outs += [sds((8, width // 2), F32)]
    low_rows = lambda cols: pltpu.VMEM((rows, cols), BF16)
    return pl.pallas_call(
        functools.partial(end_body, plan=plan, bits=bits, length=length, tile=tile),
        in_specs=[hbm] * 9 + [vmem] * 6 + [vmem] * 4 + [hbm],
        out_specs=[vmem] * len(outs),
        out_shape=outs,
        scratch_shapes=[
            pltpu.SemaphoreType.DMA((copies,)), pltpu.SemaphoreType.DMA((copies,)),
            pltpu.SemaphoreType.DMA((9,)),
            pltpu.VMEM((captions, length, width), BF16), pltpu.VMEM((captions, length, width), BF16),
            pltpu.VMEM((rows, width), F32), pltpu.VMEM((rows, width), F32), low_rows(width),
            low_rows(3 * width), low_rows(width), pltpu.VMEM(qkv_mat.shape, BF16),
            pltpu.VMEM(out_mat.shape, BF16), pltpu.VMEM(query_mat.shape, BF16),
            low_rows(width), low_rows(width), low_rows(width), low_rows(width), low_rows(3 * width),
            pltpu.VMEM((width, 3 * width // 2), F32), pltpu.VMEM((8, width), F32),
            pltpu.VMEM((8, width // 2), F32), pltpu.VMEM((len(bits) + 1, 8, width // 2), F32),
            pltpu.VMEM((len(bits), 8, width // 2), F32),
            cut(3 * width // 2), cut(3 * width // 2), cut(width // 2), cut(width // 2),
            cut(width // 2), cut(width // 2),
        ] + buffers,
        compiler_params=pltpu.CompilerParams(
            vmem_limit_bytes=VMEM_MOST, collective_id=0, has_side_effects=True
        ),
        name="end",
    )(
        back, hidden, grad_two, att, qkv, tokens, qkv_mat, out_mat, query_mat, gain_one, shift_one,
        gain_two, shift_two, gain_three, shift_three, up, down, cross, kv_mine, kv_send,
    )


def hand_over_body(*refs):
    count = len(refs) // 2
    for source, target in zip(refs[:count], refs[count:]):
        target[...] = source[...]


def hand_over(*arrays):
    vmem = pl.BlockSpec(memory_space=pltpu.VMEM)
    return pl.pallas_call(
        hand_over_body,
        in_specs=[vmem] * len(arrays),
        out_specs=[vmem] * len(arrays),
        out_shape=[jax.ShapeDtypeStruct(v.shape, v.dtype) for v in arrays],
        name="hand_over",
    )(*arrays)


def exchange(value, axis, bit, size):
    return lax.ppermute(value, axis, [(i, i ^ bit) for i in range(size)])


def split_rows(array, size):
    bits = size.bit_length() - 1
    return array.reshape((2,) * bits + (array.shape[0] // size, array.shape[1]))


def body(
    tokens, images, image_counts, cotangent, norm1_gain, norm1_shift, self_qkv, self_out,
    norm2_gain, norm2_shift, cross_q, cross_kv, cross_out, norm3_gain, norm3_shift, w_up, w_down,
):
    captions, length, width = tokens.shape
    caps, slots, _ = images.shape
    side = lax.axis_index("kv")
    me = lax.axis_index("dp")
    groups = lax.axis_size("dp")
    side_arr = side.reshape(1)
    row = lambda v: v
    tok = tokens.reshape(captions * length, width)
    cot = cotangent.reshape(captions * length, width)
    short = -(-SHORT // 16) * 16
    valid = jnp.clip(image_counts - side * slots, 0, slots)
    swap = lambda v: exchange(v, "kv", 1, 2)

    qkv, att, hidden, query = token_start(
        tok, row(norm1_gain), row(norm1_shift), self_qkv, self_out, row(norm2_gain),
        row(norm2_shift), cross_q, length,
    )

    def both(own):
        other = swap(own)
        first = jnp.where(side == 0, own, other)
        second = jnp.where(side == 0, other, own)
        return jnp.concatenate([first, second], axis=0)

    def own_part(array):
        return lax.dynamic_slice_in_dim(array, side * captions, captions, 0)

    def other_part(array):
        return lax.dynamic_slice_in_dim(array, (1 - side) * captions, captions, 0)

    queries = both(query.reshape(captions, length, width))
    kv, part, lse_part = cross_start(valid, images, cross_kv, queries, short)
    flat = lambda v: v.reshape(captions * length, width)
    (
        layer_out, grad_two, grad_att, lse, delta, up_mine, up_send, down_mine, down_send,
        cross_mine, cross_send, gain3, shift3,
    ) = feed(
        side_arr, flat(own_part(part)), own_part(lse_part), flat(swap(other_part(part))),
        swap(other_part(lse_part)), hidden, cot, cross_out, row(norm3_gain), row(norm3_shift),
        w_up, w_down, length,
    )
    early = [
        split_rows(add_low(mine, exchange(send, "kv", 1, 2)), groups)
        for mine, send in ((up_mine, up_send), (down_mine, down_send), (cross_mine, cross_send))
    ]

    grads = both(grad_att.reshape(captions, length, width))
    back, images_grad, kv_mine, kv_send = cross_back(
        valid, side_arr, kv, queries, grads, both(lse), both(delta), cross_kv, images, short
    )
    cut = lambda v: split_rows(v, groups)
    (
        tokens_grad, w_up_grad, down_grad, cross_out_grad, self_qkv_grad, self_out_grad, cross_q_grad,
        cross_kv_grad, gains,
    ) = hand_over(*end(
        back, hidden, grad_two, att, qkv, tok, self_qkv, self_out, cross_q, norm1_gain, norm1_shift,
        norm2_gain, norm2_shift, gain3, shift3, early, cut(kv_mine), cut(kv_send), length, groups,
    ))
    return (
        layer_out.reshape(captions, length, width),
        tokens_grad.reshape(captions, length, width),
        images_grad,
        gains[0], gains[1], self_qkv_grad, self_out_grad, gains[2], gains[3], cross_q_grad,
        cross_kv_grad, cross_out_grad, gains[4], gains[5], w_up_grad, down_grad,
    )


def solution(mesh):
    return jax.shard_map(
        body,
        mesh=mesh,
        in_specs=(
            P(("dp", "kv"), None, None), P("dp", "kv", None), P("dp"), P(("dp", "kv"), None, None),
        ) + (P(),) * 13,
        out_specs=(
            P(("dp", "kv"), None, None), P(("dp", "kv"), None, None), P("dp", "kv", None),
            P("kv"), P("kv"), P("dp", "kv"), P("dp", "kv"), P("kv"), P("kv"), P("dp", "kv"),
            P("dp", "kv"), P("dp", "kv"), P("kv"), P("kv"), P("dp", "kv"), P("dp", "kv"),
        ),
        check_vma=False,
    )
```

```python
import functools

import jax
import jax.numpy as jnp
from jax import lax
from jax.experimental import pallas as pl
from jax.experimental.pallas import tpu as pltpu
from jax.sharding import PartitionSpec as P

HEADS = 12
HEAD_DIM = 64
SHORT = 196
LANES = 256
PACK = LANES // HEAD_DIM
GROUPS = HEADS // PACK
SCALE = HEAD_DIM ** (-0.5)
NEG = -1e30
F32 = jnp.float32
BF16 = jnp.bfloat16
VMEM_LIMIT = 60 * 1024 * 1024
VMEM_MOST = 67043328


def dot(a, b):
    return jnp.dot(a, b, preferred_element_type=F32)


def dot_nt(a, b):
    return lax.dot_general(a, b, (((1,), (1,)), ((), ())), preferred_element_type=F32)


def dot_tn(a, b):
    return lax.dot_general(a, b, (((0,), (0,)), ((), ())), preferred_element_type=F32)


def normalize(values):
    centered = values - jnp.mean(values, axis=-1, keepdims=True)
    inverse = lax.rsqrt(jnp.mean(centered * centered, axis=-1, keepdims=True) + 1e-05)
    return centered * inverse, inverse


def norm_back(grad, gain, unit, inverse):
    scaled = grad * gain
    mean_one = jnp.mean(scaled, axis=-1, keepdims=True)
    mean_two = jnp.mean(scaled * unit, axis=-1, keepdims=True)
    return (scaled - mean_one - unit * mean_two) * inverse


def as_row(ref):
    return ref[...].reshape(1, ref.shape[0])


def iota(shape, dim):
    return lax.broadcasted_iota(jnp.int32, shape, dim)


def same_head():
    shape = (LANES, LANES)
    return (iota(shape, 0) // HEAD_DIM) == (iota(shape, 1) // HEAD_DIM)


def spread(rows, mask):
    stacked = jnp.concatenate([rows] * PACK, axis=0)
    return jnp.where(mask, stacked, jnp.zeros_like(stacked))


def gather_heads(full):
    count = full.shape[0] // PACK
    head = iota((count, LANES), 1) // HEAD_DIM
    out = full[:count]
    for index in range(1, PACK):
        out = jnp.where(head == index, full[index * count : (index + 1) * count], out)
    return out


def split_two(value):
    high = value.astype(BF16)
    return high, (value - high.astype(F32)).astype(BF16)


def lanes_to_rows(row, mask_low):
    shape = (HEAD_DIM, LANES)
    pick = iota(shape, 0) == (iota(shape, 1) % HEAD_DIM)
    high, low = split_two(jnp.where(pick, row, 0.0))
    return dot(high, mask_low) + dot(low, mask_low)


def rows_to_lanes(rows, mask_low):
    high, low = split_two(rows)
    summed = dot(high, mask_low) + dot(low, mask_low)
    shape = (HEAD_DIM, LANES)
    pick = iota(shape, 0) == (iota(shape, 1) % HEAD_DIM)
    return jnp.sum(jnp.where(pick, summed, 0.0), axis=0, keepdims=True)


def lane_slice(group):
    return slice(group * LANES, (group + 1) * LANES)


def causal_mask(length):
    shape = (length, LANES)
    return iota(shape, 0) <= (iota(shape, 1) % HEAD_DIM)


def token_start_body(
    tok_ref, gain_one, shift_one, qkv_mat, out_mat, gain_two, shift_two, query_mat,
    qkv_ref, att_ref, hidden_ref, query_ref, *, length
):
    x = tok_ref[...].astype(F32)
    unit, _ = normalize(x)
    normed = (unit * as_row(gain_one) + as_row(shift_one)).astype(BF16)
    width = x.shape[1]
    qkv_ref[...] = dot(normed, qkv_mat[...]).astype(BF16)
    mask = same_head()
    causal = causal_mask(length)
    for cap in range(x.shape[0] // length):
        rows = slice(cap * length, (cap + 1) * length)
        for group in range(GROUPS):
            lo = group * LANES
            query = qkv_ref[rows, lo : lo + LANES] * SCALE
            key = qkv_ref[rows, width + lo : width + lo + LANES]
            value = qkv_ref[rows, 2 * width + lo : 2 * width + lo + LANES]
            scores = jnp.where(causal, dot_nt(key, spread(query, mask)), NEG)
            exponent = jnp.exp(scores - jnp.max(scores, axis=0, keepdims=True))
            probs = exponent / jnp.sum(exponent, axis=0, keepdims=True)
            full = dot_tn(probs.astype(BF16), value)
            att_ref[rows, lo : lo + LANES] = gather_heads(full).astype(BF16)
    hidden = x + dot(att_ref[...], out_mat[...])
    hidden_ref[...] = hidden
    unit, _ = normalize(hidden)
    normed = (unit * as_row(gain_two) + as_row(shift_two)).astype(BF16)
    query_ref[...] = (dot(normed, query_mat[...]).astype(BF16).astype(F32) * SCALE).astype(BF16)


def whole(shape):
    zeros = (0,) * len(shape)
    return pl.BlockSpec(shape, lambda *_: zeros)


def token_start(tokens, gain_one, shift_one, qkv_mat, out_mat, gain_two, shift_two, query_mat, length):
    rows, width = tokens.shape
    tile = min(256, rows)
    row_block = lambda cols: pl.BlockSpec((tile, cols), lambda i: (i, 0))
    return pl.pallas_call(
        functools.partial(token_start_body, length=length),
        grid=(rows // tile,),
        in_specs=[
            row_block(width), whole((width,)), whole((width,)), whole(qkv_mat.shape),
            whole(out_mat.shape), whole((width,)), whole((width,)), whole(query_mat.shape),
        ],
        out_specs=[row_block(3 * width), row_block(width), row_block(width), row_block(width)],
        out_shape=[
            jax.ShapeDtypeStruct((rows, 3 * width), BF16),
            jax.ShapeDtypeStruct((rows, width), BF16),
            jax.ShapeDtypeStruct((rows, width), F32),
            jax.ShapeDtypeStruct((rows, width), BF16),
        ],
        compiler_params=pltpu.CompilerParams(vmem_limit_bytes=VMEM_LIMIT),
        name="token_start",
    )(tokens, gain_one, shift_one, qkv_mat, out_mat, gain_two, shift_two, query_mat)


def cross_start_body(valid_ref, img_ref, kv_mat, query_ref, kv_ref, att_ref, lse_ref, *, short):
    cap = pl.program_id(0)
    valid = valid_ref[cap]
    width = query_ref.shape[2]
    slots = img_ref.shape[1]

    def work(count):
        kv_ref[0, :count] = dot(img_ref[0, :count], kv_mat[...]).astype(BF16)
        mask = same_head()
        inside = iota((count, LANES), 0) < valid
        for group in range(GROUPS):
            lo = group * LANES
            key = kv_ref[0, :count, lo : lo + LANES]
            value = kv_ref[0, :count, width + lo : width + lo + LANES]
            scores = dot_nt(key, spread(query_ref[0, :, lo : lo + LANES], mask))
            scores = jnp.where(inside, scores, NEG)
            peak = jnp.max(scores, axis=0, keepdims=True)
            exponent = jnp.where(inside, jnp.exp(scores - peak), 0.0)
            total = jnp.sum(exponent, axis=0, keepdims=True)
            probs = (exponent * (1.0 / total)).astype(BF16)
            att_ref[0, :, lo : lo + LANES] = gather_heads(dot_tn(probs, value)).astype(BF16)
            lse_ref[0, group : group + 1] = peak + jnp.log(total)

    @pl.when(valid <= 0)
    def _():
        att_ref[...] = jnp.zeros_like(att_ref)
        lse_ref[...] = jnp.full_like(lse_ref, NEG)

    if short < slots:
        pl.when((valid > 0) & (valid <= short))(lambda: work(short))
        pl.when(valid > short)(lambda: work(slots))
    else:
        pl.when(valid > 0)(lambda: work(slots))


def cross_start(valid, images, kv_mat, queries, short):
    caps, slots, width = images.shape
    length = queries.shape[1]
    block = lambda *shape: pl.BlockSpec((1,) + shape, lambda i, *_: (i, 0, 0))
    return pl.pallas_call(
        functools.partial(cross_start_body, short=short),
        grid_spec=pltpu.PrefetchScalarGridSpec(
            num_scalar_prefetch=1,
            grid=(caps,),
            in_specs=[block(slots, width), whole(kv_mat.shape), block(length, width)],
            out_specs=[block(slots, 2 * width), block(length, width), block(GROUPS, LANES)],
        ),
        out_shape=[
            jax.ShapeDtypeStruct((caps, slots, 2 * width), BF16),
            jax.ShapeDtypeStruct((caps, length, width), BF16),
            jax.ShapeDtypeStruct((caps, GROUPS, LANES), F32),
        ],
        compiler_params=pltpu.CompilerParams(vmem_limit_bytes=VMEM_LIMIT),
        name="cross_start",
    )(valid, images, kv_mat, queries)


def feed_body(
    part_hbm, lse_hbm, hidden_ref, cot_ref, cross_mat, gain_ref, shift_ref, up_one, up_two, down_ref,
    out_ref, grad_two_ref, grads_hbm, lse_out, delta_out, up_keep, up_first, up_second, up_both,
    down_keep, down_away, cross_sum, gain_grad, shift_grad,
    send_sem, recv_sem, load_sem, att_one, att_two, lse_one, lse_two, att_full, att_low, hidden_two,
    normed_ref, acc_out, acc_grad, grad_att, lse_own, delta_own, up_pair, up_got, down_pair, down_got,
    cross_pair, cross_got, *, length, tile, bits, steps
):
    step = pl.program_id(0)
    me, side = lax.axis_index("dp"), lax.axis_index("kv")
    rows, width = hidden_ref.shape
    captions = rows // length
    tiles = rows // tile
    half = width // 2
    sub = up_one.shape[1]
    blocks = up_pair.shape[2]
    own = lambda bit: (me // (1 << bit)) % 2

    def remote(src, dst, index):
        return pltpu.make_async_remote_copy(
            src_ref=src, dst_ref=dst, send_sem=send_sem.at[index], recv_sem=recv_sem.at[index],
            device_id={"kv": 1 - side}, device_id_type=pl.DeviceIdType.MESH,
        )

    def row_span(index):
        return pl.ds(pl.multiple_of(index * tile, tile), tile)

    def chunk_copies(slot):
        return (
            remote(up_pair.at[slot, 1 - side], up_got.at[slot], 2 + slot),
            remote(down_pair.at[slot, 1 - side], down_got.at[slot], 4 + slot),
        )

    cross_copy = lambda: remote(cross_pair.at[1 - side], cross_got, 6)
    lse_copy = lambda: remote(lse_own, lse_out.at[side], 7)
    delta_copy = lambda: remote(delta_own, delta_out.at[side], 8)
    grad_copy = lambda index: remote(
        grad_att.at[pl.ds(index * tile, tile)], grads_hbm.at[side, pl.ds(index * tile, tile)], 9 + index
    )
    lse_store = lambda: pltpu.make_async_copy(lse_own, lse_out.at[side], load_sem.at[2])

    def cut(target, value):
        count, height, _ = target.shape
        if height % 16 == 0:
            target[...] = value.astype(BF16).reshape(target.shape)
        else:
            for index in range(count):
                target[index] = value[index * height : (index + 1) * height].astype(BF16)

    @pl.when(step == 0)
    def _():
        part_load = pltpu.make_async_copy(part_hbm.at[side], att_one, load_sem.at[0])
        lse_load = pltpu.make_async_copy(lse_hbm.at[side], lse_one, load_sem.at[1])
        part_load.start()
        lse_load.start()
        barrier = pltpu.get_barrier_semaphore()
        pl.semaphore_signal(barrier, inc=1, device_id={"kv": 1 - side}, device_id_type=pl.DeviceIdType.MESH)
        pl.semaphore_wait(barrier, 1)
        part_swap = remote(part_hbm.at[1 - side], att_two, 0)
        lse_swap = remote(lse_hbm.at[1 - side], lse_two, 1)
        lse_swap.start()
        part_swap.start()
        mask_low = same_head().astype(BF16)
        lse_load.wait()
        part_load.wait()
        lse_swap.wait()
        part_swap.wait()

        def one_caption(cap, carry):
            span = pl.ds(pl.multiple_of(cap * length, length), length)
            for group in range(GROUPS):
                lo = group * LANES
                first = lse_one[cap, group : group + 1]
                second = lse_two[cap, group : group + 1]
                peak = jnp.maximum(first, second)
                lse = peak + jnp.log(jnp.exp(first - peak) + jnp.exp(second - peak))
                lse_own[cap, group : group + 1] = lse
                weight_one = lanes_to_rows(jnp.exp(first - lse), mask_low)
                weight_two = lanes_to_rows(jnp.exp(second - lse), mask_low)
                mixed = (
                    weight_one * att_one[span, lo : lo + LANES].astype(F32)
                    + weight_two * att_two[span, lo : lo + LANES].astype(F32)
                )
                att_full[span, lo : lo + LANES] = mixed
                att_low[span, lo : lo + LANES] = mixed.astype(BF16)
            return carry

        lax.fori_loop(0, captions, one_caption, 0)
        lse_copy().start()
        lse_store().start()

        def one_tile(index, carry):
            span = row_span(index)
            two = hidden_ref[span, :] + dot(att_low[span, :], cross_mat[...])
            hidden_two[span, :] = two
            unit, _ = normalize(two)
            normed_ref[span, :] = (unit * as_row(gain_ref) + as_row(shift_ref)).astype(BF16)
            acc_out[span, :] = two
            acc_grad[span, :] = jnp.zeros_like(two)
            return carry

        lax.fori_loop(0, tiles, one_tile, 0)

    slot = step % 2
    up_mat = jnp.concatenate([up_one[...], up_two[...]], axis=1)
    down_mat = down_ref[...].reshape(2 * sub, width)
    pre = dot(normed_ref[...], up_mat)
    cdf = 0.5 * (1.0 + lax.erf(pre * 0.7071067811865476))
    act = (pre * cdf).astype(BF16)
    acc_out[...] += dot(act, down_mat)
    cot = cot_ref[...]
    density = jnp.exp(-0.5 * pre * pre) * 0.3989422804014327
    grad_up = (dot_nt(cot, down_mat) * (cdf + pre * density)).astype(BF16)
    acc_grad[...] += dot_nt(grad_up, up_mat)
    grad_down = dot_tn(act, cot).astype(BF16)
    grad_w = dot_tn(normed_ref[...], grad_up)
    for part in range(2):
        cut(up_pair.at[slot, part], grad_w[:, part * sub : (part + 1) * sub])
        down_pair[slot, part] = grad_down[:, part * half : (part + 1) * half].reshape(2, sub, half)

    def take(chunk, place):
        for copy in chunk_copies(place):
            copy.wait()
        cols = pl.ds(pl.multiple_of(chunk * sub, sub), sub)
        for index, target in enumerate((up_keep, up_first, up_second, up_both)):
            flip = (index % 2, index // 2)
            low_bit, high_bit = (own(b) + f - 2 * own(b) * f for b, f in zip(bits[:2], flip))
            near = high_bit * 2 + low_bit

            def one(block, carry):
                source = block * 4 + near
                target[block, :, cols] = add_low(up_pair[place, side, source], up_got[place, source])
                return carry

            lax.fori_loop(0, blocks // 4, one, 0)
        total = add_low(down_pair[place, side], down_got[place])
        span = pl.ds(pl.multiple_of(chunk % (steps // 2) * sub, sub), sub)
        stays = chunk // (steps // 2) == own(bits[-2])

        @pl.when(stays)
        def _():
            down_keep[:, span, :] = total

        @pl.when(jnp.logical_not(stays))
        def _():
            down_away[:, span, :] = total

    @pl.when(step > 0)
    def _():
        take(step - 1, (step + 1) % 2)

    for copy in chunk_copies(slot):
        copy.start()

    @pl.when(step == steps - 1)
    def _():
        mask_low = same_head().astype(BF16)
        gain_grad[...] = jnp.zeros_like(gain_grad)
        shift_grad[...] = jnp.zeros_like(shift_grad)
        for index in range(tiles):
            span = pl.ds(index * tile, tile)
            unit, inverse = normalize(hidden_two[span, :])
            grad = acc_grad[span, :]
            gain_grad[...] += jnp.sum(grad * unit, axis=0, keepdims=True)
            shift_grad[...] += jnp.sum(grad, axis=0, keepdims=True)
            two = cot_ref[span, :].astype(F32) + norm_back(grad, as_row(gain_ref), unit, inverse)
            grad_two_ref[span, :] = two
            low = two.astype(BF16)
            normed_ref[span, :] = low
            grad_att[span, :] = dot_nt(low, cross_mat[...]).astype(BF16)
            grad_copy(index).start()
        grad_store = pltpu.make_async_copy(grad_att, grads_hbm.at[side], load_sem.at[0])
        grad_store.start()

        def one_caption(cap, carry):
            span = pl.ds(pl.multiple_of(cap * length, length), length)
            for group in range(GROUPS):
                lo = group * LANES
                product = grad_att[span, lo : lo + LANES].astype(F32) * att_full[span, lo : lo + LANES]
                delta_own[cap, group : group + 1] = rows_to_lanes(product, mask_low)
            return carry

        lax.fori_loop(0, captions, one_caption, 0)
        delta_copy().start()
        delta_store = pltpu.make_async_copy(delta_own, delta_out.at[side], load_sem.at[1])
        delta_store.start()
        grad_cross = dot_tn(att_low[...], normed_ref[...])
        for part in range(2):
            cut(cross_pair.at[part], grad_cross[:, part * half : (part + 1) * half])
        cross_copy().start()
        out_ref[...] = acc_out[...].astype(BF16)
        take(steps - 1, (steps - 1) % 2)
        cross_copy().wait()

        def one(block, carry):
            cross_sum[block] = add_low(cross_pair[side, block], cross_got[block])
            return carry

        lax.fori_loop(0, blocks, one, 0)
        for copy in [lse_copy(), lse_store(), delta_copy(), delta_store, grad_store]:
            copy.wait()
        for index in range(tiles):
            grad_copy(index).wait()


def feed(part, lse_part, hidden, cot, cross_mat, gain, shift, up_mat, down_mat, length, size):
    rows, width = hidden.shape
    captions = rows // length
    units = up_mat.shape[1]
    sub = 256
    steps = units // 2 // sub
    tile = min(256, rows)
    half = width // 2
    block = width // size
    bits = list(range(size.bit_length() - 1))
    stat = (captions, GROUPS, LANES)
    sds = jax.ShapeDtypeStruct
    once = lambda shape: pl.BlockSpec(shape, lambda *_: (0,) * len(shape), pipeline_mode=pl.Buffered(1))
    hbm = pl.BlockSpec(memory_space=pl.ANY)
    copies = 9 + rows // tile
    f32_rows = lambda: pltpu.VMEM((rows, width), F32)
    low_rows = lambda: pltpu.VMEM((rows, width), BF16)
    quarter = (size // 4, block, units // 2)
    return pl.pallas_call(
        functools.partial(feed_body, length=length, tile=tile, bits=bits, steps=steps),
        grid=(steps,),
        in_specs=[
            hbm, hbm, once((rows, width)), once((rows, width)), once((width, width)),
            once((width,)), once((width,)),
            pl.BlockSpec((width, sub), lambda i: (0, i)),
            pl.BlockSpec((width, sub), lambda i: (0, i + steps)),
            pl.BlockSpec((2, sub, width), lambda i: (0, i, 0)),
        ],
        out_specs=[
            whole((rows, width)), whole((rows, width)), hbm, hbm, hbm,
            whole(quarter), whole(quarter), whole(quarter), whole(quarter),
            whole((2, units // 4, half)), whole((2, units // 4, half)),
            whole((size, block, half)), whole((1, width)), whole((1, width)),
        ],
        out_shape=[
            sds((rows, width), BF16), sds((rows, width), F32), sds((2, rows, width), BF16),
            sds((2,) + stat, F32), sds((2,) + stat, F32),
            sds(quarter, BF16), sds(quarter, BF16), sds(quarter, BF16), sds(quarter, BF16),
            sds((2, units // 4, half), BF16), sds((2, units // 4, half), BF16),
            sds((size, block, half), BF16), sds((1, width), F32), sds((1, width), F32),
        ],
        scratch_shapes=[
            pltpu.SemaphoreType.DMA((copies,)), pltpu.SemaphoreType.DMA((copies,)),
            pltpu.SemaphoreType.DMA((3,)),
            low_rows(), low_rows(), pltpu.VMEM(stat, F32), pltpu.VMEM(stat, F32), f32_rows(), low_rows(),
            f32_rows(), low_rows(), f32_rows(), f32_rows(), low_rows(),
            pltpu.VMEM(stat, F32), pltpu.VMEM(stat, F32),
            pltpu.VMEM((2, 2, size, block, sub), BF16), pltpu.VMEM((2, size, block, sub), BF16),
            pltpu.VMEM((2, 2, 2, sub, half), BF16), pltpu.VMEM((2, 2, sub, half), BF16),
            pltpu.VMEM((2, size, block, half), BF16), pltpu.VMEM((size, block, half), BF16),
        ],
        compiler_params=pltpu.CompilerParams(
            vmem_limit_bytes=VMEM_MOST, collective_id=1, has_side_effects=True
        ),
        name="feed",
    )(
        part.reshape(2, rows, width), lse_part.reshape((2,) + stat), hidden, cot, cross_mat, gain, shift,
        up_mat, up_mat, down_mat.reshape(2, units // 2, width),
    )


def cross_back_body(
    valid_ref, side_ref, kv_ref, query_ref, grad_ref, lse_ref, delta_ref, kv_mat, img_ref,
    grad_query_ref, grad_img_ref, mine_ref, send_ref, grad_kv_ref, acc_ref, *, short
):
    cap = pl.program_id(0)
    valid = valid_ref[cap]
    width = query_ref.shape[2]
    slots = kv_ref.shape[1]
    batch = img_ref.shape[0]
    place = cap % batch

    @pl.when(cap == 0)
    def _():
        acc_ref[...] = jnp.zeros_like(acc_ref)

    def work(count):
        mask = same_head()
        inside = iota((count, LANES), 0) < valid
        for group in range(GROUPS):
            lo = group * LANES
            key = kv_ref[0, :count, lo : lo + LANES]
            value = kv_ref[0, :count, width + lo : width + lo + LANES]
            query = spread(query_ref[0, :, lo : lo + LANES], mask)
            grad = spread(grad_ref[0, :, lo : lo + LANES], mask)
            scores = dot_nt(key, query)
            probs = jnp.where(inside, jnp.exp(scores - lse_ref[0, group : group + 1]), 0.0)
            grad_probs = dot_nt(value, grad)
            grad_scores = (probs * (grad_probs - delta_ref[0, group : group + 1])).astype(BF16)
            back = gather_heads(dot_tn(grad_scores, key)) * SCALE
            grad_query_ref[0, :, lo : lo + LANES] = back.astype(BF16)
            grad_kv_ref[place, :count, lo : lo + LANES] = dot(grad_scores, query).astype(BF16)
            grad_kv_ref[place, :count, width + lo : width + lo + LANES] = dot(
                probs.astype(BF16), grad
            ).astype(BF16)
        grad_img_ref[0, :count] = dot_nt(grad_kv_ref[place, :count], kv_mat[...]).astype(BF16)
        if count < slots:
            grad_kv_ref[place, count:] = jnp.zeros((slots - count, 2 * width), BF16)
            grad_img_ref[0, count:] = jnp.zeros((slots - count, width), BF16)

    @pl.when(valid <= 0)
    def _():
        grad_query_ref[...] = jnp.zeros_like(grad_query_ref)
        grad_kv_ref[place] = jnp.zeros((slots, 2 * width), BF16)
        grad_img_ref[...] = jnp.zeros_like(grad_img_ref)

    if short < slots:
        pl.when((valid > 0) & (valid <= short))(lambda: work(short))
        pl.when(valid > short)(lambda: work(slots))
    else:
        pl.when(valid > 0)(lambda: work(slots))

    @pl.when(place == batch - 1)
    def _():
        left = img_ref[...].reshape(batch * slots, width)
        right = grad_kv_ref[...].reshape(batch * slots, 2 * width)
        acc_ref[...] += dot_tn(left, right)

    @pl.when(cap == pl.num_programs(0) - 1)
    def _():
        side = side_ref[0]
        own = pl.ds(pl.multiple_of(side * width, width), width)
        other = pl.ds(pl.multiple_of((1 - side) * width, width), width)
        mine_ref[...] = acc_ref[:, own].astype(BF16)
        send_ref[...] = acc_ref[:, other].astype(BF16)


def cross_back(valid, side, kv, queries, grads, lse, delta, kv_mat, images, short):
    caps, slots, double = kv.shape
    width = double // 2
    length = queries.shape[1]
    batch = 4 if caps % 4 == 0 else 1
    block = lambda *shape: pl.BlockSpec((1,) + shape, lambda i, *_: (i, 0, 0))
    sds = jax.ShapeDtypeStruct
    return pl.pallas_call(
        functools.partial(cross_back_body, short=short),
        grid_spec=pltpu.PrefetchScalarGridSpec(
            num_scalar_prefetch=2,
            grid=(caps,),
            in_specs=[
                block(slots, double), block(length, width), block(length, width),
                block(GROUPS, LANES), block(GROUPS, LANES), whole(kv_mat.shape),
                pl.BlockSpec((batch, slots, width), lambda i, *_: (i // batch, 0, 0)),
            ],
            out_specs=[
                block(length, width), block(slots, width), whole((width, width)), whole((width, width)),
            ],
            scratch_shapes=[
                pltpu.VMEM((batch, slots, double), BF16), pltpu.VMEM((width, double), F32),
            ],
        ),
        out_shape=[
            sds((caps, length, width), BF16), sds((caps, slots, width), BF16),
            sds((width, width), BF16), sds((width, width), BF16),
        ],
        compiler_params=pltpu.CompilerParams(vmem_limit_bytes=VMEM_LIMIT),
        name="cross_back",
    )(valid, side, kv, queries, grads, lse, delta, kv_mat, images)


def add_low(first, second):
    return (first.astype(F32) + second.astype(F32)).astype(BF16)


class Piece:
    def __init__(self, sums, source, out, col, width, bits, order, recvs, mine=None, send=None, kv_recv=None):
        self.sums, self.out, self.col, self.width = sums, out, col, width
        self.bits, self.order, self.recvs = list(bits), list(order), recvs
        self.mine, self.send, self.kv_recv = mine, send, kv_recv
        self.now, self.holds, self.pending = 0, source, None

    def columns(self, ref):
        return (slice(None), pl.ds(self.col, self.width) if ref.shape[-1] != self.width else slice(None))

    def start_kv(self):
        whole_lead = (slice(None),) * len(self.bits)
        self.pending = self.sums.copy(
            self.send.at[whole_lead + self.columns(self.send)], self.kv_recv, {"kv": 1 - self.sums.side}
        )
        self.pending.start()

    def start(self):
        bit = self.order[self.now]
        lead = tuple(1 - self.sums.own(bit) if b == bit else slice(None) for b in self.bits)
        self.pending = self.sums.copy(
            self.holds.at[lead + self.columns(self.holds)], self.recvs[self.now], self.sums.partner(bit)
        )
        self.pending.start()

    def add(self, kept, arrived, cols, left, fixed):
        def one(i, carry):
            inner = {b: (i // (1 << (len(left) - 1 - d))) % 2 for d, b in enumerate(left)}
            lead = tuple(inner[b] if b in inner else fixed[b] for b in self.bits)
            into = tuple(inner[b] for b in left)
            arrived[into] = add_low(kept[lead + cols], arrived[into])
            return carry

        lax.fori_loop(0, 1 << len(left), one, 0)

    def advance(self):
        if self.pending is None:
            return True
        self.pending.wait()
        self.pending = None
        if self.holds is None:
            self.add(self.mine, self.kv_recv, self.columns(self.mine), self.bits, {})
            self.holds = self.kv_recv
            self.start()
            return False
        bit = self.order[self.now]
        arrived, cols = self.recvs[self.now], self.columns(self.holds)
        left = [b for b in self.bits if b != bit]
        if not left:
            total = self.holds[(self.sums.own(bit),) + cols].astype(F32) + arrived[...].astype(F32)
            self.out[:, self.col : self.col + self.width] = total
            return True
        self.add(self.holds, arrived, cols, left, {bit: self.sums.own(bit)})
        self.bits, self.holds, self.now = left, arrived, self.now + 1
        self.start()
        return False


class Sums:
    def __init__(self, send_sem, recv_sem):
        self.send_sem, self.recv_sem, self.count = send_sem, recv_sem, 0
        self.me, self.side = lax.axis_index("dp"), lax.axis_index("kv")

    def own(self, bit):
        return (self.me // (1 << bit)) % 2

    def partner(self, bit):
        return {"dp": self.me + (1 - 2 * self.own(bit)) * (1 << bit)}

    def copy(self, src, dst, device):
        index = self.count
        self.count += 1
        return pltpu.make_async_remote_copy(
            src_ref=src, dst_ref=dst, send_sem=self.send_sem.at[index], recv_sem=self.recv_sem.at[index],
            device_id=device, device_id_type=pl.DeviceIdType.MESH,
        )

    def greet(self, bits):
        barrier = pltpu.get_barrier_semaphore()
        for device in [{"kv": 1 - self.side}] + [self.partner(bit) for bit in bits]:
            pl.semaphore_signal(barrier, inc=1, device_id=device, device_id_type=pl.DeviceIdType.MESH)
        pl.semaphore_wait(barrier, 1 + len(bits))


def turned(bits, by):
    first = bits[:-1]
    by %= len(first)
    return first[by:] + first[:by] + bits[-1:]


def end_body(
    back_hbm, hidden_hbm, grad_two_hbm, att_hbm, qkv_hbm, tok_hbm, qkv_mat_hbm, out_mat_hbm, query_mat_hbm,
    gain_one, shift_one, gain_two, shift_two, gain_three, shift_three,
    up_keep, up_first, up_second, up_both, down_keep, down_away, cross_ref, kv_mine, kv_send,
    grad_tok, up_out, down_out, cross_out, qkv_out, out_out, query_out, kv_out, gains_out,
    *scratch, plan, bits, length, tile
):
    scratch = list(scratch)
    (
        send_sem, recv_sem, load_sem, back_one, back_two, hidden, grad_two, att, qkv, tok, qkv_mat,
        out_mat, query_mat, back_sum, normed, low, grad_att, grad_qkv, acc, gains_all, gain_kv,
        gain_buf, gain_recv, qkv_mine, qkv_send, out_mine, out_send, query_mine, query_send,
        up_ref, down_ref,
    ) = scratch[:31]
    rest = scratch[31:]
    sums = Sums(send_sem, recv_sem)
    side = sums.side
    captions = back_one.shape[0]
    rows, width = hidden.shape
    half = width // 2
    named = dict(
        up=(up_ref, None, None, up_out), down=(down_ref, None, None, down_out),
        cross=(cross_ref, None, None, cross_out), qkv=(None, qkv_mine, qkv_send, qkv_out),
        out=(None, out_mine, out_send, out_out), query=(None, query_mine, query_send, query_out),
        kv=(None, kv_mine, kv_send, kv_out),
    )
    pieces = {}
    for name, col, cols, axes, order, kv in plan:
        source, mine, send, out = named[name]
        kv_recv = rest.pop(0) if kv else None
        recvs = [rest.pop(0) for _ in order]
        pieces.setdefault(name, []).append(
            Piece(sums, source, out, col, cols, axes, order, recvs, mine, send, kv_recv)
        )
    early = pieces["up"] + pieces["down"] + pieces["cross"]
    image = pieces["kv"]
    middle = pieces["query"] + pieces["out"]
    late = pieces["qkv"]

    own_caps = pl.ds(pl.multiple_of(side * captions, captions), captions)
    other_caps = pl.ds(pl.multiple_of((1 - side) * captions, captions), captions)
    pairs = [
        (back_hbm.at[own_caps], back_one), (hidden_hbm, hidden), (query_mat_hbm, query_mat),
        (grad_two_hbm, grad_two), (out_mat_hbm, out_mat), (att_hbm, att), (qkv_hbm, qkv),
        (tok_hbm, tok), (qkv_mat_hbm, qkv_mat),
    ]
    loads = [pltpu.make_async_copy(src, dst, load_sem.at[i]) for i, (src, dst) in enumerate(pairs)]
    for load in loads:
        load.start()
    sums.greet(bits)
    swap = sums.copy(back_hbm.at[other_caps], back_two, {"kv": 1 - side})
    swap.start()
    for piece in image:
        piece.start_kv()

    def sum_terms(target, terms):
        count = len(target.shape) - 2

        def one(i, carry):
            lead = tuple((i // (1 << (count - 1 - d))) % 2 for d in range(count))
            total = terms[0][lead].astype(F32)
            for term in terms[1:]:
                total += term[lead].astype(F32)
            target[lead] = total.astype(BF16)
            return carry

        lax.fori_loop(0, 1 << count, one, 0)

    sum_terms(up_ref, (up_keep, up_first, up_second, up_both))
    sum_terms(down_ref, (down_keep, down_away))
    for piece in early:
        piece.start()
    gains_all[...] = jnp.zeros_like(gains_all)
    gains_all[4:5] = gain_three[...]
    gains_all[5:6] = shift_three[...]
    for load in loads[:5]:
        load.wait()
    swap.wait()

    def rows_at(index):
        return pl.ds(pl.multiple_of(index * tile, tile), tile)

    def query_back(index, carry):
        span = rows_at(index)
        caps = pl.ds(index * (tile // length), tile // length)
        back = add_low(back_one[caps], back_two[caps]).reshape(tile, width)
        back_sum[span, :] = back
        unit, inverse = normalize(hidden[span, :])
        normed[span, :] = (unit * as_row(gain_two) + as_row(shift_two)).astype(BF16)
        grad = dot_nt(back, query_mat[...])
        gains_all[2:3] += jnp.sum(grad * unit, axis=0, keepdims=True)
        gains_all[3:4] += jnp.sum(grad, axis=0, keepdims=True)
        grad_one = grad_two[span, :] + norm_back(grad, as_row(gain_two), unit, inverse)
        grad_two[span, :] = grad_one
        low[span, :] = grad_one.astype(BF16)
        grad_att[span, :] = dot_nt(grad_one.astype(BF16), out_mat[...]).astype(BF16)
        return carry

    lax.fori_loop(0, rows // tile, query_back, 0)
    for piece in image:
        piece.advance()

    def weight(left, right, target, which):
        cols = target.shape[-1]
        block = target.shape[-2]
        start = pl.multiple_of(which * cols, 128)
        acc[:, :cols] = dot_tn(left[...], right[:, pl.ds(start, cols)])

        def one(i, carry):
            lead = tuple((i // (1 << (len(bits) - 1 - d))) % 2 for d in range(len(bits)))
            span = pl.ds(i * block, block) if isinstance(i, int) else pl.ds(pl.multiple_of(i * block, 8), block)
            target[lead] = acc[span, :cols].astype(BF16)
            return carry

        if block % 8 == 0:
            lax.fori_loop(0, 1 << len(bits), one, 0)
        else:
            for i in range(1 << len(bits)):
                one(i, 0)

    def weights(left, right, mine, send, group):
        weight(left, right, send, 1 - side)
        for piece in group:
            piece.start_kv()
        weight(left, right, mine, side)

    weights(normed, back_sum, query_mine, query_send, pieces["query"])
    loads[5].wait()
    loads[6].wait()
    weights(att, low, out_mine, out_send, pieces["out"])
    for piece in middle:
        piece.advance()

    mask = same_head()
    causal = causal_mask(length)

    def attend(cap, carry):
        span = pl.ds(pl.multiple_of(cap * length, length), length)
        for group in range(GROUPS):
            lo = group * LANES
            query = spread(qkv[span, lo : lo + LANES] * SCALE, mask)
            key = qkv[span, width + lo : width + lo + LANES]
            value = qkv[span, 2 * width + lo : 2 * width + lo + LANES]
            cot = spread(grad_att[span, lo : lo + LANES], mask)
            scores = jnp.where(causal, dot_nt(key, query), NEG)
            exponent = jnp.exp(scores - jnp.max(scores, axis=0, keepdims=True))
            probs = exponent / jnp.sum(exponent, axis=0, keepdims=True)
            grad_probs = dot_nt(value, cot)
            mean = jnp.sum(probs * grad_probs, axis=0, keepdims=True)
            grad_scores = (probs * (grad_probs - mean)).astype(BF16)
            grad_q = gather_heads(dot_tn(grad_scores, key)) * SCALE
            grad_qkv[span, lo : lo + LANES] = grad_q.astype(BF16)
            grad_qkv[span, width + lo : width + lo + LANES] = dot(grad_scores, query).astype(BF16)
            grad_qkv[span, 2 * width + lo : 2 * width + lo + LANES] = dot(
                probs.astype(BF16), cot
            ).astype(BF16)
        return carry

    lax.fori_loop(0, captions // 2, attend, 0)
    lax.fori_loop(captions // 2, captions, attend, 0)
    for piece in early:
        piece.advance()
    loads[7].wait()
    loads[8].wait()

    def token_norm(index, carry):
        span = rows_at(index)
        unit, _ = normalize(tok[span, :].astype(F32))
        normed[span, :] = (unit * as_row(gain_one) + as_row(shift_one)).astype(BF16)
        return carry

    lax.fori_loop(0, rows // tile, token_norm, 0)
    weights(normed, grad_qkv, qkv_mine, qkv_send, late)
    for piece in late + image:
        piece.advance()

    def token_back(index, carry):
        span = rows_at(index)
        unit, inverse = normalize(tok[span, :].astype(F32))
        grad = dot_nt(grad_qkv[span, :], qkv_mat[...])
        gains_all[0:1] += jnp.sum(grad * unit, axis=0, keepdims=True)
        gains_all[1:2] += jnp.sum(grad, axis=0, keepdims=True)
        back = grad_two[span, :] + norm_back(grad, as_row(gain_one), unit, inverse)
        grad_tok[span, :] = back.astype(BF16)
        return carry

    lax.fori_loop(0, rows // tile, token_back, 0)
    own_cols = pl.ds(pl.multiple_of(side * half, 128), half)
    other_cols = pl.ds(pl.multiple_of((1 - side) * half, 128), half)
    gain_copy = sums.copy(gains_all.at[:, other_cols], gain_kv, {"kv": 1 - side})
    gain_copy.start()
    stage = -1
    everything = early + image + middle + late
    while stage < len(bits) or not all(piece.pending is None for piece in everything):
        if stage < len(bits):
            gain_copy.wait()
            if stage < 0:
                gain_buf[0] = gains_all[:, own_cols] + gain_kv[...]
            else:
                gain_buf[stage + 1] = gain_buf[stage] + gain_recv[stage]
            stage += 1
            if stage < len(bits):
                gain_copy = sums.copy(gain_buf.at[stage], gain_recv.at[stage], sums.partner(bits[stage]))
                gain_copy.start()
            else:
                gains_out[...] = gain_buf[stage]
        for piece in everything:
            piece.advance()


def end(
    back, hidden, grad_two, att, qkv, tokens, qkv_mat, out_mat, query_mat, gain_one, shift_one,
    gain_two, shift_two, gain_three, shift_three, early, kv_mine, kv_send, length, size
):
    bits = list(range(size.bit_length() - 1))
    axes = bits[::-1]
    rows, width = hidden.shape
    captions = rows // length
    tile = min(256, rows)
    block = width // size
    lead = (2,) * len(bits)
    up_terms, down_terms, cross = early
    up, down = up_terms[0], down_terms[0]
    cut_down = down.shape[-1] // 384 * 256
    third = width // 3
    plan = [("up", 0, up.shape[-1], axes[:-2], bits[2:], False)]
    down_axes = axes[:1] + axes[2:]
    for col, cols, by in ((0, cut_down, 0), (cut_down, down.shape[-1] - cut_down, 1)):
        order = [b for b in turned(bits, by) if b in down_axes]
        plan.append(("down", col, cols, down_axes, order, False))
    plan.append(("cross", 0, cross.shape[-1], axes, turned(bits, 2), False))
    plan.append(("query", 0, width // 2, axes, turned(bits, 0), True))
    plan.append(("out", 0, width // 2, axes, turned(bits, 1), True))
    for by in range(3):
        plan.append(("kv", by * third, third, axes, turned(bits, by), True))
        plan.append(("qkv", by * (width // 2), width // 2, axes, turned(bits, by), True))
    heights = dict(up=up.shape[-2], down=down.shape[-2], cross=cross.shape[-2])
    buffers = []
    copies = 2 + len(bits)
    for name, col, cols, piece_axes, order, kv in plan:
        shape = (heights.get(name, block), cols)
        for count in range(len(order) if kv else len(order) - 1, -1, -1):
            buffers.append(pltpu.VMEM((2,) * count + shape, BF16))
            copies += 1
    vmem = pl.BlockSpec(memory_space=pltpu.VMEM)
    hbm = pl.BlockSpec(memory_space=pl.ANY)
    sds = jax.ShapeDtypeStruct
    cut = lambda cols: pltpu.VMEM(lead + (block, cols), BF16)
    outs = [sds((rows, width), BF16)]
    outs += [sds(v.shape[-2:], F32) for v in (up, down, cross)]
    outs += [sds((block, cols), F32) for cols in (3 * width // 2, width // 2, width // 2, width)]
    outs += [sds((8, width // 2), F32)]
    low_rows = lambda cols: pltpu.VMEM((rows, cols), BF16)
    return pl.pallas_call(
        functools.partial(end_body, plan=plan, bits=bits, length=length, tile=tile),
        in_specs=[hbm] * 9 + [vmem] * 6 + [vmem] * 8 + [hbm],
        out_specs=[vmem] * len(outs),
        out_shape=outs,
        scratch_shapes=[
            pltpu.SemaphoreType.DMA((copies,)), pltpu.SemaphoreType.DMA((copies,)),
            pltpu.SemaphoreType.DMA((9,)),
            pltpu.VMEM((captions, length, width), BF16), pltpu.VMEM((captions, length, width), BF16),
            pltpu.VMEM((rows, width), F32), pltpu.VMEM((rows, width), F32), low_rows(width),
            low_rows(3 * width), low_rows(width), pltpu.VMEM(qkv_mat.shape, BF16),
            pltpu.VMEM(out_mat.shape, BF16), pltpu.VMEM(query_mat.shape, BF16),
            low_rows(width), low_rows(width), low_rows(width), low_rows(width), low_rows(3 * width),
            pltpu.VMEM((width, 3 * width // 2), F32), pltpu.VMEM((8, width), F32),
            pltpu.VMEM((8, width // 2), F32), pltpu.VMEM((len(bits) + 1, 8, width // 2), F32),
            pltpu.VMEM((len(bits), 8, width // 2), F32),
            cut(3 * width // 2), cut(3 * width // 2), cut(width // 2), cut(width // 2),
            cut(width // 2), cut(width // 2), pltpu.VMEM(up.shape, BF16), pltpu.VMEM(down.shape, BF16),
        ] + buffers,
        compiler_params=pltpu.CompilerParams(
            vmem_limit_bytes=VMEM_MOST, collective_id=0, has_side_effects=True
        ),
        name="end",
    )(
        back, hidden, grad_two, att, qkv, tokens, qkv_mat, out_mat, query_mat, gain_one, shift_one,
        gain_two, shift_two, gain_three, shift_three, *up_terms, *down_terms, cross, kv_mine, kv_send,
    )


def hand_over_body(*refs):
    count = len(refs) // 2
    for source, target in zip(refs[:count], refs[count:]):
        target[...] = source[...]


def hand_over(*arrays):
    vmem = pl.BlockSpec(memory_space=pltpu.VMEM)
    return pl.pallas_call(
        hand_over_body,
        in_specs=[vmem] * len(arrays),
        out_specs=[vmem] * len(arrays),
        out_shape=[jax.ShapeDtypeStruct(v.shape, v.dtype) for v in arrays],
        name="hand_over",
    )(*arrays)


def exchange(value, axis, bit, size):
    return lax.ppermute(value, axis, [(i, i ^ bit) for i in range(size)])


def split_rows(array, size):
    bits = size.bit_length() - 1
    return array.reshape((2,) * bits + (array.shape[0] // size, array.shape[1]))


def body(
    tokens, images, image_counts, cotangent, norm1_gain, norm1_shift, self_qkv, self_out,
    norm2_gain, norm2_shift, cross_q, cross_kv, cross_out, norm3_gain, norm3_shift, w_up, w_down,
):
    captions, length, width = tokens.shape
    caps, slots, _ = images.shape
    side = lax.axis_index("kv")
    me = lax.axis_index("dp")
    groups = lax.axis_size("dp")
    side_arr = side.reshape(1)
    tok = tokens.reshape(captions * length, width)
    cot = cotangent.reshape(captions * length, width)
    short = -(-SHORT // 16) * 16
    valid = jnp.clip(image_counts - side * slots, 0, slots)
    swap = lambda v: exchange(v, "kv", 1, 2)

    qkv, att, hidden, query = token_start(
        tok, norm1_gain, norm1_shift, self_qkv, self_out, norm2_gain,
        norm2_shift, cross_q, length,
    )

    def both(own):
        other = swap(own)
        first = jnp.where(side == 0, own, other)
        second = jnp.where(side == 0, other, own)
        return jnp.concatenate([first, second], axis=0)

    queries = both(query.reshape(captions, length, width))
    kv, part, lse_part = cross_start(valid, images, cross_kv, queries, short)
    (
        layer_out, grad_two, grads, lse, delta, up_keep, up_first, up_second, up_both, down_keep,
        down_away, cross_sum, gain3, shift3,
    ) = feed(
        part, lse_part, hidden, cot, cross_out, norm3_gain, norm3_shift, w_up, w_down, length, groups
    )
    bits = groups.bit_length() - 1
    cubes = lambda v, count: v.reshape((2,) * count + (v.shape[0] * v.shape[1] >> count, v.shape[2]))
    up_terms = [up_keep] + [
        exchange(away, "dp", flip, groups) for away, flip in ((up_first, 1), (up_second, 2), (up_both, 3))
    ]
    down_terms = [down_keep, exchange(down_away, "dp", 1 << (bits - 2), groups)]
    early = (
        [cubes(v, bits - 2) for v in up_terms], [cubes(v, bits - 1) for v in down_terms],
        cubes(cross_sum, bits),
    )

    stats = lambda v: v.reshape(caps, GROUPS, LANES)
    back, images_grad, kv_mine, kv_send = cross_back(
        valid, side_arr, kv, queries, grads.reshape(caps, length, width), stats(lse), stats(delta),
        cross_kv, images, short
    )
    cut = lambda v: split_rows(v, groups)
    (
        tokens_grad, w_up_grad, down_grad, cross_out_grad, self_qkv_grad, self_out_grad, cross_q_grad,
        cross_kv_grad, gains, layer_out,
    ) = hand_over(*end(
        back, hidden, grad_two, att, qkv, tok, self_qkv, self_out, cross_q, norm1_gain, norm1_shift,
        norm2_gain, norm2_shift, gain3, shift3, early, cut(kv_mine), cut(kv_send), length, groups,
    ), layer_out)
    return (
        layer_out.reshape(captions, length, width),
        tokens_grad.reshape(captions, length, width),
        images_grad,
        gains[0], gains[1], self_qkv_grad, self_out_grad, gains[2], gains[3], cross_q_grad,
        cross_kv_grad, cross_out_grad, gains[4], gains[5], w_up_grad, down_grad,
    )


def solution(mesh):
    return jax.shard_map(
        body,
        mesh=mesh,
        in_specs=(
            P(("dp", "kv"), None, None), P("dp", "kv", None), P("dp"), P(("dp", "kv"), None, None),
        ) + (P(),) * 13,
        out_specs=(
            P(("dp", "kv"), None, None), P(("dp", "kv"), None, None), P("dp", "kv", None),
            P("kv"), P("kv"), P("dp", "kv"), P("dp", "kv"), P("kv"), P("kv"), P("dp", "kv"),
            P("dp", "kv"), P("dp", "kv"), P("kv"), P("kv"), P("dp", "kv"), P("dp", "kv"),
        ),
        check_vma=False,
    )
```

```python
import functools

import jax
import jax.numpy as jnp
from jax import lax
from jax.experimental import pallas as pl
from jax.experimental.pallas import tpu as pltpu
from jax.sharding import PartitionSpec as P

HEADS = 12
HEAD_DIM = 64
SHORT = 196
LANES = 256
PACK = LANES // HEAD_DIM
GROUPS = HEADS // PACK
SCALE = HEAD_DIM ** (-0.5)
NEG = -1e30
F32 = jnp.float32
BF16 = jnp.bfloat16
VMEM_LIMIT = 60 * 1024 * 1024
VMEM_MOST = 67043328


def dot(a, b):
    return jnp.dot(a, b, preferred_element_type=F32)


def dot_nt(a, b):
    return lax.dot_general(a, b, (((1,), (1,)), ((), ())), preferred_element_type=F32)


def dot_tn(a, b):
    return lax.dot_general(a, b, (((0,), (0,)), ((), ())), preferred_element_type=F32)


def normalize(values):
    centered = values - jnp.mean(values, axis=-1, keepdims=True)
    inverse = lax.rsqrt(jnp.mean(centered * centered, axis=-1, keepdims=True) + 1e-05)
    return centered * inverse, inverse


def norm_back(grad, gain, unit, inverse):
    scaled = grad * gain
    mean_one = jnp.mean(scaled, axis=-1, keepdims=True)
    mean_two = jnp.mean(scaled * unit, axis=-1, keepdims=True)
    return (scaled - mean_one - unit * mean_two) * inverse


def as_row(ref):
    return ref[...].reshape(1, ref.shape[0])


def iota(shape, dim):
    return lax.broadcasted_iota(jnp.int32, shape, dim)


def same_head():
    shape = (LANES, LANES)
    return (iota(shape, 0) // HEAD_DIM) == (iota(shape, 1) // HEAD_DIM)


def spread(rows, mask):
    stacked = jnp.concatenate([rows] * PACK, axis=0)
    return jnp.where(mask, stacked, jnp.zeros_like(stacked))


def gather_heads(full):
    count = full.shape[0] // PACK
    head = iota((count, LANES), 1) // HEAD_DIM
    out = full[:count]
    for index in range(1, PACK):
        out = jnp.where(head == index, full[index * count : (index + 1) * count], out)
    return out


def split_two(value):
    high = value.astype(BF16)
    return high, (value - high.astype(F32)).astype(BF16)


def lanes_to_rows(row, mask_low):
    shape = (HEAD_DIM, LANES)
    pick = iota(shape, 0) == (iota(shape, 1) % HEAD_DIM)
    high, low = split_two(jnp.where(pick, row, 0.0))
    return dot(high, mask_low) + dot(low, mask_low)


def rows_to_lanes(rows, mask_low):
    high, low = split_two(rows)
    summed = dot(high, mask_low) + dot(low, mask_low)
    shape = (HEAD_DIM, LANES)
    pick = iota(shape, 0) == (iota(shape, 1) % HEAD_DIM)
    return jnp.sum(jnp.where(pick, summed, 0.0), axis=0, keepdims=True)


def lane_slice(group):
    return slice(group * LANES, (group + 1) * LANES)


def causal_mask(length):
    shape = (length, LANES)
    return iota(shape, 0) <= (iota(shape, 1) % HEAD_DIM)


def token_start_body(
    tok_ref, gain_one, shift_one, qkv_mat, out_mat, gain_two, shift_two, query_mat,
    qkv_ref, att_ref, hidden_ref, query_ref, *, length
):
    x = tok_ref[...].astype(F32)
    unit, _ = normalize(x)
    normed = (unit * as_row(gain_one) + as_row(shift_one)).astype(BF16)
    width = x.shape[1]
    qkv_ref[...] = dot(normed, qkv_mat[...]).astype(BF16)
    mask = same_head()
    causal = causal_mask(length)
    for cap in range(x.shape[0] // length):
        rows = slice(cap * length, (cap + 1) * length)
        for group in range(GROUPS):
            lo = group * LANES
            query = qkv_ref[rows, lo : lo + LANES] * SCALE
            key = qkv_ref[rows, width + lo : width + lo + LANES]
            value = qkv_ref[rows, 2 * width + lo : 2 * width + lo + LANES]
            scores = jnp.where(causal, dot_nt(key, spread(query, mask)), NEG)
            exponent = jnp.exp(scores - jnp.max(scores, axis=0, keepdims=True))
            probs = exponent / jnp.sum(exponent, axis=0, keepdims=True)
            full = dot_tn(probs.astype(BF16), value)
            att_ref[rows, lo : lo + LANES] = gather_heads(full).astype(BF16)
    hidden = x + dot(att_ref[...], out_mat[...])
    hidden_ref[...] = hidden
    unit, _ = normalize(hidden)
    normed = (unit * as_row(gain_two) + as_row(shift_two)).astype(BF16)
    query_ref[...] = (dot(normed, query_mat[...]).astype(BF16).astype(F32) * SCALE).astype(BF16)


def whole(shape):
    zeros = (0,) * len(shape)
    return pl.BlockSpec(shape, lambda *_: zeros)


def token_start(tokens, gain_one, shift_one, qkv_mat, out_mat, gain_two, shift_two, query_mat, length):
    rows, width = tokens.shape
    tile = min(256, rows)
    row_block = lambda cols: pl.BlockSpec((tile, cols), lambda i: (i, 0))
    return pl.pallas_call(
        functools.partial(token_start_body, length=length),
        grid=(rows // tile,),
        in_specs=[
            row_block(width), whole((width,)), whole((width,)), whole(qkv_mat.shape),
            whole(out_mat.shape), whole((width,)), whole((width,)), whole(query_mat.shape),
        ],
        out_specs=[row_block(3 * width), row_block(width), row_block(width), row_block(width)],
        out_shape=[
            jax.ShapeDtypeStruct((rows, 3 * width), BF16),
            jax.ShapeDtypeStruct((rows, width), BF16),
            jax.ShapeDtypeStruct((rows, width), F32),
            jax.ShapeDtypeStruct((rows, width), BF16),
        ],
        compiler_params=pltpu.CompilerParams(vmem_limit_bytes=VMEM_LIMIT),
        name="token_start",
    )(tokens, gain_one, shift_one, qkv_mat, out_mat, gain_two, shift_two, query_mat)


def cross_start_body(valid_ref, img_ref, kv_mat, query_ref, kv_ref, att_ref, lse_ref, *, short):
    cap = pl.program_id(0)
    valid = valid_ref[cap]
    width = query_ref.shape[2]
    slots = img_ref.shape[1]

    def work(count):
        kv_ref[0, :count] = dot(img_ref[0, :count], kv_mat[...]).astype(BF16)
        mask = same_head()
        inside = iota((count, LANES), 0) < valid
        for group in range(GROUPS):
            lo = group * LANES
            key = kv_ref[0, :count, lo : lo + LANES]
            value = kv_ref[0, :count, width + lo : width + lo + LANES]
            scores = dot_nt(key, spread(query_ref[0, :, lo : lo + LANES], mask))
            scores = jnp.where(inside, scores, NEG)
            peak = jnp.max(scores, axis=0, keepdims=True)
            exponent = jnp.where(inside, jnp.exp(scores - peak), 0.0)
            total = jnp.sum(exponent, axis=0, keepdims=True)
            probs = (exponent * (1.0 / total)).astype(BF16)
            att_ref[0, :, lo : lo + LANES] = gather_heads(dot_tn(probs, value)).astype(BF16)
            lse_ref[0, group : group + 1] = peak + jnp.log(total)

    @pl.when(valid <= 0)
    def _():
        att_ref[...] = jnp.zeros_like(att_ref)
        lse_ref[...] = jnp.full_like(lse_ref, NEG)

    if short < slots:
        pl.when((valid > 0) & (valid <= short))(lambda: work(short))
        pl.when(valid > short)(lambda: work(slots))
    else:
        pl.when(valid > 0)(lambda: work(slots))


def cross_start(valid, images, kv_mat, queries, short):
    caps, slots, width = images.shape
    length = queries.shape[1]
    block = lambda *shape: pl.BlockSpec((1,) + shape, lambda i, *_: (i, 0, 0))
    return pl.pallas_call(
        functools.partial(cross_start_body, short=short),
        grid_spec=pltpu.PrefetchScalarGridSpec(
            num_scalar_prefetch=1,
            grid=(caps,),
            in_specs=[block(slots, width), whole(kv_mat.shape), block(length, width)],
            out_specs=[block(slots, 2 * width), block(length, width), block(GROUPS, LANES)],
        ),
        out_shape=[
            jax.ShapeDtypeStruct((caps, slots, 2 * width), BF16),
            jax.ShapeDtypeStruct((caps, length, width), BF16),
            jax.ShapeDtypeStruct((caps, GROUPS, LANES), F32),
        ],
        compiler_params=pltpu.CompilerParams(vmem_limit_bytes=VMEM_LIMIT),
        name="cross_start",
    )(valid, images, kv_mat, queries)


def cut_rows(target, value):
    count, height, _ = target.shape
    if height % 16 == 0:
        target[...] = value.astype(BF16).reshape(target.shape)
    else:
        for index in range(count):
            target[index] = value[index * height : (index + 1) * height].astype(BF16)


def feed_body(
    part_hbm, lse_hbm, hidden_ref, cot_ref, cross_mat, gain_ref, shift_ref, up_one, up_two, down_ref,
    out_ref, grad_two_ref, grads_hbm, lse_out, delta_out, up_sum, down_sum, cross_sum, gain_grad, shift_grad,
    send_sem, recv_sem, load_sem, att_one, att_two, lse_one, lse_two, att_full, att_low, hidden_two,
    normed_ref, acc_out, acc_grad, grad_att, lse_own, delta_own, up_pair, up_got, down_pair, down_got,
    cross_pair, cross_got, *, length, tile, steps
):
    step = pl.program_id(0)
    side = lax.axis_index("kv")
    rows, width = hidden_ref.shape
    captions = rows // length
    tiles = rows // tile
    half = width // 2
    sub = up_one.shape[1]
    blocks = up_pair.shape[2]

    def remote(src, dst, index):
        return pltpu.make_async_remote_copy(
            src_ref=src, dst_ref=dst, send_sem=send_sem.at[index], recv_sem=recv_sem.at[index],
            device_id={"kv": 1 - side}, device_id_type=pl.DeviceIdType.MESH,
        )

    def row_span(index):
        return pl.ds(pl.multiple_of(index * tile, tile), tile)

    def chunk_copies(slot):
        return (
            remote(up_pair.at[slot, 1 - side], up_got.at[slot], 2 + slot),
            remote(down_pair.at[slot, 1 - side], down_got.at[slot], 4 + slot),
        )

    cross_copy = lambda: remote(cross_pair.at[1 - side], cross_got, 6)
    lse_copy = lambda: remote(lse_own, lse_out.at[side], 7)
    delta_copy = lambda: remote(delta_own, delta_out.at[side], 8)
    grad_copy = lambda index: remote(
        grad_att.at[pl.ds(index * tile, tile)], grads_hbm.at[side, pl.ds(index * tile, tile)], 9 + index
    )
    lse_store = lambda: pltpu.make_async_copy(lse_own, lse_out.at[side], load_sem.at[2])

    @pl.when(step == 0)
    def _():
        part_load = pltpu.make_async_copy(part_hbm.at[side], att_one, load_sem.at[0])
        lse_load = pltpu.make_async_copy(lse_hbm.at[side], lse_one, load_sem.at[1])
        part_load.start()
        lse_load.start()
        barrier = pltpu.get_barrier_semaphore()
        pl.semaphore_signal(barrier, inc=1, device_id={"kv": 1 - side}, device_id_type=pl.DeviceIdType.MESH)
        pl.semaphore_wait(barrier, 1)
        part_swap = remote(part_hbm.at[1 - side], att_two, 0)
        lse_swap = remote(lse_hbm.at[1 - side], lse_two, 1)
        lse_swap.start()
        part_swap.start()
        mask_low = same_head().astype(BF16)
        lse_load.wait()
        part_load.wait()
        lse_swap.wait()
        part_swap.wait()

        def one_caption(cap, carry):
            span = pl.ds(pl.multiple_of(cap * length, length), length)
            for group in range(GROUPS):
                lo = group * LANES
                first = lse_one[cap, group : group + 1]
                second = lse_two[cap, group : group + 1]
                peak = jnp.maximum(first, second)
                lse = peak + jnp.log(jnp.exp(first - peak) + jnp.exp(second - peak))
                lse_own[cap, group : group + 1] = lse
                weight_one = lanes_to_rows(jnp.exp(first - lse), mask_low)
                weight_two = lanes_to_rows(jnp.exp(second - lse), mask_low)
                mixed = (
                    weight_one * att_one[span, lo : lo + LANES].astype(F32)
                    + weight_two * att_two[span, lo : lo + LANES].astype(F32)
                )
                att_full[span, lo : lo + LANES] = mixed
                att_low[span, lo : lo + LANES] = mixed.astype(BF16)
            return carry

        lax.fori_loop(0, captions, one_caption, 0)
        lse_copy().start()
        lse_store().start()

        def one_tile(index, carry):
            span = row_span(index)
            two = hidden_ref[span, :] + dot(att_low[span, :], cross_mat[...])
            hidden_two[span, :] = two
            unit, _ = normalize(two)
            normed_ref[span, :] = (unit * as_row(gain_ref) + as_row(shift_ref)).astype(BF16)
            acc_out[span, :] = two
            acc_grad[span, :] = jnp.zeros_like(two)
            return carry

        lax.fori_loop(0, tiles, one_tile, 0)

    slot = step % 2
    up_mat = jnp.concatenate([up_one[...], up_two[...]], axis=1)
    down_mat = down_ref[...].reshape(2 * sub, width)
    pre = dot(normed_ref[...], up_mat)
    cdf = 0.5 * (1.0 + lax.erf(pre * 0.7071067811865476))
    act = (pre * cdf).astype(BF16)
    acc_out[...] += dot(act, down_mat)
    cot = cot_ref[...]
    density = jnp.exp(-0.5 * pre * pre) * 0.3989422804014327
    grad_up = (dot_nt(cot, down_mat) * (cdf + pre * density)).astype(BF16)
    acc_grad[...] += dot_nt(grad_up, up_mat)
    grad_down = dot_tn(act, cot).astype(BF16)
    grad_w = dot_tn(normed_ref[...], grad_up)
    for part in range(2):
        cut_rows(up_pair.at[slot, part], grad_w[:, part * sub : (part + 1) * sub])
        down_pair[slot, part] = grad_down[:, part * half : (part + 1) * half].reshape(2, sub, half)

    def take(chunk, place):
        for copy in chunk_copies(place):
            copy.wait()
        span = pl.ds(pl.multiple_of(chunk * sub, sub), sub)
        up_sum[:, :, span] = add_low(up_pair[place, side], up_got[place])
        down_sum[:, span, :] = add_low(down_pair[place, side], down_got[place])

    @pl.when(step > 0)
    def _():
        take(step - 1, (step + 1) % 2)

    for copy in chunk_copies(slot):
        copy.start()

    @pl.when(step == steps - 1)
    def _():
        mask_low = same_head().astype(BF16)
        gain_grad[...] = jnp.zeros_like(gain_grad)
        shift_grad[...] = jnp.zeros_like(shift_grad)
        for index in range(tiles):
            span = pl.ds(index * tile, tile)
            unit, inverse = normalize(hidden_two[span, :])
            grad = acc_grad[span, :]
            gain_grad[...] += jnp.sum(grad * unit, axis=0, keepdims=True)
            shift_grad[...] += jnp.sum(grad, axis=0, keepdims=True)
            two = cot_ref[span, :].astype(F32) + norm_back(grad, as_row(gain_ref), unit, inverse)
            grad_two_ref[span, :] = two
            low = two.astype(BF16)
            normed_ref[span, :] = low
            grad_att[span, :] = dot_nt(low, cross_mat[...]).astype(BF16)
            grad_copy(index).start()
        grad_store = pltpu.make_async_copy(grad_att, grads_hbm.at[side], load_sem.at[0])
        grad_store.start()

        def one_caption(cap, carry):
            span = pl.ds(pl.multiple_of(cap * length, length), length)
            for group in range(GROUPS):
                lo = group * LANES
                product = grad_att[span, lo : lo + LANES].astype(F32) * att_full[span, lo : lo + LANES]
                delta_own[cap, group : group + 1] = rows_to_lanes(product, mask_low)
            return carry

        lax.fori_loop(0, captions, one_caption, 0)
        delta_copy().start()
        delta_store = pltpu.make_async_copy(delta_own, delta_out.at[side], load_sem.at[1])
        delta_store.start()
        grad_cross = dot_tn(att_low[...], normed_ref[...])
        for part in range(2):
            cut_rows(cross_pair.at[part], grad_cross[:, part * half : (part + 1) * half])
        cross_copy().start()
        out_ref[...] = acc_out[...].astype(BF16)
        take(steps - 1, (steps - 1) % 2)
        cross_copy().wait()

        def one(block, carry):
            cross_sum[block] = add_low(cross_pair[side, block], cross_got[block])
            return carry

        lax.fori_loop(0, blocks, one, 0)
        for copy in [lse_copy(), lse_store(), delta_copy(), delta_store, grad_store]:
            copy.wait()
        for index in range(tiles):
            grad_copy(index).wait()


def feed(part, lse_part, hidden, cot, cross_mat, gain, shift, up_mat, down_mat, length, size):
    rows, width = hidden.shape
    captions = rows // length
    units = up_mat.shape[1]
    sub = 256
    steps = units // 2 // sub
    tile = min(256, rows)
    half = width // 2
    block = width // size
    stat = (captions, GROUPS, LANES)
    sds = jax.ShapeDtypeStruct
    once = lambda shape: pl.BlockSpec(shape, lambda *_: (0,) * len(shape), pipeline_mode=pl.Buffered(1))
    hbm = pl.BlockSpec(memory_space=pl.ANY)
    copies = 9 + rows // tile
    f32_rows = lambda: pltpu.VMEM((rows, width), F32)
    low_rows = lambda: pltpu.VMEM((rows, width), BF16)
    up_shape, down_shape = (size, block, units // 2), (2, units // 2, half)
    return pl.pallas_call(
        functools.partial(feed_body, length=length, tile=tile, steps=steps),
        grid=(steps,),
        in_specs=[
            hbm, hbm, once((rows, width)), once((rows, width)), once((width, width)),
            once((width,)), once((width,)),
            pl.BlockSpec((width, sub), lambda i: (0, i)),
            pl.BlockSpec((width, sub), lambda i: (0, i + steps)),
            pl.BlockSpec((2, sub, width), lambda i: (0, i, 0)),
        ],
        out_specs=[
            whole((rows, width)), whole((rows, width)), hbm, hbm, hbm,
            whole(up_shape), whole(down_shape), whole((size, block, half)), whole((1, width)), whole((1, width)),
        ],
        out_shape=[
            sds((rows, width), BF16), sds((rows, width), F32), sds((2, rows, width), BF16),
            sds((2,) + stat, F32), sds((2,) + stat, F32),
            sds(up_shape, BF16), sds(down_shape, BF16), sds((size, block, half), BF16), sds((1, width), F32), sds((1, width), F32),
        ],
        scratch_shapes=[
            pltpu.SemaphoreType.DMA((copies,)), pltpu.SemaphoreType.DMA((copies,)),
            pltpu.SemaphoreType.DMA((3,)),
            low_rows(), low_rows(), pltpu.VMEM(stat, F32), pltpu.VMEM(stat, F32), f32_rows(), low_rows(),
            f32_rows(), low_rows(), f32_rows(), f32_rows(), low_rows(),
            pltpu.VMEM(stat, F32), pltpu.VMEM(stat, F32),
            pltpu.VMEM((2, 2, size, block, sub), BF16), pltpu.VMEM((2, size, block, sub), BF16),
            pltpu.VMEM((2, 2, 2, sub, half), BF16), pltpu.VMEM((2, 2, sub, half), BF16),
            pltpu.VMEM((2, size, block, half), BF16), pltpu.VMEM((size, block, half), BF16),
        ],
        compiler_params=pltpu.CompilerParams(
            vmem_limit_bytes=VMEM_MOST, collective_id=1, has_side_effects=True
        ),
        name="feed",
    )(
        part.reshape(2, rows, width), lse_part.reshape((2,) + stat), hidden, cot, cross_mat, gain, shift,
        up_mat, up_mat, down_mat.reshape(2, units // 2, width),
    )


def cross_back_body(
    valid_ref, kv_ref, query_ref, grad_ref, lse_ref, delta_ref, kv_mat, img_ref, up_ref, down_ref, cross_ref,
    back_ref, grad_img_ref, mine_ref, send_ref, up_out, down_out, cross_out,
    send_sem, recv_sem, back_send_sem, back_recv_sem, grad_kv_ref, acc_ref, back_away, back_got,
    *buffers, plan, bits
):
    cap = pl.program_id(0)
    caps = valid_ref.shape[0]
    captions, length, width = back_ref.shape
    valid = valid_ref[cap]
    slots = kv_ref.shape[1]
    batch = img_ref.shape[0]
    place = cap % batch
    buffers = list(buffers)
    sums = Sums(send_sem, recv_sem)
    side = sums.side
    named = dict(up=(up_ref, up_out), down=(down_ref, down_out), cross=(cross_ref, cross_out))
    pieces = []
    for name, col, cols, axes, order, _ in plan:
        source, out = named[name]
        recvs = [buffers.pop(0) for _ in order]
        pieces.append(Piece(sums, source, out, col, cols, axes, order, recvs))

    def back_copy(index):
        return pltpu.make_async_remote_copy(
            src_ref=back_away.at[index], dst_ref=back_got.at[index], send_sem=back_send_sem.at[index],
            recv_sem=back_recv_sem.at[index], device_id={"kv": 1 - side},
            device_id_type=pl.DeviceIdType.MESH,
        )

    @pl.when(cap == 0)
    def _():
        sums.greet(bits)
        for piece in pieces:
            piece.start()
        acc_ref[...] = jnp.zeros_like(acc_ref)

    for stage in range(len(bits) - 1):

        @pl.when(cap == caps - 1 - (caps >> (stage + 1)))
        def _():
            for piece in pieces:
                piece.advance()

    mask = same_head()
    inside = iota((slots, LANES), 0) < valid
    away = cap // captions != side
    index = cap % captions
    for group in range(GROUPS):
        lo = group * LANES
        key = kv_ref[0, :, lo : lo + LANES]
        value = kv_ref[0, :, width + lo : width + lo + LANES]
        query = spread(query_ref[0, :, lo : lo + LANES], mask)
        grad = spread(grad_ref[0, :, lo : lo + LANES], mask)
        scores = dot_nt(key, query)
        probs = jnp.where(inside, jnp.exp(scores - lse_ref[0, group : group + 1]), 0.0)
        grad_probs = dot_nt(value, grad)
        grad_scores = (probs * (grad_probs - delta_ref[0, group : group + 1])).astype(BF16)
        back = (gather_heads(dot_tn(grad_scores, key)) * SCALE).astype(BF16)

        @pl.when(away)
        def _():
            back_away[index, :, lo : lo + LANES] = back

        @pl.when(jnp.logical_not(away))
        def _():
            back_ref[index, :, lo : lo + LANES] = back

        grad_kv_ref[place, :, lo : lo + LANES] = dot(grad_scores, query).astype(BF16)
        grad_kv_ref[place, :, width + lo : width + lo + LANES] = dot(probs.astype(BF16), grad).astype(BF16)

    @pl.when(away)
    def _():
        back_copy(index).start()

    grad_img_ref[0] = dot_nt(grad_kv_ref[place], kv_mat[...]).astype(BF16)

    @pl.when(place == batch - 1)
    def _():
        left = img_ref[...].reshape(batch * slots, width)
        right = grad_kv_ref[...].reshape(batch * slots, 2 * width)
        acc_ref[...] += dot_tn(left, right)

    @pl.when(cap == caps - 1)
    def _():
        own = pl.ds(pl.multiple_of(side * width, width), width)
        other = pl.ds(pl.multiple_of((1 - side) * width, width), width)
        mine_ref[...] = acc_ref[:, own].astype(BF16)
        send_ref[...] = acc_ref[:, other].astype(BF16)

        def one(i, carry):
            back_copy(i).wait()
            back_ref[i] = add_low(back_ref[i], back_got[i])
            return carry

        lax.fori_loop(0, captions, one, 0)
        for piece in pieces:
            piece.advance()


def cross_back(valid, kv, queries, grads, lse, delta, kv_mat, images, early, size):
    caps, slots, double = kv.shape
    width = double // 2
    length = queries.shape[1]
    captions = caps // 2
    batch = 4 if caps % 4 == 0 else 1
    bits = list(range(size.bit_length() - 1))
    axes = bits[::-1]
    up, down, cross = early
    plan = []
    for by in range(3):
        for name, array in (("up", up), ("down", down)):
            third = array.shape[-1] // 3
            plan.append((name, by * third, third, axes, turned(bits, by), False))
    plan.append(("cross", 0, cross.shape[-1], axes, turned(bits, 1), False))
    heights = dict(up=up.shape[-2], down=down.shape[-2], cross=cross.shape[-2])
    buffers = [
        pltpu.VMEM((2,) * count + (heights[name], cols), BF16)
        for name, _, cols, _, order, _ in plan
        for count in range(len(order) - 1, -1, -1)
    ]
    block = lambda *shape: pl.BlockSpec((1,) + shape, lambda i, *_: (i, 0, 0))
    once = lambda shape: pl.BlockSpec(shape, lambda *_: (0,) * len(shape), pipeline_mode=pl.Buffered(1))
    sds = jax.ShapeDtypeStruct
    sems = pltpu.SemaphoreType.DMA((len(buffers),))
    back_sems = pltpu.SemaphoreType.DMA((captions,))
    swapped = pltpu.VMEM((captions, length, width), BF16)
    outs = [sds(v.shape[-2:], F32) for v in early]
    return pl.pallas_call(
        functools.partial(cross_back_body, plan=plan, bits=bits),
        grid_spec=pltpu.PrefetchScalarGridSpec(
            num_scalar_prefetch=1,
            grid=(caps,),
            in_specs=[
                block(slots, double), block(length, width), block(length, width),
                block(GROUPS, LANES), block(GROUPS, LANES), once(kv_mat.shape),
                pl.BlockSpec((batch, slots, width), lambda i, *_: (i // batch, 0, 0)),
                once(up.shape), once(down.shape), once(cross.shape),
            ],
            out_specs=[
                whole((captions, length, width)), block(slots, width), whole((width, width)),
                whole((width, width)),
            ] + [whole(v.shape) for v in outs],
            scratch_shapes=[
                sems, sems, back_sems, back_sems,
                pltpu.VMEM((batch, slots, double), BF16), pltpu.VMEM((width, double), F32), swapped, swapped,
            ] + buffers,
        ),
        out_shape=[
            sds((captions, length, width), BF16), sds((caps, slots, width), BF16),
            sds((width, width), BF16), sds((width, width), BF16),
        ] + outs,
        compiler_params=pltpu.CompilerParams(
            vmem_limit_bytes=VMEM_MOST, collective_id=2, has_side_effects=True
        ),
        name="cross_back",
    )(valid, kv, queries, grads, lse, delta, kv_mat, images, up, down, cross)


def add_low(first, second):
    return (first.astype(F32) + second.astype(F32)).astype(BF16)


def cut_blocks(target, value):
    height = target.shape[-2]
    count = len(target.shape) - 2
    if height % 16 == 0:
        target[...] = value.astype(BF16).reshape(target.shape)
    else:
        for i in range(1 << count):
            lead = tuple((i >> (count - 1 - d)) % 2 for d in range(count))
            target[lead] = value[i * height : (i + 1) * height].astype(BF16)


class Piece:
    def __init__(self, sums, source, out, col, width, bits, order, recvs, mine=None, send=None, kv_recv=None):
        self.sums, self.out, self.col, self.width = sums, out, col, width
        self.bits, self.order, self.recvs = list(bits), list(order), recvs
        self.mine, self.send, self.kv_recv = mine, send, kv_recv
        self.now, self.holds, self.pending = 0, source, None

    def columns(self, ref):
        return (slice(None), pl.ds(self.col, self.width) if ref.shape[-1] != self.width else slice(None))

    def start_kv(self):
        whole_lead = (slice(None),) * len(self.bits)
        index = self.sums.take_index()
        self.pending = lambda: self.sums.copy(
            index, self.send.at[whole_lead + self.columns(self.send)], self.kv_recv,
            {"kv": 1 - self.sums.side},
        )
        self.pending().start()

    def start(self):
        bit, bits, holds, arrives = self.order[self.now], self.bits, self.holds, self.recvs[self.now]
        index = self.sums.take_index()

        def make():
            lead = tuple(1 - self.sums.own(bit) if b == bit else slice(None) for b in bits)
            return self.sums.copy(index, holds.at[lead + self.columns(holds)], arrives, self.sums.partner(bit))

        self.pending = make
        make().start()

    def add(self, kept, arrived, cols, left, fixed):
        def one(i, carry):
            inner = {b: (i // (1 << (len(left) - 1 - d))) % 2 for d, b in enumerate(left)}
            lead = tuple(inner[b] if b in inner else fixed[b] for b in self.bits)
            into = tuple(inner[b] for b in left)
            arrived[into] = add_low(kept[lead + cols], arrived[into])
            return carry

        lax.fori_loop(0, 1 << len(left), one, 0)

    def advance(self):
        if self.pending is None:
            return True
        self.pending().wait()
        self.pending = None
        if self.holds is None:
            self.add(self.mine, self.kv_recv, self.columns(self.mine), self.bits, {})
            self.holds = self.kv_recv
            self.start()
            return False
        bit = self.order[self.now]
        arrived, cols = self.recvs[self.now], self.columns(self.holds)
        left = [b for b in self.bits if b != bit]
        if not left:
            total = self.holds[(self.sums.own(bit),) + cols].astype(F32) + arrived[...].astype(F32)
            self.out[:, self.col : self.col + self.width] = total
            return True
        self.add(self.holds, arrived, cols, left, {bit: self.sums.own(bit)})
        self.bits, self.holds, self.now = left, arrived, self.now + 1
        self.start()
        return False


class Sums:
    def __init__(self, send_sem, recv_sem):
        self.send_sem, self.recv_sem, self.count = send_sem, recv_sem, 0
        self.me, self.side = lax.axis_index("dp"), lax.axis_index("kv")

    def own(self, bit):
        return (self.me // (1 << bit)) % 2

    def partner(self, bit):
        return {"dp": self.me + (1 - 2 * self.own(bit)) * (1 << bit)}

    def take_index(self):
        self.count += 1
        return self.count - 1

    def copy(self, index, src, dst, device):
        return pltpu.make_async_remote_copy(
            src_ref=src, dst_ref=dst, send_sem=self.send_sem.at[index], recv_sem=self.recv_sem.at[index],
            device_id=device, device_id_type=pl.DeviceIdType.MESH,
        )

    def greet(self, bits):
        barrier = pltpu.get_barrier_semaphore()
        for device in [{"kv": 1 - self.side}] + [self.partner(bit) for bit in bits]:
            pl.semaphore_signal(barrier, inc=1, device_id=device, device_id_type=pl.DeviceIdType.MESH)
        pl.semaphore_wait(barrier, 1 + len(bits))


def turned(bits, by):
    first = bits[:-1]
    by %= len(first)
    return first[by:] + first[:by] + bits[-1:]


def end_body(
    back_hbm, hidden_hbm, grad_two_hbm, att_hbm, qkv_hbm, tok_hbm, qkv_mat_hbm, out_mat_hbm, query_mat_hbm,
    gain_one, shift_one, gain_two, shift_two, gain_three, shift_three,
    kv_mine, kv_send, grad_tok, qkv_out, out_out, query_out, kv_out, gains_out,
    *scratch, plan, bits, length, tile
):
    scratch = list(scratch)
    (
        send_sem, recv_sem, load_sem, back_sum, hidden, grad_two, att, qkv, tok, qkv_mat,
        out_mat, query_mat, normed, low, grad_att, grad_qkv, gains_all, gain_kv,
        gain_buf, gain_recv, qkv_mine, qkv_send, out_mine, out_send, query_mine, query_send,
    ) = scratch[:26]
    rest = scratch[26:]
    sums = Sums(send_sem, recv_sem)
    side = sums.side
    rows, width = hidden.shape
    captions = rows // length
    half = width // 2
    named = dict(
        qkv=(None, qkv_mine, qkv_send, qkv_out),
        out=(None, out_mine, out_send, out_out), query=(None, query_mine, query_send, query_out),
        kv=(None, kv_mine, kv_send, kv_out),
    )
    pieces = {}
    for name, col, cols, axes, order, kv in plan:
        source, mine, send, out = named[name]
        kv_recv = rest.pop(0)
        recvs = [rest.pop(0) for _ in order]
        pieces.setdefault(name, []).append(
            Piece(sums, source, out, col, cols, axes, order, recvs, mine, send, kv_recv)
        )
    image = pieces["kv"]
    middle = pieces["query"] + pieces["out"]
    late = pieces["qkv"]

    pairs = [
        (back_hbm, back_sum), (hidden_hbm, hidden), (query_mat_hbm, query_mat),
        (grad_two_hbm, grad_two), (out_mat_hbm, out_mat), (att_hbm, att), (qkv_hbm, qkv),
        (tok_hbm, tok), (qkv_mat_hbm, qkv_mat),
    ]
    loads = [pltpu.make_async_copy(src, dst, load_sem.at[i]) for i, (src, dst) in enumerate(pairs)]
    for load in loads:
        load.start()
    sums.greet(bits)
    for piece in image:
        piece.start_kv()
    gains_all[...] = jnp.zeros_like(gains_all)
    gains_all[4:5] = gain_three[...]
    gains_all[5:6] = shift_three[...]
    for load in loads[:5]:
        load.wait()

    def rows_at(index):
        return pl.ds(pl.multiple_of(index * tile, tile), tile)

    def query_back(index, carry):
        span = rows_at(index)
        back = back_sum[span, :]
        unit, inverse = normalize(hidden[span, :])
        normed[span, :] = (unit * as_row(gain_two) + as_row(shift_two)).astype(BF16)
        grad = dot_nt(back, query_mat[...])
        gains_all[2:3] += jnp.sum(grad * unit, axis=0, keepdims=True)
        gains_all[3:4] += jnp.sum(grad, axis=0, keepdims=True)
        grad_one = grad_two[span, :] + norm_back(grad, as_row(gain_two), unit, inverse)
        grad_two[span, :] = grad_one
        low[span, :] = grad_one.astype(BF16)
        grad_att[span, :] = dot_nt(grad_one.astype(BF16), out_mat[...]).astype(BF16)
        return carry

    lax.fori_loop(0, rows // tile, query_back, 0)
    for piece in image:
        piece.advance()

    def weight(left, right, target, which):
        cols = target.shape[-1]
        start = pl.multiple_of(which * cols, 128)
        cut_blocks(target, dot_tn(left[...], right[:, pl.ds(start, cols)]))

    def weights(left, right, mine, send, group):
        weight(left, right, send, 1 - side)
        for piece in group:
            piece.start_kv()
        weight(left, right, mine, side)

    weights(normed, back_sum, query_mine, query_send, pieces["query"])
    loads[5].wait()
    loads[6].wait()
    weights(att, low, out_mine, out_send, pieces["out"])
    for piece in image + middle:
        piece.advance()

    mask = same_head()
    causal = causal_mask(length)

    def attend(cap):
        span = pl.ds(cap * length, length)
        for group in range(GROUPS):
            lo = group * LANES
            query = spread(qkv[span, lo : lo + LANES] * SCALE, mask)
            key = qkv[span, width + lo : width + lo + LANES]
            value = qkv[span, 2 * width + lo : 2 * width + lo + LANES]
            cot = spread(grad_att[span, lo : lo + LANES], mask)
            scores = jnp.where(causal, dot_nt(key, query), NEG)
            exponent = jnp.exp(scores - jnp.max(scores, axis=0, keepdims=True))
            probs = exponent / jnp.sum(exponent, axis=0, keepdims=True)
            grad_probs = dot_nt(value, cot)
            mean = jnp.sum(probs * grad_probs, axis=0, keepdims=True)
            grad_scores = (probs * (grad_probs - mean)).astype(BF16)
            grad_q = gather_heads(dot_tn(grad_scores, key)) * SCALE
            grad_qkv[span, lo : lo + LANES] = grad_q.astype(BF16)
            grad_qkv[span, width + lo : width + lo + LANES] = dot(grad_scores, query).astype(BF16)
            grad_qkv[span, 2 * width + lo : 2 * width + lo + LANES] = dot(
                probs.astype(BF16), cot
            ).astype(BF16)

    for first_cap in range(0, captions, 4):
        for cap in range(first_cap, min(first_cap + 4, captions)):
            attend(cap)
        for piece in middle + image:
            piece.advance()
    loads[7].wait()
    loads[8].wait()

    def token_norm(index, carry):
        span = rows_at(index)
        unit, _ = normalize(tok[span, :].astype(F32))
        normed[span, :] = (unit * as_row(gain_one) + as_row(shift_one)).astype(BF16)
        return carry

    lax.fori_loop(0, rows // tile, token_norm, 0)
    weights(normed, grad_qkv, qkv_mine, qkv_send, late)
    for piece in late + middle + image:
        piece.advance()

    def token_back(index, carry):
        span = rows_at(index)
        unit, inverse = normalize(tok[span, :].astype(F32))
        grad = dot_nt(grad_qkv[span, :], qkv_mat[...])
        gains_all[0:1] += jnp.sum(grad * unit, axis=0, keepdims=True)
        gains_all[1:2] += jnp.sum(grad, axis=0, keepdims=True)
        back = grad_two[span, :] + norm_back(grad, as_row(gain_one), unit, inverse)
        grad_tok[span, :] = back.astype(BF16)
        return carry

    lax.fori_loop(0, rows // tile, token_back, 0)
    own_cols = pl.ds(pl.multiple_of(side * half, 128), half)
    other_cols = pl.ds(pl.multiple_of((1 - side) * half, 128), half)
    gain_copy = sums.copy(sums.take_index(), gains_all.at[:, other_cols], gain_kv, {"kv": 1 - side})
    gain_copy.start()
    stage = -1
    everything = late + image + middle
    while stage < len(bits) or not all(piece.pending is None for piece in everything):
        if stage < len(bits):
            gain_copy.wait()
            if stage < 0:
                gain_buf[0] = gains_all[:, own_cols] + gain_kv[...]
            else:
                gain_buf[stage + 1] = gain_buf[stage] + gain_recv[stage]
            stage += 1
            if stage < len(bits):
                gain_copy = sums.copy(
                    sums.take_index(), gain_buf.at[stage], gain_recv.at[stage], sums.partner(bits[stage])
                )
                gain_copy.start()
            else:
                gains_out[...] = gain_buf[stage]
        for piece in everything:
            piece.advance()


def end(
    back, hidden, grad_two, att, qkv, tokens, qkv_mat, out_mat, query_mat, gain_one, shift_one,
    gain_two, shift_two, gain_three, shift_three, kv_mine, kv_send, length, size
):
    bits = list(range(size.bit_length() - 1))
    axes = bits[::-1]
    rows, width = hidden.shape
    captions = rows // length
    tile = min(256, rows)
    block = width // size
    lead = (2,) * len(bits)
    third = width // 3
    plan = []
    plan.append(("query", 0, width // 2, axes, turned(bits, 0), True))
    plan.append(("out", 0, width // 2, axes, turned(bits, 1), True))
    for by in range(3):
        plan.append(("kv", by * third, third, axes, turned(bits, by), True))
    col = 0
    for cols in (width // 3, width // 6):
        for by in range(3):
            plan.append(("qkv", col, cols, axes, turned(bits, by), True))
            col += cols
    buffers = []
    copies = 2 + len(bits)
    for name, col, cols, piece_axes, order, kv in plan:
        for count in range(len(order), -1, -1):
            buffers.append(pltpu.VMEM((2,) * count + (block, cols), BF16))
            copies += 1
    vmem = pl.BlockSpec(memory_space=pltpu.VMEM)
    hbm = pl.BlockSpec(memory_space=pl.ANY)
    sds = jax.ShapeDtypeStruct
    cut = lambda cols: pltpu.VMEM(lead + (block, cols), BF16)
    outs = [sds((rows, width), BF16)]
    outs += [sds((block, cols), F32) for cols in (3 * width // 2, width // 2, width // 2, width)]
    outs += [sds((8, width // 2), F32)]
    low_rows = lambda cols: pltpu.VMEM((rows, cols), BF16)
    return pl.pallas_call(
        functools.partial(end_body, plan=plan, bits=bits, length=length, tile=tile),
        in_specs=[hbm] * 9 + [vmem] * 7 + [hbm],
        out_specs=[vmem] * len(outs),
        out_shape=outs,
        scratch_shapes=[
            pltpu.SemaphoreType.DMA((copies,)), pltpu.SemaphoreType.DMA((copies,)),
            pltpu.SemaphoreType.DMA((9,)),
            low_rows(width), pltpu.VMEM((rows, width), F32), pltpu.VMEM((rows, width), F32), low_rows(width),
            low_rows(3 * width), low_rows(width), pltpu.VMEM(qkv_mat.shape, BF16),
            pltpu.VMEM(out_mat.shape, BF16), pltpu.VMEM(query_mat.shape, BF16),
            low_rows(width), low_rows(width), low_rows(width), low_rows(3 * width),
            pltpu.VMEM((8, width), F32),
            pltpu.VMEM((8, width // 2), F32), pltpu.VMEM((len(bits) + 1, 8, width // 2), F32),
            pltpu.VMEM((len(bits), 8, width // 2), F32),
            cut(3 * width // 2), cut(3 * width // 2), cut(width // 2), cut(width // 2),
            cut(width // 2), cut(width // 2),
        ] + buffers,
        compiler_params=pltpu.CompilerParams(
            vmem_limit_bytes=VMEM_MOST, collective_id=0, has_side_effects=True
        ),
        name="end",
    )(
        back, hidden, grad_two, att, qkv, tokens, qkv_mat, out_mat, query_mat, gain_one, shift_one,
        gain_two, shift_two, gain_three, shift_three, kv_mine, kv_send,
    )


def hand_over_body(*refs):
    count = len(refs) // 2
    for source, target in zip(refs[:count], refs[count:]):
        target[...] = source[...]


def hand_over(*arrays):
    vmem = pl.BlockSpec(memory_space=pltpu.VMEM)
    return pl.pallas_call(
        hand_over_body,
        in_specs=[vmem] * len(arrays),
        out_specs=[vmem] * len(arrays),
        out_shape=[jax.ShapeDtypeStruct(v.shape, v.dtype) for v in arrays],
        name="hand_over",
    )(*arrays)


def exchange(value, axis, bit, size):
    return lax.ppermute(value, axis, [(i, i ^ bit) for i in range(size)])


def split_rows(array, size):
    bits = size.bit_length() - 1
    return array.reshape((2,) * bits + (array.shape[0] // size, array.shape[1]))


def body(
    tokens, images, image_counts, cotangent, norm1_gain, norm1_shift, self_qkv, self_out,
    norm2_gain, norm2_shift, cross_q, cross_kv, cross_out, norm3_gain, norm3_shift, w_up, w_down,
):
    captions, length, width = tokens.shape
    caps, slots, _ = images.shape
    side = lax.axis_index("kv")
    me = lax.axis_index("dp")
    groups = lax.axis_size("dp")
    tok = tokens.reshape(captions * length, width)
    cot = cotangent.reshape(captions * length, width)
    short = -(-SHORT // 16) * 16
    valid = jnp.clip(image_counts - side * slots, 0, slots)
    swap = lambda v: exchange(v, "kv", 1, 2)

    qkv, att, hidden, query = token_start(
        tok, norm1_gain, norm1_shift, self_qkv, self_out, norm2_gain,
        norm2_shift, cross_q, length,
    )

    def both(own):
        other = swap(own)
        first = jnp.where(side == 0, own, other)
        second = jnp.where(side == 0, other, own)
        return jnp.concatenate([first, second], axis=0)

    queries = both(query.reshape(captions, length, width))
    kv, part, lse_part = cross_start(valid, images, cross_kv, queries, short)
    layer_out, grad_two, grads, lse, delta, up_sum, down_sum, cross_sum, gain3, shift3 = feed(
        part, lse_part, hidden, cot, cross_out, norm3_gain, norm3_shift, w_up, w_down, length, groups
    )
    cut = lambda v: split_rows(v, groups)
    early = [cut(v.reshape(-1, v.shape[-1])) for v in (up_sum, down_sum, cross_sum)]
    stats = lambda v: v.reshape(caps, GROUPS, LANES)
    back, images_grad, kv_mine, kv_send, w_up_grad, down_grad, cross_out_grad = cross_back(
        valid, kv, queries, grads.reshape(caps, length, width), stats(lse), stats(delta), cross_kv,
        images, early, groups
    )
    (
        tokens_grad, self_qkv_grad, self_out_grad, cross_q_grad, cross_kv_grad, gains, layer_out,
        w_up_grad, down_grad, cross_out_grad,
    ) = hand_over(*end(
        back.reshape(captions * length, width), hidden, grad_two, att, qkv, tok, self_qkv, self_out,
        cross_q, norm1_gain, norm1_shift, norm2_gain, norm2_shift, gain3, shift3, cut(kv_mine),
        cut(kv_send), length, groups,
    ), layer_out, w_up_grad, down_grad, cross_out_grad)
    return (
        layer_out.reshape(captions, length, width),
        tokens_grad.reshape(captions, length, width),
        images_grad,
        gains[0], gains[1], self_qkv_grad, self_out_grad, gains[2], gains[3], cross_q_grad,
        cross_kv_grad, cross_out_grad, gains[4], gains[5], w_up_grad, down_grad,
    )


def solution(mesh):
    return jax.shard_map(
        body,
        mesh=mesh,
        in_specs=(
            P(("dp", "kv"), None, None), P("dp", "kv", None), P("dp"), P(("dp", "kv"), None, None),
        ) + (P(),) * 13,
        out_specs=(
            P(("dp", "kv"), None, None), P(("dp", "kv"), None, None), P("dp", "kv", None),
            P("kv"), P("kv"), P("dp", "kv"), P("dp", "kv"), P("kv"), P("kv"), P("dp", "kv"),
            P("dp", "kv"), P("dp", "kv"), P("kv"), P("kv"), P("dp", "kv"), P("dp", "kv"),
        ),
        check_vma=False,
    )
```

```python
import functools

import jax
import jax.numpy as jnp
from jax import lax
from jax.experimental import pallas as pl
from jax.experimental.pallas import tpu as pltpu
from jax.sharding import PartitionSpec as P

HEADS = 12
HEAD_DIM = 64
SHORT = 196
LANES = 256
PACK = LANES // HEAD_DIM
GROUPS = HEADS // PACK
SCALE = HEAD_DIM ** (-0.5)
NEG = -1e30
F32 = jnp.float32
BF16 = jnp.bfloat16
VMEM_LIMIT = 60 * 1024 * 1024
VMEM_MOST = 67043328


def dot(a, b):
    return jnp.dot(a, b, preferred_element_type=F32)


def dot_nt(a, b):
    return lax.dot_general(a, b, (((1,), (1,)), ((), ())), preferred_element_type=F32)


def dot_tn(a, b):
    return lax.dot_general(a, b, (((0,), (0,)), ((), ())), preferred_element_type=F32)


def normalize(values):
    centered = values - jnp.mean(values, axis=-1, keepdims=True)
    inverse = lax.rsqrt(jnp.mean(centered * centered, axis=-1, keepdims=True) + 1e-05)
    return centered * inverse, inverse


def norm_back(grad, gain, unit, inverse):
    scaled = grad * gain
    mean_one = jnp.mean(scaled, axis=-1, keepdims=True)
    mean_two = jnp.mean(scaled * unit, axis=-1, keepdims=True)
    return (scaled - mean_one - unit * mean_two) * inverse


def as_row(ref):
    return ref[...].reshape(1, ref.shape[0])


def iota(shape, dim):
    return lax.broadcasted_iota(jnp.int32, shape, dim)


def same_head():
    shape = (LANES, LANES)
    return (iota(shape, 0) // HEAD_DIM) == (iota(shape, 1) // HEAD_DIM)


def spread(rows, mask):
    stacked = jnp.concatenate([rows] * PACK, axis=0)
    return jnp.where(mask, stacked, jnp.zeros_like(stacked))


def gather_heads(full):
    count = full.shape[0] // PACK
    head = iota((count, LANES), 1) // HEAD_DIM
    out = full[:count]
    for index in range(1, PACK):
        out = jnp.where(head == index, full[index * count : (index + 1) * count], out)
    return out


def split_two(value):
    high = value.astype(BF16)
    return high, (value - high.astype(F32)).astype(BF16)


def lanes_to_rows(row, mask_low):
    shape = (HEAD_DIM, LANES)
    pick = iota(shape, 0) == (iota(shape, 1) % HEAD_DIM)
    high, low = split_two(jnp.where(pick, row, 0.0))
    return dot(high, mask_low) + dot(low, mask_low)


def rows_to_lanes(rows, mask_low):
    high, low = split_two(rows)
    summed = dot(high, mask_low) + dot(low, mask_low)
    shape = (HEAD_DIM, LANES)
    pick = iota(shape, 0) == (iota(shape, 1) % HEAD_DIM)
    return jnp.sum(jnp.where(pick, summed, 0.0), axis=0, keepdims=True)


def lane_slice(group):
    return slice(group * LANES, (group + 1) * LANES)


def causal_mask(length):
    shape = (length, LANES)
    return iota(shape, 0) <= (iota(shape, 1) % HEAD_DIM)


def token_start_body(
    tok_ref, gain_one, shift_one, qkv_mat, out_mat, gain_two, shift_two, query_mat,
    qkv_ref, att_ref, hidden_ref, queries_hbm, send_sem, recv_sem, store_sem, held, *, length
):
    step = pl.program_id(0)
    side = lax.axis_index("kv")
    tiles, tile, _ = held.shape

    def copies(index):
        into = queries_hbm.at[side, pl.ds(pl.multiple_of(index * tile, tile), tile)]
        return (
            pltpu.make_async_copy(held.at[index], into, store_sem.at[index]),
            pltpu.make_async_remote_copy(
                src_ref=held.at[index], dst_ref=into, send_sem=send_sem.at[index],
                recv_sem=recv_sem.at[index], device_id={"kv": 1 - side},
                device_id_type=pl.DeviceIdType.MESH,
            ),
        )

    @pl.when(step == 0)
    def _():
        barrier = pltpu.get_barrier_semaphore()
        pl.semaphore_signal(barrier, inc=1, device_id={"kv": 1 - side}, device_id_type=pl.DeviceIdType.MESH)
        pl.semaphore_wait(barrier, 1)

    x = tok_ref[...].astype(F32)
    unit, _ = normalize(x)
    normed = (unit * as_row(gain_one) + as_row(shift_one)).astype(BF16)
    width = x.shape[1]
    qkv_ref[...] = dot(normed, qkv_mat[...]).astype(BF16)
    mask = same_head()
    causal = causal_mask(length)
    for cap in range(x.shape[0] // length):
        rows = slice(cap * length, (cap + 1) * length)
        for group in range(GROUPS):
            lo = group * LANES
            query = qkv_ref[rows, lo : lo + LANES] * SCALE
            key = qkv_ref[rows, width + lo : width + lo + LANES]
            value = qkv_ref[rows, 2 * width + lo : 2 * width + lo + LANES]
            scores = jnp.where(causal, dot_nt(key, spread(query, mask)), NEG)
            exponent = jnp.exp(scores - jnp.max(scores, axis=0, keepdims=True))
            probs = exponent / jnp.sum(exponent, axis=0, keepdims=True)
            full = dot_tn(probs.astype(BF16), value)
            att_ref[rows, lo : lo + LANES] = gather_heads(full).astype(BF16)
    hidden = x + dot(att_ref[...], out_mat[...])
    hidden_ref[...] = hidden
    unit, _ = normalize(hidden)
    normed = (unit * as_row(gain_two) + as_row(shift_two)).astype(BF16)
    held[step] = (dot(normed, query_mat[...]).astype(BF16).astype(F32) * SCALE).astype(BF16)
    for copy in copies(step):
        copy.start()

    @pl.when(step == tiles - 1)
    def _():
        for index in range(tiles):
            for copy in copies(index):
                copy.wait()


def whole(shape):
    zeros = (0,) * len(shape)
    return pl.BlockSpec(shape, lambda *_: zeros)


def token_start(tokens, gain_one, shift_one, qkv_mat, out_mat, gain_two, shift_two, query_mat, length):
    rows, width = tokens.shape
    tile = min(256, rows)
    row_block = lambda cols: pl.BlockSpec((tile, cols), lambda i: (i, 0))
    return pl.pallas_call(
        functools.partial(token_start_body, length=length),
        grid=(rows // tile,),
        in_specs=[
            row_block(width), whole((width,)), whole((width,)), whole(qkv_mat.shape),
            whole(out_mat.shape), whole((width,)), whole((width,)), whole(query_mat.shape),
        ],
        out_specs=[
            row_block(3 * width), row_block(width), row_block(width), pl.BlockSpec(memory_space=pl.ANY),
        ],
        out_shape=[
            jax.ShapeDtypeStruct((rows, 3 * width), BF16),
            jax.ShapeDtypeStruct((rows, width), BF16),
            jax.ShapeDtypeStruct((rows, width), F32),
            jax.ShapeDtypeStruct((2, rows, width), BF16),
        ],
        scratch_shapes=[pltpu.SemaphoreType.DMA((rows // tile,))] * 3
        + [pltpu.VMEM((rows // tile, tile, width), BF16)],
        compiler_params=pltpu.CompilerParams(
            vmem_limit_bytes=VMEM_LIMIT, collective_id=2, has_side_effects=True
        ),
        name="token_start",
    )(tokens, gain_one, shift_one, qkv_mat, out_mat, gain_two, shift_two, query_mat)


def most(values):
    return functools.reduce(jnp.maximum, values)


def cross_start_body(valid_ref, img_ref, kv_mat, query_ref, kv_ref, att_ref, lse_ref, *, short):
    batch, slots, _ = img_ref.shape
    width = query_ref.shape[2]
    valids = [valid_ref[pl.program_id(0) * batch + cap] for cap in range(batch)]
    longest = most(valids)

    def work(count):
        mask = same_head()
        row = iota((count, LANES), 0)
        units = [(cap, group) for cap in range(batch) for group in range(GROUPS)]

        def project(unit, first):
            cap, group = unit
            lo = first + group * LANES
            columns = dot(img_ref[cap, :count], kv_mat[:, lo : lo + LANES]).astype(BF16)
            kv_ref[cap, :count, lo : lo + LANES] = columns
            return columns

        key, value = project(units[0], 0), project(units[0], width)
        for unit, later in zip(units, units[1:] + [None]):
            cap, group = unit
            lo = group * LANES
            inside = row < valids[cap]
            scores = dot_nt(key, spread(query_ref[cap, :, lo : lo + LANES], mask))
            if later:
                key = project(later, 0)
            scores = jnp.where(inside, scores, NEG)
            peak = jnp.max(scores, axis=0, keepdims=True)
            exponent = jnp.where(inside, jnp.exp(scores - peak), 0.0)
            total = jnp.maximum(jnp.sum(exponent, axis=0, keepdims=True), 1.0)
            held = value
            if later:
                value = project(later, width)
            probs = (exponent * (1.0 / total)).astype(BF16)
            att_ref[cap, :, lo : lo + LANES] = gather_heads(dot_tn(probs, held)).astype(BF16)
            lse_ref[cap, group : group + 1] = peak + jnp.log(total)

    @pl.when(longest <= 0)
    def _():
        att_ref[...] = jnp.zeros_like(att_ref)
        lse_ref[...] = jnp.full_like(lse_ref, NEG)

    if short < slots and batch <= 2:
        pl.when((longest > 0) & (longest <= short))(lambda: work(short))
        pl.when(longest > short)(lambda: work(slots))
    else:
        pl.when(longest > 0)(lambda: work(slots))


def cross_start(valid, images, kv_mat, queries, short):
    caps, slots, width = images.shape
    length = queries.shape[1]
    batch = 4 if caps % 4 == 0 else 1
    block = lambda *shape: pl.BlockSpec((batch,) + shape, lambda i, *_: (i, 0, 0))
    return pl.pallas_call(
        functools.partial(cross_start_body, short=short),
        grid_spec=pltpu.PrefetchScalarGridSpec(
            num_scalar_prefetch=1,
            grid=(caps // batch,),
            in_specs=[block(slots, width), whole(kv_mat.shape), block(length, width)],
            out_specs=[block(slots, 2 * width), block(length, width), block(GROUPS, LANES)],
        ),
        out_shape=[
            jax.ShapeDtypeStruct((caps, slots, 2 * width), BF16),
            jax.ShapeDtypeStruct((caps, length, width), BF16),
            jax.ShapeDtypeStruct((caps, GROUPS, LANES), F32),
        ],
        compiler_params=pltpu.CompilerParams(vmem_limit_bytes=VMEM_LIMIT),
        name="cross_start",
    )(valid, images, kv_mat, queries)


def feed_body(
    part_hbm, lse_hbm, hidden_ref, cot_ref, cross_mat, gain_ref, shift_ref, up_one, up_two, down_ref,
    out_ref, grad_two_ref, grads_hbm, lse_out, delta_out, up_keep, up_first, up_second, up_both,
    down_keep, down_away, cross_sum, gain_grad, shift_grad,
    send_sem, recv_sem, load_sem, att_one, att_two, lse_one, lse_two, att_full, att_low, hidden_two,
    normed_ref, acc_out, acc_grad, grad_att, lse_own, delta_own, up_pair, up_got, down_pair, down_got,
    cross_pair, cross_got, *, length, tile, bits, steps
):
    step = pl.program_id(0)
    me, side = lax.axis_index("dp"), lax.axis_index("kv")
    rows, width = hidden_ref.shape
    captions = rows // length
    tiles = rows // tile
    half = width // 2
    sub = up_one.shape[1]
    blocks = up_pair.shape[2]
    own = lambda bit: (me // (1 << bit)) % 2

    def remote(src, dst, index):
        return pltpu.make_async_remote_copy(
            src_ref=src, dst_ref=dst, send_sem=send_sem.at[index], recv_sem=recv_sem.at[index],
            device_id={"kv": 1 - side}, device_id_type=pl.DeviceIdType.MESH,
        )

    def row_span(index):
        return pl.ds(pl.multiple_of(index * tile, tile), tile)

    def chunk_copies(slot):
        return (
            remote(up_pair.at[slot, 1 - side], up_got.at[slot], 2 + slot),
            remote(down_pair.at[slot, 1 - side], down_got.at[slot], 4 + slot),
        )

    cross_copy = lambda: remote(cross_pair.at[1 - side], cross_got, 6)
    lse_copy = lambda: remote(lse_own, lse_out.at[side], 7)
    delta_copy = lambda: remote(delta_own, delta_out.at[side], 8)
    grad_copy = lambda index: remote(
        grad_att.at[pl.ds(index * tile, tile)], grads_hbm.at[side, pl.ds(index * tile, tile)], 9 + index
    )
    lse_store = lambda: pltpu.make_async_copy(lse_own, lse_out.at[side], load_sem.at[2])

    def cut(target, value):
        count, height, _ = target.shape
        if height % 16 == 0:
            target[...] = value.astype(BF16).reshape(target.shape)
        else:
            for index in range(count):
                target[index] = value[index * height : (index + 1) * height].astype(BF16)

    @pl.when(step == 0)
    def _():
        part_load = pltpu.make_async_copy(part_hbm.at[side], att_one, load_sem.at[0])
        lse_load = pltpu.make_async_copy(lse_hbm.at[side], lse_one, load_sem.at[1])
        part_load.start()
        lse_load.start()
        barrier = pltpu.get_barrier_semaphore()
        pl.semaphore_signal(barrier, inc=1, device_id={"kv": 1 - side}, device_id_type=pl.DeviceIdType.MESH)
        pl.semaphore_wait(barrier, 1)
        part_swap = remote(part_hbm.at[1 - side], att_two, 0)
        lse_swap = remote(lse_hbm.at[1 - side], lse_two, 1)
        lse_swap.start()
        part_swap.start()
        mask_low = same_head().astype(BF16)
        lse_load.wait()
        part_load.wait()
        lse_swap.wait()
        part_swap.wait()

        def one_caption(cap, carry):
            span = pl.ds(pl.multiple_of(cap * length, length), length)
            for group in range(GROUPS):
                lo = group * LANES
                first = lse_one[cap, group : group + 1]
                second = lse_two[cap, group : group + 1]
                peak = jnp.maximum(first, second)
                lse = peak + jnp.log(jnp.exp(first - peak) + jnp.exp(second - peak))
                lse_own[cap, group : group + 1] = lse
                weight_one = lanes_to_rows(jnp.exp(first - lse), mask_low)
                weight_two = lanes_to_rows(jnp.exp(second - lse), mask_low)
                mixed = (
                    weight_one * att_one[span, lo : lo + LANES].astype(F32)
                    + weight_two * att_two[span, lo : lo + LANES].astype(F32)
                )
                att_full[span, lo : lo + LANES] = mixed
                att_low[span, lo : lo + LANES] = mixed.astype(BF16)
            return carry

        lax.fori_loop(0, captions, one_caption, 0)
        lse_copy().start()
        lse_store().start()

        def one_tile(index, carry):
            span = row_span(index)
            two = hidden_ref[span, :] + dot(att_low[span, :], cross_mat[...])
            hidden_two[span, :] = two
            unit, _ = normalize(two)
            normed_ref[span, :] = (unit * as_row(gain_ref) + as_row(shift_ref)).astype(BF16)
            acc_out[span, :] = two
            acc_grad[span, :] = jnp.zeros_like(two)
            return carry

        lax.fori_loop(0, tiles, one_tile, 0)

    slot = step % 2
    up_mat = jnp.concatenate([up_one[...], up_two[...]], axis=1)
    down_mat = down_ref[...].reshape(2 * sub, width)
    pre = dot(normed_ref[...], up_mat)
    cdf = 0.5 * (1.0 + lax.erf(pre * 0.7071067811865476))
    act = (pre * cdf).astype(BF16)
    acc_out[...] += dot(act, down_mat)
    cot = cot_ref[...]
    density = jnp.exp(-0.5 * pre * pre) * 0.3989422804014327
    grad_up = (dot_nt(cot, down_mat) * (cdf + pre * density)).astype(BF16)
    acc_grad[...] += dot_nt(grad_up, up_mat)
    grad_down = dot_tn(act, cot).astype(BF16)
    grad_w = dot_tn(normed_ref[...], grad_up)
    for part in range(2):
        cut(up_pair.at[slot, part], grad_w[:, part * sub : (part + 1) * sub])
        down_pair[slot, part] = grad_down[:, part * half : (part + 1) * half].reshape(2, sub, half)

    def take(chunk, place):
        for copy in chunk_copies(place):
            copy.wait()
        cols = pl.ds(pl.multiple_of(chunk * sub, sub), sub)
        for index, target in enumerate((up_keep, up_first, up_second, up_both)):
            flip = (index % 2, index // 2)
            low_bit, high_bit = (own(b) + f - 2 * own(b) * f for b, f in zip(bits[:2], flip))
            near = high_bit * 2 + low_bit

            def one(block, carry):
                source = block * 4 + near
                target[block, :, cols] = add_low(up_pair[place, side, source], up_got[place, source])
                return carry

            lax.fori_loop(0, blocks // 4, one, 0)
        total = add_low(down_pair[place, side], down_got[place])
        span = pl.ds(pl.multiple_of(chunk % (steps // 2) * sub, sub), sub)
        stays = chunk // (steps // 2) == own(bits[-2])

        @pl.when(stays)
        def _():
            down_keep[:, span, :] = total

        @pl.when(jnp.logical_not(stays))
        def _():
            down_away[:, span, :] = total

    @pl.when(step > 0)
    def _():
        take(step - 1, (step + 1) % 2)

    for copy in chunk_copies(slot):
        copy.start()

    @pl.when(step == steps - 1)
    def _():
        mask_low = same_head().astype(BF16)
        gain_grad[...] = jnp.zeros_like(gain_grad)
        shift_grad[...] = jnp.zeros_like(shift_grad)
        for index in range(tiles):
            span = pl.ds(index * tile, tile)
            unit, inverse = normalize(hidden_two[span, :])
            grad = acc_grad[span, :]
            gain_grad[...] += jnp.sum(grad * unit, axis=0, keepdims=True)
            shift_grad[...] += jnp.sum(grad, axis=0, keepdims=True)
            two = cot_ref[span, :].astype(F32) + norm_back(grad, as_row(gain_ref), unit, inverse)
            grad_two_ref[span, :] = two
            low = two.astype(BF16)
            normed_ref[span, :] = low
            grad_att[span, :] = dot_nt(low, cross_mat[...]).astype(BF16)
            grad_copy(index).start()
        grad_store = pltpu.make_async_copy(grad_att, grads_hbm.at[side], load_sem.at[0])
        grad_store.start()

        def one_caption(cap, carry):
            span = pl.ds(pl.multiple_of(cap * length, length), length)
            for group in range(GROUPS):
                lo = group * LANES
                product = grad_att[span, lo : lo + LANES].astype(F32) * att_full[span, lo : lo + LANES]
                delta_own[cap, group : group + 1] = rows_to_lanes(product, mask_low)
            return carry

        lax.fori_loop(0, captions, one_caption, 0)
        delta_copy().start()
        delta_store = pltpu.make_async_copy(delta_own, delta_out.at[side], load_sem.at[1])
        delta_store.start()
        grad_cross = dot_tn(att_low[...], normed_ref[...])
        for part in range(2):
            cut(cross_pair.at[part], grad_cross[:, part * half : (part + 1) * half])
        cross_copy().start()
        out_ref[...] = acc_out[...].astype(BF16)
        take(steps - 1, (steps - 1) % 2)
        cross_copy().wait()

        def one(block, carry):
            cross_sum[block] = add_low(cross_pair[side, block], cross_got[block])
            return carry

        lax.fori_loop(0, blocks, one, 0)
        for copy in [lse_copy(), lse_store(), delta_copy(), delta_store, grad_store]:
            copy.wait()
        for index in range(tiles):
            grad_copy(index).wait()


def feed(part, lse_part, hidden, cot, cross_mat, gain, shift, up_mat, down_mat, length, size):
    rows, width = hidden.shape
    captions = rows // length
    units = up_mat.shape[1]
    sub = 256
    steps = units // 2 // sub
    tile = min(256, rows)
    half = width // 2
    block = width // size
    bits = list(range(size.bit_length() - 1))
    stat = (captions, GROUPS, LANES)
    sds = jax.ShapeDtypeStruct
    once = lambda shape: pl.BlockSpec(shape, lambda *_: (0,) * len(shape), pipeline_mode=pl.Buffered(1))
    hbm = pl.BlockSpec(memory_space=pl.ANY)
    copies = 9 + rows // tile
    f32_rows = lambda: pltpu.VMEM((rows, width), F32)
    low_rows = lambda: pltpu.VMEM((rows, width), BF16)
    quarter = (size // 4, block, units // 2)
    return pl.pallas_call(
        functools.partial(feed_body, length=length, tile=tile, bits=bits, steps=steps),
        grid=(steps,),
        in_specs=[
            hbm, hbm, once((rows, width)), once((rows, width)), once((width, width)),
            once((width,)), once((width,)),
            pl.BlockSpec((width, sub), lambda i: (0, i)),
            pl.BlockSpec((width, sub), lambda i: (0, i + steps)),
            pl.BlockSpec((2, sub, width), lambda i: (0, i, 0)),
        ],
        out_specs=[
            whole((rows, width)), whole((rows, width)), hbm, hbm, hbm,
            whole(quarter), whole(quarter), whole(quarter), whole(quarter),
            whole((2, units // 4, half)), whole((2, units // 4, half)),
            whole((size, block, half)), whole((1, width)), whole((1, width)),
        ],
        out_shape=[
            sds((rows, width), BF16), sds((rows, width), F32), sds((2, rows, width), BF16),
            sds((2,) + stat, F32), sds((2,) + stat, F32),
            sds(quarter, BF16), sds(quarter, BF16), sds(quarter, BF16), sds(quarter, BF16),
            sds((2, units // 4, half), BF16), sds((2, units // 4, half), BF16),
            sds((size, block, half), BF16), sds((1, width), F32), sds((1, width), F32),
        ],
        scratch_shapes=[
            pltpu.SemaphoreType.DMA((copies,)), pltpu.SemaphoreType.DMA((copies,)),
            pltpu.SemaphoreType.DMA((3,)),
            low_rows(), low_rows(), pltpu.VMEM(stat, F32), pltpu.VMEM(stat, F32), f32_rows(), low_rows(),
            f32_rows(), low_rows(), f32_rows(), f32_rows(), low_rows(),
            pltpu.VMEM(stat, F32), pltpu.VMEM(stat, F32),
            pltpu.VMEM((2, 2, size, block, sub), BF16), pltpu.VMEM((2, size, block, sub), BF16),
            pltpu.VMEM((2, 2, 2, sub, half), BF16), pltpu.VMEM((2, 2, sub, half), BF16),
            pltpu.VMEM((2, size, block, half), BF16), pltpu.VMEM((size, block, half), BF16),
        ],
        compiler_params=pltpu.CompilerParams(
            vmem_limit_bytes=VMEM_MOST, collective_id=1, has_side_effects=True
        ),
        name="feed",
    )(
        part.reshape(2, rows, width), lse_part.reshape((2,) + stat), hidden, cot, cross_mat, gain, shift,
        up_mat, up_mat, down_mat.reshape(2, units // 2, width),
    )


def cross_back_body(
    valid_ref, side_ref, kv_ref, query_ref, grad_ref, lse_ref, delta_ref, kv_mat, img_ref,
    grad_query_ref, grad_img_ref, mine_ref, send_ref, grad_kv_ref, acc_ref, *, short
):
    step = pl.program_id(0)
    batch, slots, _ = kv_ref.shape
    width = query_ref.shape[2]
    held = img_ref.shape[0]
    base = step % (held // batch) * batch
    valids = [valid_ref[step * batch + cap] for cap in range(batch)]
    longest = most(valids)

    @pl.when(step == 0)
    def _():
        acc_ref[...] = jnp.zeros_like(acc_ref)

    def work(count):
        mask = same_head()
        row = iota((count, LANES), 0)

        def image_back(cap, part):
            place = base + cap if held > batch else cap
            lo = part * LANES
            columns = dot_nt(grad_kv_ref[place, :count], kv_mat[lo : lo + LANES, :])
            grad_img_ref[cap, :count, lo : lo + LANES] = columns.astype(BF16)

        for cap, valid in enumerate(valids):
            place = base + cap if held > batch else cap
            inside = row < valid
            for group in range(GROUPS):
                lo = group * LANES
                key = kv_ref[cap, :count, lo : lo + LANES]
                value = kv_ref[cap, :count, width + lo : width + lo + LANES]
                query = spread(query_ref[cap, :, lo : lo + LANES], mask)
                grad = spread(grad_ref[cap, :, lo : lo + LANES], mask)
                scores = dot_nt(key, query)
                probs = jnp.where(inside, jnp.exp(scores - lse_ref[cap, group : group + 1]), 0.0)
                grad_probs = dot_nt(value, grad)
                if cap > 0:
                    image_back(cap - 1, group)
                grad_scores = (probs * (grad_probs - delta_ref[cap, group : group + 1])).astype(BF16)
                back = gather_heads(dot_tn(grad_scores, key)) * SCALE
                grad_query_ref[cap, :, lo : lo + LANES] = back.astype(BF16)
                grad_kv_ref[place, :count, lo : lo + LANES] = dot(grad_scores, query).astype(BF16)
                grad_kv_ref[place, :count, width + lo : width + lo + LANES] = dot(
                    probs.astype(BF16), grad
                ).astype(BF16)
            if count < slots:
                grad_kv_ref[place, count:] = jnp.zeros((slots - count, 2 * width), BF16)
                grad_img_ref[cap, count:] = jnp.zeros((slots - count, width), BF16)
        for group in range(GROUPS):
            image_back(batch - 1, group)

    @pl.when(longest <= 0)
    def _():
        grad_query_ref[...] = jnp.zeros_like(grad_query_ref)
        for cap in range(batch):
            grad_kv_ref[base + cap] = jnp.zeros((slots, 2 * width), BF16)
        grad_img_ref[...] = jnp.zeros_like(grad_img_ref)

    if short < slots and batch <= 2:
        pl.when((longest > 0) & (longest <= short))(lambda: work(short))
        pl.when(longest > short)(lambda: work(slots))
    else:
        pl.when(longest > 0)(lambda: work(slots))

    @pl.when(base == held - batch)
    def _():
        left = img_ref[...].reshape(held * slots, width)
        right = grad_kv_ref[...].reshape(held * slots, 2 * width)
        acc_ref[...] += dot_tn(left, right)

    @pl.when(step == pl.num_programs(0) - 1)
    def _():
        side = side_ref[0]
        own = pl.ds(pl.multiple_of(side * width, width), width)
        other = pl.ds(pl.multiple_of((1 - side) * width, width), width)
        mine_ref[...] = acc_ref[:, own].astype(BF16)
        send_ref[...] = acc_ref[:, other].astype(BF16)


def cross_back(valid, side, kv, queries, grads, lse, delta, kv_mat, images, short):
    caps, slots, double = kv.shape
    width = double // 2
    length = queries.shape[1]
    held = 4 if caps % 4 == 0 else 1
    batch = min(4, held)
    block = lambda *shape: pl.BlockSpec((batch,) + shape, lambda i, *_: (i, 0, 0))
    sds = jax.ShapeDtypeStruct
    return pl.pallas_call(
        functools.partial(cross_back_body, short=short),
        grid_spec=pltpu.PrefetchScalarGridSpec(
            num_scalar_prefetch=2,
            grid=(caps // batch,),
            in_specs=[
                block(slots, double), block(length, width), block(length, width),
                block(GROUPS, LANES), block(GROUPS, LANES), whole(kv_mat.shape),
                pl.BlockSpec((held, slots, width), lambda i, *_: (i // (held // batch), 0, 0)),
            ],
            out_specs=[
                block(length, width), block(slots, width), whole((width, width)), whole((width, width)),
            ],
            scratch_shapes=[
                pltpu.VMEM((held, slots, double), BF16), pltpu.VMEM((width, double), F32),
            ],
        ),
        out_shape=[
            sds((caps, length, width), BF16), sds((caps, slots, width), BF16),
            sds((width, width), BF16), sds((width, width), BF16),
        ],
        compiler_params=pltpu.CompilerParams(vmem_limit_bytes=VMEM_LIMIT),
        name="cross_back",
    )(valid, side, kv, queries, grads, lse, delta, kv_mat, images)


def add_low(first, second):
    return (first.astype(F32) + second.astype(F32)).astype(BF16)


def cut_blocks(target, value):
    height = target.shape[-2]
    count = len(target.shape) - 2
    if height % 16 == 0:
        target[...] = value.astype(BF16).reshape(target.shape)
    else:
        for i in range(1 << count):
            lead = tuple((i >> (count - 1 - d)) % 2 for d in range(count))
            target[lead] = value[i * height : (i + 1) * height].astype(BF16)


class Piece:
    def __init__(self, sums, source, out, col, width, bits, order, recvs, mine=None, send=None, kv_recv=None):
        self.sums, self.out, self.col, self.width = sums, out, col, width
        self.bits, self.order, self.recvs = list(bits), list(order), recvs
        self.mine, self.send, self.kv_recv = mine, send, kv_recv
        self.now, self.holds, self.pending = 0, source, None

    def columns(self, ref):
        return (slice(None), pl.ds(self.col, self.width) if ref.shape[-1] != self.width else slice(None))

    def start_kv(self):
        whole_lead = (slice(None),) * len(self.bits)
        self.pending = self.sums.copy(
            self.send.at[whole_lead + self.columns(self.send)], self.kv_recv, {"kv": 1 - self.sums.side}
        )
        self.pending.start()

    def start(self):
        bit = self.order[self.now]
        lead = tuple(1 - self.sums.own(bit) if b == bit else slice(None) for b in self.bits)
        self.pending = self.sums.copy(
            self.holds.at[lead + self.columns(self.holds)], self.recvs[self.now], self.sums.partner(bit)
        )
        self.pending.start()

    def add(self, kept, arrived, cols, left, fixed):
        def one(i, carry):
            inner = {b: (i // (1 << (len(left) - 1 - d))) % 2 for d, b in enumerate(left)}
            lead = tuple(inner[b] if b in inner else fixed[b] for b in self.bits)
            into = tuple(inner[b] for b in left)
            arrived[into] = add_low(kept[lead + cols], arrived[into])
            return carry

        lax.fori_loop(0, 1 << len(left), one, 0)

    def advance(self):
        if self.pending is None:
            return True
        self.pending.wait()
        self.pending = None
        if self.holds is None:
            self.add(self.mine, self.kv_recv, self.columns(self.mine), self.bits, {})
            self.holds = self.kv_recv
            self.start()
            return False
        bit = self.order[self.now]
        arrived, cols = self.recvs[self.now], self.columns(self.holds)
        left = [b for b in self.bits if b != bit]
        if not left:
            total = self.holds[(self.sums.own(bit),) + cols].astype(F32) + arrived[...].astype(F32)
            self.out[:, self.col : self.col + self.width] = total
            return True
        self.add(self.holds, arrived, cols, left, {bit: self.sums.own(bit)})
        self.bits, self.holds, self.now = left, arrived, self.now + 1
        self.start()
        return False


class Sums:
    def __init__(self, send_sem, recv_sem):
        self.send_sem, self.recv_sem, self.count = send_sem, recv_sem, 0
        self.me, self.side = lax.axis_index("dp"), lax.axis_index("kv")

    def own(self, bit):
        return (self.me // (1 << bit)) % 2

    def partner(self, bit):
        return {"dp": self.me + (1 - 2 * self.own(bit)) * (1 << bit)}

    def copy(self, src, dst, device):
        index = self.count
        self.count += 1
        return pltpu.make_async_remote_copy(
            src_ref=src, dst_ref=dst, send_sem=self.send_sem.at[index], recv_sem=self.recv_sem.at[index],
            device_id=device, device_id_type=pl.DeviceIdType.MESH,
        )

    def greet(self, bits):
        barrier = pltpu.get_barrier_semaphore()
        for device in [{"kv": 1 - self.side}] + [self.partner(bit) for bit in bits]:
            pl.semaphore_signal(barrier, inc=1, device_id=device, device_id_type=pl.DeviceIdType.MESH)
        pl.semaphore_wait(barrier, 1 + len(bits))


def turned(bits, by):
    first = bits[:-1]
    by %= len(first)
    return first[by:] + first[:by] + bits[-1:]


def end_body(
    back_hbm, hidden_hbm, grad_two_hbm, att_hbm, qkv_hbm, tok_hbm, qkv_mat_hbm, out_mat_hbm, query_mat_hbm,
    gain_one, shift_one, gain_two, shift_two, gain_three, shift_three,
    up_keep, up_first, up_second, up_both, down_keep, down_away, cross_ref, kv_mine, kv_send,
    grad_tok, up_out, down_out, cross_out, qkv_out, out_out, query_out, kv_out, gains_out,
    *scratch, plan, bits, length, tile
):
    scratch = list(scratch)
    (
        send_sem, recv_sem, load_sem, back_one, back_two, hidden, grad_two, att, qkv, tok, qkv_mat,
        out_mat, query_mat, back_sum, normed, low, grad_att, grad_qkv, gains_all, gain_kv,
        gain_buf, gain_recv, qkv_mine, qkv_send, out_mine, out_send, query_mine, query_send,
        up_ref, down_ref,
    ) = scratch[:30]
    rest = scratch[30:]
    sums = Sums(send_sem, recv_sem)
    side = sums.side
    captions = back_one.shape[0]
    rows, width = hidden.shape
    half = width // 2
    named = dict(
        up=(up_ref, None, None, up_out), down=(down_ref, None, None, down_out),
        cross=(cross_ref, None, None, cross_out), qkv=(None, qkv_mine, qkv_send, qkv_out),
        out=(None, out_mine, out_send, out_out), query=(None, query_mine, query_send, query_out),
        kv=(None, kv_mine, kv_send, kv_out),
    )
    pieces = {}
    for name, col, cols, axes, order, kv in plan:
        source, mine, send, out = named[name]
        kv_recv = rest.pop(0) if kv else None
        recvs = [rest.pop(0) for _ in order]
        pieces.setdefault(name, []).append(
            Piece(sums, source, out, col, cols, axes, order, recvs, mine, send, kv_recv)
        )
    early = pieces["up"] + pieces["down"] + pieces["cross"]
    image = pieces["kv"]
    middle = pieces["query"] + pieces["out"]
    late = pieces["qkv"]

    own_caps = pl.ds(pl.multiple_of(side * captions, captions), captions)
    other_caps = pl.ds(pl.multiple_of((1 - side) * captions, captions), captions)
    pairs = [
        (back_hbm.at[own_caps], back_one), (hidden_hbm, hidden), (query_mat_hbm, query_mat),
        (grad_two_hbm, grad_two), (out_mat_hbm, out_mat), (att_hbm, att), (qkv_hbm, qkv),
        (tok_hbm, tok), (qkv_mat_hbm, qkv_mat),
    ]
    loads = [pltpu.make_async_copy(src, dst, load_sem.at[i]) for i, (src, dst) in enumerate(pairs)]
    for load in loads:
        load.start()
    sums.greet(bits)
    swap = sums.copy(back_hbm.at[other_caps], back_two, {"kv": 1 - side})
    swap.start()
    for piece in image:
        piece.start_kv()

    def sum_terms(target, terms):
        count = len(target.shape) - 2

        def one(i, carry):
            lead = tuple((i // (1 << (count - 1 - d))) % 2 for d in range(count))
            total = terms[0][lead].astype(F32)
            for term in terms[1:]:
                total += term[lead].astype(F32)
            target[lead] = total.astype(BF16)
            return carry

        lax.fori_loop(0, 1 << count, one, 0)

    sum_terms(up_ref, (up_keep, up_first, up_second, up_both))
    sum_terms(down_ref, (down_keep, down_away))
    for piece in early:
        piece.start()
    gains_all[...] = jnp.zeros_like(gains_all)
    gains_all[4:5] = gain_three[...]
    gains_all[5:6] = shift_three[...]
    for load in loads[:5]:
        load.wait()
    swap.wait()

    def rows_at(index):
        return pl.ds(pl.multiple_of(index * tile, tile), tile)

    def query_back(index, carry):
        span = rows_at(index)
        caps = pl.ds(index * (tile // length), tile // length)
        back = add_low(back_one[caps], back_two[caps]).reshape(tile, width)
        back_sum[span, :] = back
        unit, inverse = normalize(hidden[span, :])
        normed[span, :] = (unit * as_row(gain_two) + as_row(shift_two)).astype(BF16)
        grad = dot_nt(back, query_mat[...])
        gains_all[2:3] += jnp.sum(grad * unit, axis=0, keepdims=True)
        gains_all[3:4] += jnp.sum(grad, axis=0, keepdims=True)
        grad_one = grad_two[span, :] + norm_back(grad, as_row(gain_two), unit, inverse)
        grad_two[span, :] = grad_one
        low[span, :] = grad_one.astype(BF16)
        grad_att[span, :] = dot_nt(grad_one.astype(BF16), out_mat[...]).astype(BF16)
        return carry

    lax.fori_loop(0, rows // tile, query_back, 0)
    for piece in image:
        piece.advance()

    def weight(left, right, target, which):
        cols = target.shape[-1]
        start = pl.multiple_of(which * cols, 128)
        cut_blocks(target, dot_tn(left[...], right[:, pl.ds(start, cols)]))

    def weights(left, right, mine, send, group):
        weight(left, right, send, 1 - side)
        for piece in group:
            piece.start_kv()
        weight(left, right, mine, side)

    weights(normed, back_sum, query_mine, query_send, pieces["query"])
    loads[5].wait()
    loads[6].wait()
    weights(att, low, out_mine, out_send, pieces["out"])
    for piece in early + image + middle:
        piece.advance()

    mask = same_head()
    causal = causal_mask(length)

    def attend(cap):
        span = pl.ds(pl.multiple_of(cap * length, length), length)
        for group in range(GROUPS):
            lo = group * LANES
            query = spread(qkv[span, lo : lo + LANES] * SCALE, mask)
            key = qkv[span, width + lo : width + lo + LANES]
            value = qkv[span, 2 * width + lo : 2 * width + lo + LANES]
            cot = spread(grad_att[span, lo : lo + LANES], mask)
            scores = jnp.where(causal, dot_nt(key, query), NEG)
            exponent = jnp.exp(scores - jnp.max(scores, axis=0, keepdims=True))
            probs = exponent / jnp.sum(exponent, axis=0, keepdims=True)
            grad_probs = dot_nt(value, cot)
            mean = jnp.sum(probs * grad_probs, axis=0, keepdims=True)
            grad_scores = (probs * (grad_probs - mean)).astype(BF16)
            grad_q = gather_heads(dot_tn(grad_scores, key)) * SCALE
            grad_qkv[span, lo : lo + LANES] = grad_q.astype(BF16)
            grad_qkv[span, width + lo : width + lo + LANES] = dot(grad_scores, query).astype(BF16)
            grad_qkv[span, 2 * width + lo : 2 * width + lo + LANES] = dot(
                probs.astype(BF16), cot
            ).astype(BF16)

    together = 2 if captions % 2 == 0 else 1

    def attend_some(index, carry):
        for cap in range(together):
            attend(index * together + cap)
        return carry

    lax.fori_loop(0, captions // together, attend_some, 0)
    for piece in early + middle + image:
        piece.advance()
    loads[7].wait()
    loads[8].wait()

    def token_norm(index, carry):
        span = rows_at(index)
        unit, _ = normalize(tok[span, :].astype(F32))
        normed[span, :] = (unit * as_row(gain_one) + as_row(shift_one)).astype(BF16)
        return carry

    lax.fori_loop(0, rows // tile, token_norm, 0)
    weights(normed, grad_qkv, qkv_mine, qkv_send, late)
    for piece in late + early + middle + image:
        piece.advance()

    def token_back(index, carry):
        span = rows_at(index)
        unit, inverse = normalize(tok[span, :].astype(F32))
        grad = dot_nt(grad_qkv[span, :], qkv_mat[...])
        gains_all[0:1] += jnp.sum(grad * unit, axis=0, keepdims=True)
        gains_all[1:2] += jnp.sum(grad, axis=0, keepdims=True)
        back = grad_two[span, :] + norm_back(grad, as_row(gain_one), unit, inverse)
        grad_tok[span, :] = back.astype(BF16)
        return carry

    lax.fori_loop(0, rows // tile, token_back, 0)
    own_cols = pl.ds(pl.multiple_of(side * half, 128), half)
    other_cols = pl.ds(pl.multiple_of((1 - side) * half, 128), half)
    gain_copy = sums.copy(gains_all.at[:, other_cols], gain_kv, {"kv": 1 - side})
    gain_copy.start()
    stage = -1
    everything = late + early + image + middle
    while stage < len(bits) or not all(piece.pending is None for piece in everything):
        if stage < len(bits):
            gain_copy.wait()
            if stage < 0:
                gain_buf[0] = gains_all[:, own_cols] + gain_kv[...]
            else:
                gain_buf[stage + 1] = gain_buf[stage] + gain_recv[stage]
            stage += 1
            if stage < len(bits):
                gain_copy = sums.copy(gain_buf.at[stage], gain_recv.at[stage], sums.partner(bits[stage]))
                gain_copy.start()
            else:
                gains_out[...] = gain_buf[stage]
        for piece in everything:
            piece.advance()


def end(
    back, hidden, grad_two, att, qkv, tokens, qkv_mat, out_mat, query_mat, gain_one, shift_one,
    gain_two, shift_two, gain_three, shift_three, early, kv_mine, kv_send, length, size
):
    bits = list(range(size.bit_length() - 1))
    axes = bits[::-1]
    rows, width = hidden.shape
    captions = rows // length
    tile = min(256, rows)
    block = width // size
    lead = (2,) * len(bits)
    up_terms, down_terms, cross = early
    up, down = up_terms[0], down_terms[0]
    cut_down = down.shape[-1] // 384 * 256
    third = width // 3
    plan = [("up", 0, up.shape[-1], axes[:-2], bits[2:], False)]
    down_axes = axes[:1] + axes[2:]
    for col, cols, by in ((0, cut_down, 0), (cut_down, down.shape[-1] - cut_down, 1)):
        order = [b for b in turned(bits, by) if b in down_axes]
        plan.append(("down", col, cols, down_axes, order, False))
    plan.append(("cross", 0, cross.shape[-1], axes, turned(bits, 2), False))
    plan.append(("query", 0, width // 2, axes, turned(bits, 0), True))
    plan.append(("out", 0, width // 2, axes, turned(bits, 1), True))
    for by in range(3):
        plan.append(("kv", by * third, third, axes, turned(bits, by), True))
    col = 0
    for cols in (width // 3, width // 6):
        for by in range(3):
            plan.append(("qkv", col, cols, axes, turned(bits, by), True))
            col += cols
    heights = dict(up=up.shape[-2], down=down.shape[-2], cross=cross.shape[-2])
    buffers = []
    copies = 2 + len(bits)
    for name, col, cols, piece_axes, order, kv in plan:
        shape = (heights.get(name, block), cols)
        for count in range(len(order) if kv else len(order) - 1, -1, -1):
            buffers.append(pltpu.VMEM((2,) * count + shape, BF16))
            copies += 1
    vmem = pl.BlockSpec(memory_space=pltpu.VMEM)
    hbm = pl.BlockSpec(memory_space=pl.ANY)
    sds = jax.ShapeDtypeStruct
    cut = lambda cols: pltpu.VMEM(lead + (block, cols), BF16)
    outs = [sds((rows, width), BF16)]
    outs += [sds(v.shape[-2:], F32) for v in (up, down, cross)]
    outs += [sds((block, cols), F32) for cols in (3 * width // 2, width // 2, width // 2, width)]
    outs += [sds((8, width // 2), F32)]
    low_rows = lambda cols: pltpu.VMEM((rows, cols), BF16)
    return pl.pallas_call(
        functools.partial(end_body, plan=plan, bits=bits, length=length, tile=tile),
        in_specs=[hbm] * 9 + [vmem] * 6 + [vmem] * 8 + [hbm],
        out_specs=[vmem] * len(outs),
        out_shape=outs,
        scratch_shapes=[
            pltpu.SemaphoreType.DMA((copies,)), pltpu.SemaphoreType.DMA((copies,)),
            pltpu.SemaphoreType.DMA((9,)),
            pltpu.VMEM((captions, length, width), BF16), pltpu.VMEM((captions, length, width), BF16),
            pltpu.VMEM((rows, width), F32), pltpu.VMEM((rows, width), F32), low_rows(width),
            low_rows(3 * width), low_rows(width), pltpu.VMEM(qkv_mat.shape, BF16),
            pltpu.VMEM(out_mat.shape, BF16), pltpu.VMEM(query_mat.shape, BF16),
            low_rows(width), low_rows(width), low_rows(width), low_rows(width), low_rows(3 * width),
            pltpu.VMEM((8, width), F32),
            pltpu.VMEM((8, width // 2), F32), pltpu.VMEM((len(bits) + 1, 8, width // 2), F32),
            pltpu.VMEM((len(bits), 8, width // 2), F32),
            cut(3 * width // 2), cut(3 * width // 2), cut(width // 2), cut(width // 2),
            cut(width // 2), cut(width // 2), pltpu.VMEM(up.shape, BF16), pltpu.VMEM(down.shape, BF16),
        ] + buffers,
        compiler_params=pltpu.CompilerParams(
            vmem_limit_bytes=VMEM_MOST, collective_id=0, has_side_effects=True
        ),
        name="end",
    )(
        back, hidden, grad_two, att, qkv, tokens, qkv_mat, out_mat, query_mat, gain_one, shift_one,
        gain_two, shift_two, gain_three, shift_three, *up_terms, *down_terms, cross, kv_mine, kv_send,
    )


def hand_over_body(gains_ref, *refs):
    count = len(refs) // 2 - 3
    for source, target in zip(refs[:count], refs[count : 2 * count]):
        target[...] = source[...]
    for index, target in enumerate(refs[2 * count :]):
        target[...] = gains_ref[index : index + 1, :].reshape(target.shape)


def hand_over(gains, *arrays):
    vmem = pl.BlockSpec(memory_space=pltpu.VMEM)
    shapes = [jax.ShapeDtypeStruct(v.shape, v.dtype) for v in arrays]
    shapes += [jax.ShapeDtypeStruct(gains.shape[1:], gains.dtype)] * 6
    return pl.pallas_call(
        hand_over_body,
        in_specs=[vmem] * (1 + len(arrays)),
        out_specs=[vmem] * len(shapes),
        out_shape=shapes,
        name="hand_over",
    )(gains, *arrays)


def exchange(value, axis, bit, size):
    return lax.ppermute(value, axis, [(i, i ^ bit) for i in range(size)])


def split_rows(array, size):
    bits = size.bit_length() - 1
    return array.reshape((2,) * bits + (array.shape[0] // size, array.shape[1]))


def body(
    tokens, images, image_counts, cotangent, norm1_gain, norm1_shift, self_qkv, self_out,
    norm2_gain, norm2_shift, cross_q, cross_kv, cross_out, norm3_gain, norm3_shift, w_up, w_down,
):
    captions, length, width = tokens.shape
    caps, slots, _ = images.shape
    side = lax.axis_index("kv")
    me = lax.axis_index("dp")
    groups = lax.axis_size("dp")
    side_arr = side.reshape(1)
    tok = tokens.reshape(captions * length, width)
    cot = cotangent.reshape(captions * length, width)
    short = -(-SHORT // 16) * 16
    valid = jnp.clip(image_counts - side * slots, 0, slots)

    qkv, att, hidden, queries = token_start(
        tok, norm1_gain, norm1_shift, self_qkv, self_out, norm2_gain,
        norm2_shift, cross_q, length,
    )

    queries = queries.reshape(caps, length, width)
    kv, part, lse_part = cross_start(valid, images, cross_kv, queries, short)
    (
        layer_out, grad_two, grads, lse, delta, up_keep, up_first, up_second, up_both, down_keep,
        down_away, cross_sum, gain3, shift3,
    ) = feed(
        part, lse_part, hidden, cot, cross_out, norm3_gain, norm3_shift, w_up, w_down, length, groups
    )
    bits = groups.bit_length() - 1
    cubes = lambda v, count: v.reshape((2,) * count + (v.shape[0] * v.shape[1] >> count, v.shape[2]))
    up_terms = [up_keep] + [
        exchange(away, "dp", flip, groups) for away, flip in ((up_first, 1), (up_second, 2), (up_both, 3))
    ]
    down_terms = [down_keep, exchange(down_away, "dp", 1 << (bits - 2), groups)]
    early = (
        [cubes(v, bits - 2) for v in up_terms], [cubes(v, bits - 1) for v in down_terms],
        cubes(cross_sum, bits),
    )

    stats = lambda v: v.reshape(caps, GROUPS, LANES)
    back, images_grad, kv_mine, kv_send = cross_back(
        valid, side_arr, kv, queries, grads.reshape(caps, length, width), stats(lse), stats(delta),
        cross_kv, images, short
    )
    cut = lambda v: split_rows(v, groups)
    *sums, gains = end(
        back, hidden, grad_two, att, qkv, tok, self_qkv, self_out, cross_q, norm1_gain, norm1_shift,
        norm2_gain, norm2_shift, gain3, shift3, early, cut(kv_mine), cut(kv_send), length, groups,
    )
    (
        tokens_grad, w_up_grad, down_grad, cross_out_grad, self_qkv_grad, self_out_grad, cross_q_grad,
        cross_kv_grad, layer_out, *gains,
    ) = hand_over(gains, *sums, layer_out)
    return (
        layer_out.reshape(captions, length, width),
        tokens_grad.reshape(captions, length, width),
        images_grad,
        gains[0], gains[1], self_qkv_grad, self_out_grad, gains[2], gains[3], cross_q_grad,
        cross_kv_grad, cross_out_grad, gains[4], gains[5], w_up_grad, down_grad,
    )


def solution(mesh):
    return jax.shard_map(
        body,
        mesh=mesh,
        in_specs=(
            P(("dp", "kv"), None, None), P("dp", "kv", None), P("dp"), P(("dp", "kv"), None, None),
        ) + (P(),) * 13,
        out_specs=(
            P(("dp", "kv"), None, None), P(("dp", "kv"), None, None), P("dp", "kv", None),
            P("kv"), P("kv"), P("dp", "kv"), P("dp", "kv"), P("kv"), P("kv"), P("dp", "kv"),
            P("dp", "kv"), P("dp", "kv"), P("kv"), P("kv"), P("dp", "kv"), P("dp", "kv"),
        ),
        check_vma=False,
    )
```

```python
import functools

import jax
import jax.numpy as jnp
from jax import lax
from jax.experimental import pallas as pl
from jax.experimental.pallas import tpu as pltpu
from jax.sharding import PartitionSpec as P

HEADS = 12
HEAD_DIM = 64
SHORT = 196
LANES = 256
PACK = LANES // HEAD_DIM
GROUPS = HEADS // PACK
SCALE = HEAD_DIM ** (-0.5)
NEG = -1e30
F32 = jnp.float32
BF16 = jnp.bfloat16
VMEM_LIMIT = 60 * 1024 * 1024
VMEM_MOST = 67043328


def dot(a, b):
    return jnp.dot(a, b, preferred_element_type=F32)


def dot_nt(a, b):
    return lax.dot_general(a, b, (((1,), (1,)), ((), ())), preferred_element_type=F32)


def dot_tn(a, b):
    return lax.dot_general(a, b, (((0,), (0,)), ((), ())), preferred_element_type=F32)


def normalize(values):
    centered = values - jnp.mean(values, axis=-1, keepdims=True)
    inverse = lax.rsqrt(jnp.mean(centered * centered, axis=-1, keepdims=True) + 1e-05)
    return centered * inverse, inverse


def norm_back(grad, gain, unit, inverse):
    scaled = grad * gain
    mean_one = jnp.mean(scaled, axis=-1, keepdims=True)
    mean_two = jnp.mean(scaled * unit, axis=-1, keepdims=True)
    return (scaled - mean_one - unit * mean_two) * inverse


def as_row(ref):
    return ref[...].reshape(1, ref.shape[0])


def iota(shape, dim):
    return lax.broadcasted_iota(jnp.int32, shape, dim)


def same_head():
    shape = (LANES, LANES)
    return (iota(shape, 0) // HEAD_DIM) == (iota(shape, 1) // HEAD_DIM)


def spread(rows, mask):
    stacked = jnp.concatenate([rows] * PACK, axis=0)
    return jnp.where(mask, stacked, jnp.zeros_like(stacked))


def gather_heads(full):
    count = full.shape[0] // PACK
    head = iota((count, LANES), 1) // HEAD_DIM
    out = full[:count]
    for index in range(1, PACK):
        out = jnp.where(head == index, full[index * count : (index + 1) * count], out)
    return out


def split_two(value):
    high = value.astype(BF16)
    return high, (value - high.astype(F32)).astype(BF16)


def lanes_to_rows(row, mask_low):
    shape = (HEAD_DIM, LANES)
    pick = iota(shape, 0) == (iota(shape, 1) % HEAD_DIM)
    high, low = split_two(jnp.where(pick, row, 0.0))
    return dot(high, mask_low) + dot(low, mask_low)


def rows_to_lanes(rows, mask_low):
    high, low = split_two(rows)
    summed = dot(high, mask_low) + dot(low, mask_low)
    shape = (HEAD_DIM, LANES)
    pick = iota(shape, 0) == (iota(shape, 1) % HEAD_DIM)
    return jnp.sum(jnp.where(pick, summed, 0.0), axis=0, keepdims=True)


def lane_slice(group):
    return slice(group * LANES, (group + 1) * LANES)


def causal_mask(length):
    shape = (length, LANES)
    return iota(shape, 0) <= (iota(shape, 1) % HEAD_DIM)


def token_start_body(
    tok_ref, gain_one, shift_one, qkv_mat, out_mat, gain_two, shift_two, query_mat,
    qkv_ref, att_ref, hidden_ref, queries_hbm, send_sem, recv_sem, store_sem, held, *, length
):
    step = pl.program_id(0)
    side = lax.axis_index("kv")
    tiles, tile, _ = held.shape

    def copies(index):
        into = queries_hbm.at[side, pl.ds(pl.multiple_of(index * tile, tile), tile)]
        return (
            pltpu.make_async_copy(held.at[index], into, store_sem.at[index]),
            pltpu.make_async_remote_copy(
                src_ref=held.at[index], dst_ref=into, send_sem=send_sem.at[index],
                recv_sem=recv_sem.at[index], device_id={"kv": 1 - side},
                device_id_type=pl.DeviceIdType.MESH,
            ),
        )

    @pl.when(step == 0)
    def _():
        barrier = pltpu.get_barrier_semaphore()
        pl.semaphore_signal(barrier, inc=1, device_id={"kv": 1 - side}, device_id_type=pl.DeviceIdType.MESH)
        pl.semaphore_wait(barrier, 1)

    x = tok_ref[...].astype(F32)
    unit, _ = normalize(x)
    normed = (unit * as_row(gain_one) + as_row(shift_one)).astype(BF16)
    width = x.shape[1]
    qkv_ref[...] = dot(normed, qkv_mat[...]).astype(BF16)
    mask = same_head()
    causal = causal_mask(length)
    for cap in range(x.shape[0] // length):
        rows = slice(cap * length, (cap + 1) * length)
        for group in range(GROUPS):
            lo = group * LANES
            query = qkv_ref[rows, lo : lo + LANES] * SCALE
            key = qkv_ref[rows, width + lo : width + lo + LANES]
            value = qkv_ref[rows, 2 * width + lo : 2 * width + lo + LANES]
            scores = jnp.where(causal, dot_nt(key, spread(query, mask)), NEG)
            exponent = jnp.exp(scores - jnp.max(scores, axis=0, keepdims=True))
            probs = exponent / jnp.sum(exponent, axis=0, keepdims=True)
            full = dot_tn(probs.astype(BF16), value)
            att_ref[rows, lo : lo + LANES] = gather_heads(full).astype(BF16)
    hidden = x + dot(att_ref[...], out_mat[...])
    hidden_ref[...] = hidden
    unit, _ = normalize(hidden)
    normed = (unit * as_row(gain_two) + as_row(shift_two)).astype(BF16)
    held[step] = (dot(normed, query_mat[...]).astype(BF16).astype(F32) * SCALE).astype(BF16)
    for copy in copies(step):
        copy.start()

    @pl.when(step == tiles - 1)
    def _():
        for index in range(tiles):
            for copy in copies(index):
                copy.wait()


def whole(shape):
    zeros = (0,) * len(shape)
    return pl.BlockSpec(shape, lambda *_: zeros)


def token_start(tokens, gain_one, shift_one, qkv_mat, out_mat, gain_two, shift_two, query_mat, length):
    rows, width = tokens.shape
    tile = min(256, rows)
    row_block = lambda cols: pl.BlockSpec((tile, cols), lambda i: (i, 0))
    return pl.pallas_call(
        functools.partial(token_start_body, length=length),
        grid=(rows // tile,),
        in_specs=[
            row_block(width), whole((width,)), whole((width,)), whole(qkv_mat.shape),
            whole(out_mat.shape), whole((width,)), whole((width,)), whole(query_mat.shape),
        ],
        out_specs=[
            row_block(3 * width), row_block(width), row_block(width), pl.BlockSpec(memory_space=pl.ANY),
        ],
        out_shape=[
            jax.ShapeDtypeStruct((rows, 3 * width), BF16),
            jax.ShapeDtypeStruct((rows, width), BF16),
            jax.ShapeDtypeStruct((rows, width), F32),
            jax.ShapeDtypeStruct((2, rows, width), BF16),
        ],
        scratch_shapes=[pltpu.SemaphoreType.DMA((rows // tile,))] * 3
        + [pltpu.VMEM((rows // tile, tile, width), BF16)],
        compiler_params=pltpu.CompilerParams(
            vmem_limit_bytes=VMEM_LIMIT, collective_id=2, has_side_effects=True
        ),
        name="token_start",
    )(tokens, gain_one, shift_one, qkv_mat, out_mat, gain_two, shift_two, query_mat)


def most(values):
    return functools.reduce(jnp.maximum, values)


def cross_start_body(valid_ref, img_ref, kv_mat, query_ref, kv_ref, att_ref, lse_ref, *, short):
    batch, slots, _ = img_ref.shape
    width = query_ref.shape[2]
    valids = [valid_ref[pl.program_id(0) * batch + cap] for cap in range(batch)]
    longest = most(valids)

    def work(count):
        mask = same_head()
        row = iota((count, LANES), 0)
        units = [(cap, group) for cap in range(batch) for group in range(GROUPS)]

        def project(unit, first):
            cap, group = unit
            lo = first + group * LANES
            columns = dot(img_ref[cap, :count], kv_mat[:, lo : lo + LANES]).astype(BF16)
            kv_ref[cap, :count, lo : lo + LANES] = columns
            return columns

        key, value = project(units[0], 0), project(units[0], width)
        for unit, later in zip(units, units[1:] + [None]):
            cap, group = unit
            lo = group * LANES
            inside = row < valids[cap]
            scores = dot_nt(key, spread(query_ref[cap, :, lo : lo + LANES], mask))
            if later:
                key = project(later, 0)
            scores = jnp.where(inside, scores, NEG)
            peak = jnp.max(scores, axis=0, keepdims=True)
            exponent = jnp.where(inside, jnp.exp(scores - peak), 0.0)
            total = jnp.maximum(jnp.sum(exponent, axis=0, keepdims=True), 1.0)
            held = value
            if later:
                value = project(later, width)
            probs = (exponent * (1.0 / total)).astype(BF16)
            att_ref[cap, :, lo : lo + LANES] = gather_heads(dot_tn(probs, held)).astype(BF16)
            lse_ref[cap, group : group + 1] = peak + jnp.log(total)

    @pl.when(longest <= 0)
    def _():
        att_ref[...] = jnp.zeros_like(att_ref)
        lse_ref[...] = jnp.full_like(lse_ref, NEG)

    if short < slots and batch <= 2:
        pl.when((longest > 0) & (longest <= short))(lambda: work(short))
        pl.when(longest > short)(lambda: work(slots))
    else:
        pl.when(longest > 0)(lambda: work(slots))


def cross_start(valid, images, kv_mat, queries, short):
    caps, slots, width = images.shape
    length = queries.shape[1]
    batch = 4 if caps % 4 == 0 else 1
    block = lambda *shape: pl.BlockSpec((batch,) + shape, lambda i, *_: (i, 0, 0))
    return pl.pallas_call(
        functools.partial(cross_start_body, short=short),
        grid_spec=pltpu.PrefetchScalarGridSpec(
            num_scalar_prefetch=1,
            grid=(caps // batch,),
            in_specs=[block(slots, width), whole(kv_mat.shape), block(length, width)],
            out_specs=[block(slots, 2 * width), block(length, width), block(GROUPS, LANES)],
        ),
        out_shape=[
            jax.ShapeDtypeStruct((caps, slots, 2 * width), BF16),
            jax.ShapeDtypeStruct((caps, length, width), BF16),
            jax.ShapeDtypeStruct((caps, GROUPS, LANES), F32),
        ],
        compiler_params=pltpu.CompilerParams(vmem_limit_bytes=VMEM_LIMIT),
        name="cross_start",
    )(valid, images, kv_mat, queries)


def feed_body(
    part_hbm, lse_hbm, hidden_ref, cot_ref, cross_mat, gain_ref, shift_ref, up_one, up_two, down_ref,
    out_ref, grad_two_ref, grads_hbm, lse_out, delta_out, up_keep, up_first, up_second, up_both,
    down_keep, down_away, cross_sum, gain_grad, shift_grad,
    send_sem, recv_sem, load_sem, att_one, att_two, lse_one, lse_two, att_full, att_low, hidden_two,
    normed_ref, acc_out, acc_grad, grad_att, lse_own, delta_own, up_pair, up_got, down_pair, down_got,
    cross_pair, cross_got, *, length, tile, bits, steps
):
    step = pl.program_id(0)
    me, side = lax.axis_index("dp"), lax.axis_index("kv")
    rows, width = hidden_ref.shape
    captions = rows // length
    tiles = rows // tile
    half = width // 2
    sub = up_one.shape[1]
    blocks = up_pair.shape[2]
    own = lambda bit: (me // (1 << bit)) % 2

    def remote(src, dst, index):
        return pltpu.make_async_remote_copy(
            src_ref=src, dst_ref=dst, send_sem=send_sem.at[index], recv_sem=recv_sem.at[index],
            device_id={"kv": 1 - side}, device_id_type=pl.DeviceIdType.MESH,
        )

    def row_span(index):
        return pl.ds(pl.multiple_of(index * tile, tile), tile)

    def chunk_copies(slot):
        return (
            remote(up_pair.at[slot, 1 - side], up_got.at[slot], 2 + slot),
            remote(down_pair.at[slot, 1 - side], down_got.at[slot], 4 + slot),
        )

    cross_copy = lambda: remote(cross_pair.at[1 - side], cross_got, 6)
    lse_copy = lambda: remote(lse_own, lse_out.at[side], 7)
    delta_copy = lambda: remote(delta_own, delta_out.at[side], 8)
    grad_copy = lambda index: remote(
        grad_att.at[pl.ds(index * tile, tile)], grads_hbm.at[side, pl.ds(index * tile, tile)], 9 + index
    )
    lse_store = lambda: pltpu.make_async_copy(lse_own, lse_out.at[side], load_sem.at[2])

    def cut(target, value):
        count, height, _ = target.shape
        if height % 16 == 0:
            target[...] = value.astype(BF16).reshape(target.shape)
        else:
            for index in range(count):
                target[index] = value[index * height : (index + 1) * height].astype(BF16)

    @pl.when(step == 0)
    def _():
        part_load = pltpu.make_async_copy(part_hbm.at[side], att_one, load_sem.at[0])
        lse_load = pltpu.make_async_copy(lse_hbm.at[side], lse_one, load_sem.at[1])
        part_load.start()
        lse_load.start()
        barrier = pltpu.get_barrier_semaphore()
        pl.semaphore_signal(barrier, inc=1, device_id={"kv": 1 - side}, device_id_type=pl.DeviceIdType.MESH)
        pl.semaphore_wait(barrier, 1)
        part_swap = remote(part_hbm.at[1 - side], att_two, 0)
        lse_swap = remote(lse_hbm.at[1 - side], lse_two, 1)
        lse_swap.start()
        part_swap.start()
        mask_low = same_head().astype(BF16)
        lse_load.wait()
        part_load.wait()
        lse_swap.wait()
        part_swap.wait()

        def one_caption(cap, carry):
            span = pl.ds(pl.multiple_of(cap * length, length), length)
            for group in range(GROUPS):
                lo = group * LANES
                first = lse_one[cap, group : group + 1]
                second = lse_two[cap, group : group + 1]
                peak = jnp.maximum(first, second)
                lse = peak + jnp.log(jnp.exp(first - peak) + jnp.exp(second - peak))
                lse_own[cap, group : group + 1] = lse
                weight_one = lanes_to_rows(jnp.exp(first - lse), mask_low)
                weight_two = lanes_to_rows(jnp.exp(second - lse), mask_low)
                mixed = (
                    weight_one * att_one[span, lo : lo + LANES].astype(F32)
                    + weight_two * att_two[span, lo : lo + LANES].astype(F32)
                )
                att_full[span, lo : lo + LANES] = mixed
                att_low[span, lo : lo + LANES] = mixed.astype(BF16)
            return carry

        lax.fori_loop(0, captions, one_caption, 0)
        lse_copy().start()
        lse_store().start()

        def one_tile(index, carry):
            span = row_span(index)
            two = hidden_ref[span, :] + dot(att_low[span, :], cross_mat[...])
            hidden_two[span, :] = two
            unit, _ = normalize(two)
            normed_ref[span, :] = (unit * as_row(gain_ref) + as_row(shift_ref)).astype(BF16)
            acc_out[span, :] = two
            acc_grad[span, :] = jnp.zeros_like(two)
            return carry

        lax.fori_loop(0, tiles, one_tile, 0)

    slot = step % 2
    up_mat = jnp.concatenate([up_one[...], up_two[...]], axis=1)
    down_mat = down_ref[...].reshape(2 * sub, width)
    pre = dot(normed_ref[...], up_mat)
    cdf = 0.5 * (1.0 + lax.erf(pre * 0.7071067811865476))
    act = (pre * cdf).astype(BF16)
    acc_out[...] += dot(act, down_mat)
    cot = cot_ref[...]
    density = jnp.exp(-0.5 * pre * pre) * 0.3989422804014327
    grad_up = (dot_nt(cot, down_mat) * (cdf + pre * density)).astype(BF16)
    acc_grad[...] += dot_nt(grad_up, up_mat)
    grad_down = dot_tn(act, cot).astype(BF16)
    grad_w = dot_tn(normed_ref[...], grad_up)
    for part in range(2):
        cut(up_pair.at[slot, part], grad_w[:, part * sub : (part + 1) * sub])
        down_pair[slot, part] = grad_down[:, part * half : (part + 1) * half].reshape(2, sub, half)

    def take(chunk, place):
        for copy in chunk_copies(place):
            copy.wait()
        cols = pl.ds(pl.multiple_of(chunk * sub, sub), sub)
        for index, target in enumerate((up_keep, up_first, up_second, up_both)):
            flip = (index % 2, index // 2)
            low_bit, high_bit = (own(b) + f - 2 * own(b) * f for b, f in zip(bits[:2], flip))
            near = high_bit * 2 + low_bit

            def one(block, carry):
                source = block * 4 + near
                target[block, :, cols] = add_low(up_pair[place, side, source], up_got[place, source])
                return carry

            lax.fori_loop(0, blocks // 4, one, 0)
        total = add_low(down_pair[place, side], down_got[place])
        span = pl.ds(pl.multiple_of(chunk % (steps // 2) * sub, sub), sub)
        stays = chunk // (steps // 2) == own(bits[-2])

        @pl.when(stays)
        def _():
            down_keep[:, span, :] = total

        @pl.when(jnp.logical_not(stays))
        def _():
            down_away[:, span, :] = total

    @pl.when(step > 0)
    def _():
        take(step - 1, (step + 1) % 2)

    for copy in chunk_copies(slot):
        copy.start()

    @pl.when(step == steps - 1)
    def _():
        mask_low = same_head().astype(BF16)
        gain_grad[...] = jnp.zeros_like(gain_grad)
        shift_grad[...] = jnp.zeros_like(shift_grad)
        for index in range(tiles):
            span = pl.ds(index * tile, tile)
            unit, inverse = normalize(hidden_two[span, :])
            grad = acc_grad[span, :]
            gain_grad[...] += jnp.sum(grad * unit, axis=0, keepdims=True)
            shift_grad[...] += jnp.sum(grad, axis=0, keepdims=True)
            two = cot_ref[span, :].astype(F32) + norm_back(grad, as_row(gain_ref), unit, inverse)
            grad_two_ref[span, :] = two
            low = two.astype(BF16)
            normed_ref[span, :] = low
            grad_att[span, :] = dot_nt(low, cross_mat[...]).astype(BF16)
            grad_copy(index).start()
        grad_store = pltpu.make_async_copy(grad_att, grads_hbm.at[side], load_sem.at[0])
        grad_store.start()

        def one_caption(cap, carry):
            span = pl.ds(pl.multiple_of(cap * length, length), length)
            for group in range(GROUPS):
                lo = group * LANES
                product = grad_att[span, lo : lo + LANES].astype(F32) * att_full[span, lo : lo + LANES]
                delta_own[cap, group : group + 1] = rows_to_lanes(product, mask_low)
            return carry

        lax.fori_loop(0, captions, one_caption, 0)
        delta_copy().start()
        delta_store = pltpu.make_async_copy(delta_own, delta_out.at[side], load_sem.at[1])
        delta_store.start()
        grad_cross = dot_tn(att_low[...], normed_ref[...])
        for part in range(2):
            cut(cross_pair.at[part], grad_cross[:, part * half : (part + 1) * half])
        cross_copy().start()
        out_ref[...] = acc_out[...].astype(BF16)
        take(steps - 1, (steps - 1) % 2)
        cross_copy().wait()

        def one(block, carry):
            cross_sum[block] = add_low(cross_pair[side, block], cross_got[block])
            return carry

        lax.fori_loop(0, blocks, one, 0)
        for copy in [lse_copy(), lse_store(), delta_copy(), delta_store, grad_store]:
            copy.wait()
        for index in range(tiles):
            grad_copy(index).wait()


def feed(part, lse_part, hidden, cot, cross_mat, gain, shift, up_mat, down_mat, length, size):
    rows, width = hidden.shape
    captions = rows // length
    units = up_mat.shape[1]
    sub = 256
    steps = units // 2 // sub
    tile = min(256, rows)
    half = width // 2
    block = width // size
    bits = list(range(size.bit_length() - 1))
    stat = (captions, GROUPS, LANES)
    sds = jax.ShapeDtypeStruct
    once = lambda shape: pl.BlockSpec(shape, lambda *_: (0,) * len(shape), pipeline_mode=pl.Buffered(1))
    hbm = pl.BlockSpec(memory_space=pl.ANY)
    copies = 9 + rows // tile
    f32_rows = lambda: pltpu.VMEM((rows, width), F32)
    low_rows = lambda: pltpu.VMEM((rows, width), BF16)
    quarter = (size // 4, block, units // 2)
    return pl.pallas_call(
        functools.partial(feed_body, length=length, tile=tile, bits=bits, steps=steps),
        grid=(steps,),
        in_specs=[
            hbm, hbm, once((rows, width)), once((rows, width)), once((width, width)),
            once((width,)), once((width,)),
            pl.BlockSpec((width, sub), lambda i: (0, i)),
            pl.BlockSpec((width, sub), lambda i: (0, i + steps)),
            pl.BlockSpec((2, sub, width), lambda i: (0, i, 0)),
        ],
        out_specs=[
            whole((rows, width)), whole((rows, width)), hbm, hbm, hbm,
            whole(quarter), whole(quarter), whole(quarter), whole(quarter),
            whole((2, units // 4, half)), whole((2, units // 4, half)),
            whole((size, block, half)), whole((1, width)), whole((1, width)),
        ],
        out_shape=[
            sds((rows, width), BF16), sds((rows, width), F32), sds((2, rows, width), BF16),
            sds((2,) + stat, F32), sds((2,) + stat, F32),
            sds(quarter, BF16), sds(quarter, BF16), sds(quarter, BF16), sds(quarter, BF16),
            sds((2, units // 4, half), BF16), sds((2, units // 4, half), BF16),
            sds((size, block, half), BF16), sds((1, width), F32), sds((1, width), F32),
        ],
        scratch_shapes=[
            pltpu.SemaphoreType.DMA((copies,)), pltpu.SemaphoreType.DMA((copies,)),
            pltpu.SemaphoreType.DMA((3,)),
            low_rows(), low_rows(), pltpu.VMEM(stat, F32), pltpu.VMEM(stat, F32), f32_rows(), low_rows(),
            f32_rows(), low_rows(), f32_rows(), f32_rows(), low_rows(),
            pltpu.VMEM(stat, F32), pltpu.VMEM(stat, F32),
            pltpu.VMEM((2, 2, size, block, sub), BF16), pltpu.VMEM((2, size, block, sub), BF16),
            pltpu.VMEM((2, 2, 2, sub, half), BF16), pltpu.VMEM((2, 2, sub, half), BF16),
            pltpu.VMEM((2, size, block, half), BF16), pltpu.VMEM((size, block, half), BF16),
        ],
        compiler_params=pltpu.CompilerParams(
            vmem_limit_bytes=VMEM_MOST, collective_id=1, has_side_effects=True
        ),
        name="feed",
    )(
        part.reshape(2, rows, width), lse_part.reshape((2,) + stat), hidden, cot, cross_mat, gain, shift,
        up_mat, up_mat, down_mat.reshape(2, units // 2, width),
    )


def cross_back_body(
    valid_ref, side_ref, kv_ref, query_ref, grad_ref, lse_ref, delta_ref, kv_mat, img_ref,
    grad_query_ref, grad_img_ref, mine_ref, send_ref, grad_kv_ref, acc_ref, *, short
):
    step = pl.program_id(0)
    batch, slots, _ = kv_ref.shape
    width = query_ref.shape[2]
    held = img_ref.shape[0]
    base = step % (held // batch) * batch
    valids = [valid_ref[step * batch + cap] for cap in range(batch)]
    longest = most(valids)

    @pl.when(step == 0)
    def _():
        acc_ref[...] = jnp.zeros_like(acc_ref)

    def work(count):
        mask = same_head()
        row = iota((count, LANES), 0)

        def image_back(cap, part):
            place = base + cap if held > batch else cap
            lo = part * LANES
            columns = dot_nt(grad_kv_ref[place, :count], kv_mat[lo : lo + LANES, :])
            grad_img_ref[cap, :count, lo : lo + LANES] = columns.astype(BF16)

        for cap, valid in enumerate(valids):
            place = base + cap if held > batch else cap
            inside = row < valid
            for group in range(GROUPS):
                lo = group * LANES
                key = kv_ref[cap, :count, lo : lo + LANES]
                value = kv_ref[cap, :count, width + lo : width + lo + LANES]
                query = spread(query_ref[cap, :, lo : lo + LANES], mask)
                grad = spread(grad_ref[cap, :, lo : lo + LANES], mask)
                scores = dot_nt(key, query)
                probs = jnp.where(inside, jnp.exp(scores - lse_ref[cap, group : group + 1]), 0.0)
                grad_probs = dot_nt(value, grad)
                if cap > 0:
                    image_back(cap - 1, group)
                grad_scores = (probs * (grad_probs - delta_ref[cap, group : group + 1])).astype(BF16)
                back = gather_heads(dot_tn(grad_scores, key)) * SCALE
                grad_query_ref[cap, :, lo : lo + LANES] = back.astype(BF16)
                grad_kv_ref[place, :count, lo : lo + LANES] = dot(grad_scores, query).astype(BF16)
                grad_kv_ref[place, :count, width + lo : width + lo + LANES] = dot(
                    probs.astype(BF16), grad
                ).astype(BF16)
            if count < slots:
                grad_kv_ref[place, count:] = jnp.zeros((slots - count, 2 * width), BF16)
                grad_img_ref[cap, count:] = jnp.zeros((slots - count, width), BF16)
        for group in range(GROUPS):
            image_back(batch - 1, group)

    @pl.when(longest <= 0)
    def _():
        grad_query_ref[...] = jnp.zeros_like(grad_query_ref)
        for cap in range(batch):
            grad_kv_ref[base + cap] = jnp.zeros((slots, 2 * width), BF16)
        grad_img_ref[...] = jnp.zeros_like(grad_img_ref)

    if short < slots and batch <= 2:
        pl.when((longest > 0) & (longest <= short))(lambda: work(short))
        pl.when(longest > short)(lambda: work(slots))
    else:
        pl.when(longest > 0)(lambda: work(slots))

    @pl.when(base == held - batch)
    def _():
        left = img_ref[...].reshape(held * slots, width)
        right = grad_kv_ref[...].reshape(held * slots, 2 * width)
        acc_ref[...] += dot_tn(left, right)

    @pl.when(step == pl.num_programs(0) - 1)
    def _():
        side = side_ref[0]
        own = pl.ds(pl.multiple_of(side * width, width), width)
        other = pl.ds(pl.multiple_of((1 - side) * width, width), width)
        mine_ref[...] = acc_ref[:, own].astype(BF16)
        send_ref[...] = acc_ref[:, other].astype(BF16)


def cross_back(valid, side, kv, queries, grads, lse, delta, kv_mat, images, short):
    caps, slots, double = kv.shape
    width = double // 2
    length = queries.shape[1]
    held = 4 if caps % 4 == 0 else 1
    batch = min(4, held)
    block = lambda *shape: pl.BlockSpec((batch,) + shape, lambda i, *_: (i, 0, 0))
    sds = jax.ShapeDtypeStruct
    return pl.pallas_call(
        functools.partial(cross_back_body, short=short),
        grid_spec=pltpu.PrefetchScalarGridSpec(
            num_scalar_prefetch=2,
            grid=(caps // batch,),
            in_specs=[
                block(slots, double), block(length, width), block(length, width),
                block(GROUPS, LANES), block(GROUPS, LANES), whole(kv_mat.shape),
                pl.BlockSpec((held, slots, width), lambda i, *_: (i // (held // batch), 0, 0)),
            ],
            out_specs=[
                block(length, width), block(slots, width), whole((width, width)), whole((width, width)),
            ],
            scratch_shapes=[
                pltpu.VMEM((held, slots, double), BF16), pltpu.VMEM((width, double), F32),
            ],
        ),
        out_shape=[
            sds((caps, length, width), BF16), sds((caps, slots, width), BF16),
            sds((width, width), BF16), sds((width, width), BF16),
        ],
        compiler_params=pltpu.CompilerParams(vmem_limit_bytes=VMEM_LIMIT),
        name="cross_back",
    )(valid, side, kv, queries, grads, lse, delta, kv_mat, images)


def add_low(first, second):
    return first + second


def cut_blocks(target, value):
    height = target.shape[-2]
    count = len(target.shape) - 2
    if height % 16 == 0:
        target[...] = value.astype(BF16).reshape(target.shape)
    else:
        for i in range(1 << count):
            lead = tuple((i >> (count - 1 - d)) % 2 for d in range(count))
            target[lead] = value[i * height : (i + 1) * height].astype(BF16)


class Piece:
    def __init__(self, sums, source, out, col, width, bits, order, recvs, mine=None, send=None, kv_recv=None):
        self.sums, self.out, self.col, self.width = sums, out, col, width
        self.bits, self.order, self.recvs = list(bits), list(order), recvs
        self.mine, self.send, self.kv_recv = mine, send, kv_recv
        self.now, self.holds, self.pending = 0, source, None

    def columns(self, ref):
        return (slice(None), pl.ds(self.col, self.width) if ref.shape[-1] != self.width else slice(None))

    def start_kv(self):
        whole_lead = (slice(None),) * len(self.bits)
        self.pending = self.sums.copy(
            self.send.at[whole_lead + self.columns(self.send)], self.kv_recv, {"kv": 1 - self.sums.side}
        )
        self.pending.start()

    def start(self):
        bit = self.order[self.now]
        lead = tuple(1 - self.sums.own(bit) if b == bit else slice(None) for b in self.bits)
        self.pending = self.sums.copy(
            self.holds.at[lead + self.columns(self.holds)], self.recvs[self.now], self.sums.partner(bit)
        )
        self.pending.start()

    def add(self, kept, arrived, cols, left, fixed):
        def one(i, carry):
            inner = {b: (i // (1 << (len(left) - 1 - d))) % 2 for d, b in enumerate(left)}
            lead = tuple(inner[b] if b in inner else fixed[b] for b in self.bits)
            into = tuple(inner[b] for b in left)
            arrived[into] = add_low(kept[lead + cols], arrived[into])
            return carry

        lax.fori_loop(0, 1 << len(left), one, 0)

    def advance(self):
        if self.pending is None:
            return True
        self.pending.wait()
        self.pending = None
        if self.holds is None:
            self.add(self.mine, self.kv_recv, self.columns(self.mine), self.bits, {})
            self.holds = self.kv_recv
            self.start()
            return False
        bit = self.order[self.now]
        arrived, cols = self.recvs[self.now], self.columns(self.holds)
        left = [b for b in self.bits if b != bit]
        if not left:
            total = self.holds[(self.sums.own(bit),) + cols].astype(F32) + arrived[...].astype(F32)
            self.out[:, self.col : self.col + self.width] = total
            return True
        self.add(self.holds, arrived, cols, left, {bit: self.sums.own(bit)})
        self.bits, self.holds, self.now = left, arrived, self.now + 1
        self.start()
        return False


class Sums:
    def __init__(self, send_sem, recv_sem):
        self.send_sem, self.recv_sem, self.count = send_sem, recv_sem, 0
        self.me, self.side = lax.axis_index("dp"), lax.axis_index("kv")

    def own(self, bit):
        return (self.me // (1 << bit)) % 2

    def partner(self, bit):
        return {"dp": self.me + (1 - 2 * self.own(bit)) * (1 << bit)}

    def copy(self, src, dst, device):
        index = self.count
        self.count += 1
        return pltpu.make_async_remote_copy(
            src_ref=src, dst_ref=dst, send_sem=self.send_sem.at[index], recv_sem=self.recv_sem.at[index],
            device_id=device, device_id_type=pl.DeviceIdType.MESH,
        )

    def greet(self, bits):
        barrier = pltpu.get_barrier_semaphore()
        for device in [{"kv": 1 - self.side}] + [self.partner(bit) for bit in bits]:
            pl.semaphore_signal(barrier, inc=1, device_id=device, device_id_type=pl.DeviceIdType.MESH)
        pl.semaphore_wait(barrier, 1 + len(bits))


def turned(bits, by):
    first = bits[:-1]
    by %= len(first)
    return first[by:] + first[:by] + bits[-1:]


def end_body(
    back_hbm, hidden_hbm, grad_two_hbm, att_hbm, qkv_hbm, tok_hbm, qkv_mat_hbm, out_mat_hbm, query_mat_hbm,
    gain_one, shift_one, gain_two, shift_two, gain_three, shift_three,
    up_keep, up_first, up_second, up_both, down_keep, down_away, cross_ref, kv_mine, kv_send,
    grad_tok, up_out, down_out, cross_out, qkv_out, out_out, query_out, kv_out, gains_out,
    *scratch, plan, bits, length, tile
):
    scratch = list(scratch)
    (
        send_sem, recv_sem, load_sem, back_one, back_two, hidden, grad_two, att, qkv, tok, qkv_mat,
        out_mat, query_mat, back_sum, normed, low, grad_att, grad_qkv, gains_all, gain_kv,
        gain_buf, gain_recv, qkv_mine, qkv_send, out_mine, out_send, query_mine, query_send,
        up_ref, down_ref,
    ) = scratch[:30]
    rest = scratch[30:]
    sums = Sums(send_sem, recv_sem)
    side = sums.side
    captions = back_one.shape[0]
    rows, width = hidden.shape
    half = width // 2
    named = dict(
        up=(up_ref, None, None, up_out), down=(down_ref, None, None, down_out),
        cross=(cross_ref, None, None, cross_out), qkv=(None, qkv_mine, qkv_send, qkv_out),
        out=(None, out_mine, out_send, out_out), query=(None, query_mine, query_send, query_out),
        kv=(None, kv_mine, kv_send, kv_out),
    )
    pieces = {}
    for name, col, cols, axes, order, kv in plan:
        source, mine, send, out = named[name]
        kv_recv = rest.pop(0) if kv else None
        recvs = [rest.pop(0) for _ in order]
        pieces.setdefault(name, []).append(
            Piece(sums, source, out, col, cols, axes, order, recvs, mine, send, kv_recv)
        )
    early = pieces["up"] + pieces["down"] + pieces["cross"]
    image = pieces["kv"]
    middle = pieces["query"] + pieces["out"]
    late = pieces["qkv"]

    own_caps = pl.ds(pl.multiple_of(side * captions, captions), captions)
    other_caps = pl.ds(pl.multiple_of((1 - side) * captions, captions), captions)
    pairs = [
        (back_hbm.at[own_caps], back_one), (hidden_hbm, hidden), (query_mat_hbm, query_mat),
        (grad_two_hbm, grad_two), (out_mat_hbm, out_mat), (att_hbm, att), (qkv_hbm, qkv),
        (tok_hbm, tok), (qkv_mat_hbm, qkv_mat),
    ]
    loads = [pltpu.make_async_copy(src, dst, load_sem.at[i]) for i, (src, dst) in enumerate(pairs)]
    for load in loads:
        load.start()
    sums.greet(bits)
    swap = sums.copy(back_hbm.at[other_caps], back_two, {"kv": 1 - side})
    swap.start()
    for piece in image:
        piece.start_kv()

    def sum_terms(target, terms):
        count = len(target.shape) - 2

        def one(i, carry):
            lead = tuple((i // (1 << (count - 1 - d))) % 2 for d in range(count))
            total = terms[0][lead].astype(F32)
            for term in terms[1:]:
                total += term[lead].astype(F32)
            target[lead] = total.astype(BF16)
            return carry

        lax.fori_loop(0, 1 << count, one, 0)

    sum_terms(up_ref, (up_keep, up_first, up_second, up_both))
    sum_terms(down_ref, (down_keep, down_away))
    for piece in early:
        piece.start()
    gains_all[...] = jnp.zeros_like(gains_all)
    gains_all[4:5] = gain_three[...]
    gains_all[5:6] = shift_three[...]
    for load in loads[:5]:
        load.wait()
    swap.wait()

    def rows_at(index):
        return pl.ds(pl.multiple_of(index * tile, tile), tile)

    def query_back(index, carry):
        span = rows_at(index)
        caps = pl.ds(index * (tile // length), tile // length)
        back = add_low(back_one[caps], back_two[caps]).reshape(tile, width)
        back_sum[span, :] = back
        unit, inverse = normalize(hidden[span, :])
        normed[span, :] = (unit * as_row(gain_two) + as_row(shift_two)).astype(BF16)
        grad = dot_nt(back, query_mat[...])
        gains_all[2:3] += jnp.sum(grad * unit, axis=0, keepdims=True)
        gains_all[3:4] += jnp.sum(grad, axis=0, keepdims=True)
        grad_one = grad_two[span, :] + norm_back(grad, as_row(gain_two), unit, inverse)
        grad_two[span, :] = grad_one
        low[span, :] = grad_one.astype(BF16)
        grad_att[span, :] = dot_nt(grad_one.astype(BF16), out_mat[...]).astype(BF16)
        return carry

    lax.fori_loop(0, rows // tile, query_back, 0)
    for piece in image:
        piece.advance()

    def weight(left, right, target, which):
        cols = target.shape[-1]
        start = pl.multiple_of(which * cols, 128)
        cut_blocks(target, dot_tn(left[...], right[:, pl.ds(start, cols)]))

    def weights(left, right, mine, send, group):
        weight(left, right, send, 1 - side)
        for piece in group:
            piece.start_kv()
        weight(left, right, mine, side)

    weights(normed, back_sum, query_mine, query_send, pieces["query"])
    loads[5].wait()
    loads[6].wait()
    weights(att, low, out_mine, out_send, pieces["out"])
    for piece in middle + pieces["cross"] + pieces["up"]:
        piece.advance()

    mask = same_head()
    causal = causal_mask(length)

    def attend(cap):
        span = pl.ds(pl.multiple_of(cap * length, length), length)
        for group in range(GROUPS):
            lo = group * LANES
            query = spread(qkv[span, lo : lo + LANES] * SCALE, mask)
            key = qkv[span, width + lo : width + lo + LANES]
            value = qkv[span, 2 * width + lo : 2 * width + lo + LANES]
            cot = spread(grad_att[span, lo : lo + LANES], mask)
            scores = jnp.where(causal, dot_nt(key, query), NEG)
            exponent = jnp.exp(scores - jnp.max(scores, axis=0, keepdims=True))
            probs = exponent / jnp.sum(exponent, axis=0, keepdims=True)
            grad_probs = dot_nt(value, cot)
            mean = jnp.sum(probs * grad_probs, axis=0, keepdims=True)
            grad_scores = (probs * (grad_probs - mean)).astype(BF16)
            grad_q = gather_heads(dot_tn(grad_scores, key)) * SCALE
            grad_qkv[span, lo : lo + LANES] = grad_q.astype(BF16)
            grad_qkv[span, width + lo : width + lo + LANES] = dot(grad_scores, query).astype(BF16)
            grad_qkv[span, 2 * width + lo : 2 * width + lo + LANES] = dot(
                probs.astype(BF16), cot
            ).astype(BF16)

    together = 2 if captions % 2 == 0 else 1

    def attend_some(index, carry):
        for cap in range(together):
            attend(index * together + cap)
        return carry

    rounds = captions // together
    lax.fori_loop(0, rounds // 2, attend_some, 0)
    for piece in image + pieces["down"]:
        piece.advance()
    lax.fori_loop(rounds // 2, rounds, attend_some, 0)
    for piece in early + image + middle:
        piece.advance()
    loads[7].wait()
    loads[8].wait()

    def token_norm(index, carry):
        span = rows_at(index)
        unit, _ = normalize(tok[span, :].astype(F32))
        normed[span, :] = (unit * as_row(gain_one) + as_row(shift_one)).astype(BF16)
        return carry

    lax.fori_loop(0, rows // tile, token_norm, 0)
    weights(normed, grad_qkv, qkv_mine, qkv_send, late)
    for piece in late + early + middle + image:
        piece.advance()

    def token_back(index, carry):
        span = rows_at(index)
        unit, inverse = normalize(tok[span, :].astype(F32))
        grad = dot_nt(grad_qkv[span, :], qkv_mat[...])
        gains_all[0:1] += jnp.sum(grad * unit, axis=0, keepdims=True)
        gains_all[1:2] += jnp.sum(grad, axis=0, keepdims=True)
        back = grad_two[span, :] + norm_back(grad, as_row(gain_one), unit, inverse)
        grad_tok[span, :] = back.astype(BF16)
        return carry

    lax.fori_loop(0, rows // tile, token_back, 0)
    own_cols = pl.ds(pl.multiple_of(side * half, 128), half)
    other_cols = pl.ds(pl.multiple_of((1 - side) * half, 128), half)
    gain_copy = sums.copy(gains_all.at[:, other_cols], gain_kv, {"kv": 1 - side})
    gain_copy.start()
    stage = -1
    everything = late + early + image + middle
    while stage < len(bits) or not all(piece.pending is None for piece in everything):
        if stage < len(bits):
            gain_copy.wait()
            if stage < 0:
                gain_buf[0] = gains_all[:, own_cols] + gain_kv[...]
            else:
                gain_buf[stage + 1] = gain_buf[stage] + gain_recv[stage]
            stage += 1
            if stage < len(bits):
                gain_copy = sums.copy(gain_buf.at[stage], gain_recv.at[stage], sums.partner(bits[stage]))
                gain_copy.start()
            else:
                gains_out[...] = gain_buf[stage]
        for piece in everything:
            piece.advance()


def end(
    back, hidden, grad_two, att, qkv, tokens, qkv_mat, out_mat, query_mat, gain_one, shift_one,
    gain_two, shift_two, gain_three, shift_three, early, kv_mine, kv_send, length, size
):
    bits = list(range(size.bit_length() - 1))
    axes = bits[::-1]
    rows, width = hidden.shape
    captions = rows // length
    tile = min(256, rows)
    block = width // size
    lead = (2,) * len(bits)
    up_terms, down_terms, cross = early
    up, down = up_terms[0], down_terms[0]
    third = width // 3
    plan = [("up", 0, up.shape[-1], axes[:-2], bits[2:], False)]
    down_axes = axes[:1] + axes[2:]
    plan.append(("down", 0, down.shape[-1], down_axes, [b for b in bits if b in down_axes], False))
    plan.append(("cross", 0, cross.shape[-1], axes, bits[1:2] + bits[:1] + bits[2:], False))
    plan.append(("query", 0, width // 2, axes, turned(bits, 0), True))
    plan.append(("out", 0, width // 2, axes, turned(bits, 1), True))
    for by in range(3):
        plan.append(("kv", by * third, third, axes, turned(bits, by), True))
    for by in range(3):
        plan.append(("qkv", by * (width // 2), width // 2, axes, turned(bits, by), True))
    heights = dict(up=up.shape[-2], down=down.shape[-2], cross=cross.shape[-2])
    buffers = []
    copies = 2 + len(bits)
    for name, col, cols, piece_axes, order, kv in plan:
        shape = (heights.get(name, block), cols)
        for count in range(len(order) if kv else len(order) - 1, -1, -1):
            buffers.append(pltpu.VMEM((2,) * count + shape, BF16))
            copies += 1
    vmem = pl.BlockSpec(memory_space=pltpu.VMEM)
    hbm = pl.BlockSpec(memory_space=pl.ANY)
    sds = jax.ShapeDtypeStruct
    cut = lambda cols: pltpu.VMEM(lead + (block, cols), BF16)
    outs = [sds((rows, width), BF16)]
    outs += [sds(v.shape[-2:], F32) for v in (up, down, cross)]
    outs += [sds((block, cols), F32) for cols in (3 * width // 2, width // 2, width // 2, width)]
    outs += [sds((8, width // 2), F32)]
    low_rows = lambda cols: pltpu.VMEM((rows, cols), BF16)
    return pl.pallas_call(
        functools.partial(end_body, plan=plan, bits=bits, length=length, tile=tile),
        in_specs=[hbm] * 9 + [vmem] * 6 + [vmem] * 8 + [hbm],
        out_specs=[vmem] * len(outs),
        out_shape=outs,
        scratch_shapes=[
            pltpu.SemaphoreType.DMA((copies,)), pltpu.SemaphoreType.DMA((copies,)),
            pltpu.SemaphoreType.DMA((9,)),
            pltpu.VMEM((captions, length, width), BF16), pltpu.VMEM((captions, length, width), BF16),
            pltpu.VMEM((rows, width), F32), pltpu.VMEM((rows, width), F32), low_rows(width),
            low_rows(3 * width), low_rows(width), pltpu.VMEM(qkv_mat.shape, BF16),
            pltpu.VMEM(out_mat.shape, BF16), pltpu.VMEM(query_mat.shape, BF16),
            low_rows(width), low_rows(width), low_rows(width), low_rows(width), low_rows(3 * width),
            pltpu.VMEM((8, width), F32),
            pltpu.VMEM((8, width // 2), F32), pltpu.VMEM((len(bits) + 1, 8, width // 2), F32),
            pltpu.VMEM((len(bits), 8, width // 2), F32),
            cut(3 * width // 2), cut(3 * width // 2), cut(width // 2), cut(width // 2),
            cut(width // 2), cut(width // 2), pltpu.VMEM(up.shape, BF16), pltpu.VMEM(down.shape, BF16),
        ] + buffers,
        compiler_params=pltpu.CompilerParams(
            vmem_limit_bytes=VMEM_MOST, collective_id=0, has_side_effects=True
        ),
        name="end",
    )(
        back, hidden, grad_two, att, qkv, tokens, qkv_mat, out_mat, query_mat, gain_one, shift_one,
        gain_two, shift_two, gain_three, shift_three, *up_terms, *down_terms, cross, kv_mine, kv_send,
    )


def hand_over_body(gains_ref, *refs):
    count = len(refs) // 2 - 3
    for source, target in zip(refs[:count], refs[count : 2 * count]):
        target[...] = source[...]
    for index, target in enumerate(refs[2 * count :]):
        target[...] = gains_ref[index : index + 1, :].reshape(target.shape)


def hand_over(gains, *arrays):
    vmem = pl.BlockSpec(memory_space=pltpu.VMEM)
    shapes = [jax.ShapeDtypeStruct(v.shape, v.dtype) for v in arrays]
    shapes += [jax.ShapeDtypeStruct(gains.shape[1:], gains.dtype)] * 6
    return pl.pallas_call(
        hand_over_body,
        in_specs=[vmem] * (1 + len(arrays)),
        out_specs=[vmem] * len(shapes),
        out_shape=shapes,
        name="hand_over",
    )(gains, *arrays)


def exchange(value, axis, bit, size):
    return lax.ppermute(value, axis, [(i, i ^ bit) for i in range(size)])


def split_rows(array, size):
    bits = size.bit_length() - 1
    return array.reshape((2,) * bits + (array.shape[0] // size, array.shape[1]))


def body(
    tokens, images, image_counts, cotangent, norm1_gain, norm1_shift, self_qkv, self_out,
    norm2_gain, norm2_shift, cross_q, cross_kv, cross_out, norm3_gain, norm3_shift, w_up, w_down,
):
    captions, length, width = tokens.shape
    caps, slots, _ = images.shape
    side = lax.axis_index("kv")
    me = lax.axis_index("dp")
    groups = lax.axis_size("dp")
    side_arr = side.reshape(1)
    tok = tokens.reshape(captions * length, width)
    cot = cotangent.reshape(captions * length, width)
    short = -(-SHORT // 16) * 16
    valid = jnp.clip(image_counts - side * slots, 0, slots)

    qkv, att, hidden, queries = token_start(
        tok, norm1_gain, norm1_shift, self_qkv, self_out, norm2_gain,
        norm2_shift, cross_q, length,
    )

    queries = queries.reshape(caps, length, width)
    kv, part, lse_part = cross_start(valid, images, cross_kv, queries, short)
    (
        layer_out, grad_two, grads, lse, delta, up_keep, up_first, up_second, up_both, down_keep,
        down_away, cross_sum, gain3, shift3,
    ) = feed(
        part, lse_part, hidden, cot, cross_out, norm3_gain, norm3_shift, w_up, w_down, length, groups
    )
    bits = groups.bit_length() - 1
    cubes = lambda v, count: v.reshape((2,) * count + (v.shape[0] * v.shape[1] >> count, v.shape[2]))
    up_terms = [up_keep] + [
        exchange(away, "dp", flip, groups) for away, flip in ((up_first, 1), (up_second, 2), (up_both, 3))
    ]
    down_terms = [down_keep, exchange(down_away, "dp", 1 << (bits - 2), groups)]
    early = (
        [cubes(v, bits - 2) for v in up_terms], [cubes(v, bits - 1) for v in down_terms],
        cubes(cross_sum, bits),
    )

    stats = lambda v: v.reshape(caps, GROUPS, LANES)
    back, images_grad, kv_mine, kv_send = cross_back(
        valid, side_arr, kv, queries, grads.reshape(caps, length, width), stats(lse), stats(delta),
        cross_kv, images, short
    )
    cut = lambda v: split_rows(v, groups)
    *sums, gains = end(
        back, hidden, grad_two, att, qkv, tok, self_qkv, self_out, cross_q, norm1_gain, norm1_shift,
        norm2_gain, norm2_shift, gain3, shift3, early, cut(kv_mine), cut(kv_send), length, groups,
    )
    (
        tokens_grad, w_up_grad, down_grad, cross_out_grad, self_qkv_grad, self_out_grad, cross_q_grad,
        cross_kv_grad, layer_out, *gains,
    ) = hand_over(gains, *sums, layer_out)
    return (
        layer_out.reshape(captions, length, width),
        tokens_grad.reshape(captions, length, width),
        images_grad,
        gains[0], gains[1], self_qkv_grad, self_out_grad, gains[2], gains[3], cross_q_grad,
        cross_kv_grad, cross_out_grad, gains[4], gains[5], w_up_grad, down_grad,
    )


def solution(mesh):
    return jax.shard_map(
        body,
        mesh=mesh,
        in_specs=(
            P(("dp", "kv"), None, None), P("dp", "kv", None), P("dp"), P(("dp", "kv"), None, None),
        ) + (P(),) * 13,
        out_specs=(
            P(("dp", "kv"), None, None), P(("dp", "kv"), None, None), P("dp", "kv", None),
            P("kv"), P("kv"), P("dp", "kv"), P("dp", "kv"), P("kv"), P("kv"), P("dp", "kv"),
            P("dp", "kv"), P("dp", "kv"), P("kv"), P("kv"), P("dp", "kv"), P("dp", "kv"),
        ),
        check_vma=False,
    )
```

```python
import functools

import jax
import jax.numpy as jnp
from jax import lax
from jax.experimental import pallas as pl
from jax.experimental.pallas import tpu as pltpu
from jax.sharding import PartitionSpec as P

HEADS = 12
HEAD_DIM = 64
SHORT = 196
LANES = 256
PACK = LANES // HEAD_DIM
GROUPS = HEADS // PACK
SCALE = HEAD_DIM ** (-0.5)
NEG = -1e30
F32 = jnp.float32
BF16 = jnp.bfloat16
VMEM_LIMIT = 60 * 1024 * 1024
VMEM_MOST = 67043328


def dot(a, b):
    return jnp.dot(a, b, preferred_element_type=F32)


def dot_nt(a, b):
    return lax.dot_general(a, b, (((1,), (1,)), ((), ())), preferred_element_type=F32)


def dot_tn(a, b):
    return lax.dot_general(a, b, (((0,), (0,)), ((), ())), preferred_element_type=F32)


def normalize(values):
    centered = values - jnp.mean(values, axis=-1, keepdims=True)
    inverse = lax.rsqrt(jnp.mean(centered * centered, axis=-1, keepdims=True) + 1e-05)
    return centered * inverse, inverse


def norm_back(grad, gain, unit, inverse):
    scaled = grad * gain
    mean_one = jnp.mean(scaled, axis=-1, keepdims=True)
    mean_two = jnp.mean(scaled * unit, axis=-1, keepdims=True)
    return (scaled - mean_one - unit * mean_two) * inverse


def as_row(ref):
    return ref[...].reshape(1, ref.shape[0])


def iota(shape, dim):
    return lax.broadcasted_iota(jnp.int32, shape, dim)


def same_head():
    shape = (LANES, LANES)
    return (iota(shape, 0) // HEAD_DIM) == (iota(shape, 1) // HEAD_DIM)


def spread(rows, mask):
    stacked = jnp.concatenate([rows] * PACK, axis=0)
    return jnp.where(mask, stacked, jnp.zeros_like(stacked))


def gather_heads(full):
    count = full.shape[0] // PACK
    head = iota((count, LANES), 1) // HEAD_DIM
    out = full[:count]
    for index in range(1, PACK):
        out = jnp.where(head == index, full[index * count : (index + 1) * count], out)
    return out


def split_two(value):
    high = value.astype(BF16)
    return high, (value - high.astype(F32)).astype(BF16)


def lanes_to_rows(row, mask_low):
    shape = (HEAD_DIM, LANES)
    pick = iota(shape, 0) == (iota(shape, 1) % HEAD_DIM)
    high, low = split_two(jnp.where(pick, row, 0.0))
    return dot(high, mask_low) + dot(low, mask_low)


def rows_to_lanes(rows, mask_low):
    high, low = split_two(rows)
    summed = dot(high, mask_low) + dot(low, mask_low)
    shape = (HEAD_DIM, LANES)
    pick = iota(shape, 0) == (iota(shape, 1) % HEAD_DIM)
    return jnp.sum(jnp.where(pick, summed, 0.0), axis=0, keepdims=True)


def lane_slice(group):
    return slice(group * LANES, (group + 1) * LANES)


def causal_mask(length):
    shape = (length, LANES)
    return iota(shape, 0) <= (iota(shape, 1) % HEAD_DIM)


def token_start_body(
    tok_ref, gain_one, shift_one, qkv_mat, out_mat, gain_two, shift_two, query_mat,
    qkv_ref, att_ref, hidden_ref, queries_hbm, send_sem, recv_sem, store_sem, held, *, length
):
    step = pl.program_id(0)
    side = lax.axis_index("kv")
    tiles, tile, _ = held.shape

    def copies(index):
        into = queries_hbm.at[side, pl.ds(pl.multiple_of(index * tile, tile), tile)]
        return (
            pltpu.make_async_copy(held.at[index], into, store_sem.at[index]),
            pltpu.make_async_remote_copy(
                src_ref=held.at[index], dst_ref=into, send_sem=send_sem.at[index],
                recv_sem=recv_sem.at[index], device_id={"kv": 1 - side},
                device_id_type=pl.DeviceIdType.MESH,
            ),
        )

    @pl.when(step == 0)
    def _():
        barrier = pltpu.get_barrier_semaphore()
        pl.semaphore_signal(barrier, inc=1, device_id={"kv": 1 - side}, device_id_type=pl.DeviceIdType.MESH)
        pl.semaphore_wait(barrier, 1)

    x = tok_ref[...].astype(F32)
    unit, _ = normalize(x)
    normed = (unit * as_row(gain_one) + as_row(shift_one)).astype(BF16)
    width = x.shape[1]
    qkv_ref[...] = dot(normed, qkv_mat[...]).astype(BF16)
    mask = same_head()
    causal = causal_mask(length)
    for cap in range(x.shape[0] // length):
        rows = slice(cap * length, (cap + 1) * length)
        for group in range(GROUPS):
            lo = group * LANES
            query = qkv_ref[rows, lo : lo + LANES] * SCALE
            key = qkv_ref[rows, width + lo : width + lo + LANES]
            value = qkv_ref[rows, 2 * width + lo : 2 * width + lo + LANES]
            scores = jnp.where(causal, dot_nt(key, spread(query, mask)), NEG)
            exponent = jnp.exp(scores - jnp.max(scores, axis=0, keepdims=True))
            probs = exponent / jnp.sum(exponent, axis=0, keepdims=True)
            full = dot_tn(probs.astype(BF16), value)
            att_ref[rows, lo : lo + LANES] = gather_heads(full).astype(BF16)
    hidden = x + dot(att_ref[...], out_mat[...])
    hidden_ref[...] = hidden
    unit, _ = normalize(hidden)
    normed = (unit * as_row(gain_two) + as_row(shift_two)).astype(BF16)
    held[step] = (dot(normed, query_mat[...]).astype(BF16).astype(F32) * SCALE).astype(BF16)
    for copy in copies(step):
        copy.start()

    @pl.when(step == tiles - 1)
    def _():
        for index in range(tiles):
            for copy in copies(index):
                copy.wait()


def whole(shape):
    zeros = (0,) * len(shape)
    return pl.BlockSpec(shape, lambda *_: zeros)


def token_start(tokens, gain_one, shift_one, qkv_mat, out_mat, gain_two, shift_two, query_mat, length):
    rows, width = tokens.shape
    tile = min(256, rows)
    row_block = lambda cols: pl.BlockSpec((tile, cols), lambda i: (i, 0))
    return pl.pallas_call(
        functools.partial(token_start_body, length=length),
        grid=(rows // tile,),
        in_specs=[
            row_block(width), whole((width,)), whole((width,)), whole(qkv_mat.shape),
            whole(out_mat.shape), whole((width,)), whole((width,)), whole(query_mat.shape),
        ],
        out_specs=[
            row_block(3 * width), row_block(width), row_block(width), pl.BlockSpec(memory_space=pl.ANY),
        ],
        out_shape=[
            jax.ShapeDtypeStruct((rows, 3 * width), BF16),
            jax.ShapeDtypeStruct((rows, width), BF16),
            jax.ShapeDtypeStruct((rows, width), F32),
            jax.ShapeDtypeStruct((2, rows, width), BF16),
        ],
        scratch_shapes=[pltpu.SemaphoreType.DMA((rows // tile,))] * 3
        + [pltpu.VMEM((rows // tile, tile, width), BF16)],
        compiler_params=pltpu.CompilerParams(
            vmem_limit_bytes=VMEM_LIMIT, collective_id=2, has_side_effects=True
        ),
        name="token_start",
    )(tokens, gain_one, shift_one, qkv_mat, out_mat, gain_two, shift_two, query_mat)


def most(values):
    return functools.reduce(jnp.maximum, values)


def cross_start_body(valid_ref, img_ref, kv_mat, query_ref, kv_ref, att_ref, lse_ref, *, short):
    batch, slots, _ = img_ref.shape
    width = query_ref.shape[2]
    valids = [valid_ref[pl.program_id(0) * batch + cap] for cap in range(batch)]
    longest = most(valids)

    def work(count):
        mask = same_head()
        row = iota((count, LANES), 0)
        units = [(cap, group) for cap in range(batch) for group in range(GROUPS)]

        def project(unit, first):
            cap, group = unit
            lo = first + group * LANES
            columns = dot(img_ref[cap, :count], kv_mat[:, lo : lo + LANES]).astype(BF16)
            kv_ref[cap, :count, lo : lo + LANES] = columns
            return columns

        key, value = project(units[0], 0), project(units[0], width)
        for unit, later in zip(units, units[1:] + [None]):
            cap, group = unit
            lo = group * LANES
            inside = row < valids[cap]
            scores = dot_nt(key, spread(query_ref[cap, :, lo : lo + LANES], mask))
            if later:
                key = project(later, 0)
            scores = jnp.where(inside, scores, NEG)
            peak = jnp.max(scores, axis=0, keepdims=True)
            exponent = jnp.where(inside, jnp.exp(scores - peak), 0.0)
            total = jnp.maximum(jnp.sum(exponent, axis=0, keepdims=True), 1.0)
            held = value
            if later:
                value = project(later, width)
            probs = (exponent * (1.0 / total)).astype(BF16)
            att_ref[cap, :, lo : lo + LANES] = gather_heads(dot_tn(probs, held)).astype(BF16)
            lse_ref[cap, group : group + 1] = peak + jnp.log(total)

    @pl.when(longest <= 0)
    def _():
        att_ref[...] = jnp.zeros_like(att_ref)
        lse_ref[...] = jnp.full_like(lse_ref, NEG)

    if short < slots and batch <= 2:
        pl.when((longest > 0) & (longest <= short))(lambda: work(short))
        pl.when(longest > short)(lambda: work(slots))
    else:
        pl.when(longest > 0)(lambda: work(slots))


def cross_start(valid, images, kv_mat, queries, short):
    caps, slots, width = images.shape
    length = queries.shape[1]
    batch = 4 if caps % 4 == 0 else 1
    block = lambda *shape: pl.BlockSpec((batch,) + shape, lambda i, *_: (i, 0, 0))
    return pl.pallas_call(
        functools.partial(cross_start_body, short=short),
        grid_spec=pltpu.PrefetchScalarGridSpec(
            num_scalar_prefetch=1,
            grid=(caps // batch,),
            in_specs=[block(slots, width), whole(kv_mat.shape), block(length, width)],
            out_specs=[block(slots, 2 * width), block(length, width), block(GROUPS, LANES)],
        ),
        out_shape=[
            jax.ShapeDtypeStruct((caps, slots, 2 * width), BF16),
            jax.ShapeDtypeStruct((caps, length, width), BF16),
            jax.ShapeDtypeStruct((caps, GROUPS, LANES), F32),
        ],
        compiler_params=pltpu.CompilerParams(vmem_limit_bytes=VMEM_LIMIT),
        name="cross_start",
    )(valid, images, kv_mat, queries)


def feed_body(
    part_hbm, lse_hbm, hidden_ref, cot_ref, cross_mat, gain_ref, shift_ref, up_one, up_two, down_ref,
    out_ref, grad_two_ref, grads_hbm, lse_out, delta_out, up_keep, up_first, up_second, up_both,
    down_keep, down_away, cross_sum, gain_grad, shift_grad,
    send_sem, recv_sem, load_sem, att_one, att_two, lse_one, lse_two, att_full, att_low, hidden_two,
    normed_ref, acc_out, acc_grad, grad_att, lse_own, delta_own, up_pair, up_got, down_pair, down_got,
    cross_pair, cross_got, *, length, tile, bits, steps
):
    step = pl.program_id(0)
    me, side = lax.axis_index("dp"), lax.axis_index("kv")
    rows, width = hidden_ref.shape
    captions = rows // length
    tiles = rows // tile
    half = width // 2
    sub = up_one.shape[1]
    blocks = up_pair.shape[2]
    own = lambda bit: (me // (1 << bit)) % 2

    def remote(src, dst, index):
        return pltpu.make_async_remote_copy(
            src_ref=src, dst_ref=dst, send_sem=send_sem.at[index], recv_sem=recv_sem.at[index],
            device_id={"kv": 1 - side}, device_id_type=pl.DeviceIdType.MESH,
        )

    def row_span(index):
        return pl.ds(pl.multiple_of(index * tile, tile), tile)

    def chunk_copies(slot):
        return (
            remote(up_pair.at[slot, 1 - side], up_got.at[slot], 2 + slot),
            remote(down_pair.at[slot, 1 - side], down_got.at[slot], 4 + slot),
        )

    cross_copy = lambda: remote(cross_pair.at[1 - side], cross_got, 6)
    lse_copy = lambda: remote(lse_own, lse_out.at[side], 7)
    delta_copy = lambda: remote(delta_own, delta_out.at[side], 8)
    grad_copy = lambda index: remote(
        grad_att.at[pl.ds(index * tile, tile)], grads_hbm.at[side, pl.ds(index * tile, tile)], 9 + index
    )
    lse_store = lambda: pltpu.make_async_copy(lse_own, lse_out.at[side], load_sem.at[2])

    def cut(target, value):
        count, height, _ = target.shape
        if height % 16 == 0:
            target[...] = value.astype(BF16).reshape(target.shape)
        else:
            for index in range(count):
                target[index] = value[index * height : (index + 1) * height].astype(BF16)

    @pl.when(step == 0)
    def _():
        part_load = pltpu.make_async_copy(part_hbm.at[side], att_one, load_sem.at[0])
        lse_load = pltpu.make_async_copy(lse_hbm.at[side], lse_one, load_sem.at[1])
        part_load.start()
        lse_load.start()
        barrier = pltpu.get_barrier_semaphore()
        pl.semaphore_signal(barrier, inc=1, device_id={"kv": 1 - side}, device_id_type=pl.DeviceIdType.MESH)
        pl.semaphore_wait(barrier, 1)
        part_swap = remote(part_hbm.at[1 - side], att_two, 0)
        lse_swap = remote(lse_hbm.at[1 - side], lse_two, 1)
        lse_swap.start()
        part_swap.start()
        mask_low = same_head().astype(BF16)
        lse_load.wait()
        part_load.wait()
        lse_swap.wait()
        part_swap.wait()

        def one_caption(cap, carry):
            span = pl.ds(pl.multiple_of(cap * length, length), length)
            for group in range(GROUPS):
                lo = group * LANES
                first = lse_one[cap, group : group + 1]
                second = lse_two[cap, group : group + 1]
                peak = jnp.maximum(first, second)
                lse = peak + jnp.log(jnp.exp(first - peak) + jnp.exp(second - peak))
                lse_own[cap, group : group + 1] = lse
                weight_one = lanes_to_rows(jnp.exp(first - lse), mask_low)
                weight_two = lanes_to_rows(jnp.exp(second - lse), mask_low)
                mixed = (
                    weight_one * att_one[span, lo : lo + LANES].astype(F32)
                    + weight_two * att_two[span, lo : lo + LANES].astype(F32)
                )
                att_full[span, lo : lo + LANES] = mixed
                att_low[span, lo : lo + LANES] = mixed.astype(BF16)
            return carry

        lax.fori_loop(0, captions, one_caption, 0)
        lse_copy().start()
        lse_store().start()

        def one_tile(index, carry):
            span = row_span(index)
            two = hidden_ref[span, :] + dot(att_low[span, :], cross_mat[...])
            hidden_two[span, :] = two
            unit, _ = normalize(two)
            normed_ref[span, :] = (unit * as_row(gain_ref) + as_row(shift_ref)).astype(BF16)
            acc_out[span, :] = two
            acc_grad[span, :] = jnp.zeros_like(two)
            return carry

        lax.fori_loop(0, tiles, one_tile, 0)

    slot = step % 2
    cot = cot_ref[...]
    pre = dot(normed_ref[...], up_one[...])
    arrived = dot_nt(cot, down_ref[0])
    for part, up_part in enumerate((up_one, up_two)):
        now, came = pre, arrived
        if part == 0:
            pre = dot(normed_ref[...], up_two[...])
            arrived = dot_nt(cot, down_ref[1])
        cdf = 0.5 * (1.0 + lax.erf(now * 0.7071067811865476))
        density = jnp.exp(-0.5 * now * now) * 0.3989422804014327
        act = (now * cdf).astype(BF16)
        grad_up = (came * (cdf + now * density)).astype(BF16)
        acc_out[...] += dot(act, down_ref[part])
        acc_grad[...] += dot_nt(grad_up, up_part[...])
        grad_down = dot_tn(act, cot).astype(BF16)
        cut(up_pair.at[slot, part], dot_tn(normed_ref[...], grad_up))
        for side_part in range(2):
            down_pair[slot, side_part, part] = grad_down[:, side_part * half : (side_part + 1) * half]

    def take(chunk, place):
        for copy in chunk_copies(place):
            copy.wait()
        cols = pl.ds(pl.multiple_of(chunk * sub, sub), sub)
        for index, target in enumerate((up_keep, up_first, up_second, up_both)):
            flip = (index % 2, index // 2)
            low_bit, high_bit = (own(b) + f - 2 * own(b) * f for b, f in zip(bits[:2], flip))
            near = high_bit * 2 + low_bit

            def one(block, carry):
                source = block * 4 + near
                target[block, :, cols] = add_low(up_pair[place, side, source], up_got[place, source])
                return carry

            lax.fori_loop(0, blocks // 4, one, 0)
        total = add_low(down_pair[place, side], down_got[place])
        span = pl.ds(pl.multiple_of(chunk % (steps // 2) * sub, sub), sub)
        stays = chunk // (steps // 2) == own(bits[-2])

        @pl.when(stays)
        def _():
            down_keep[:, span, :] = total

        @pl.when(jnp.logical_not(stays))
        def _():
            down_away[:, span, :] = total

    @pl.when(step > 0)
    def _():
        take(step - 1, (step + 1) % 2)

    for copy in chunk_copies(slot):
        copy.start()

    @pl.when(step == steps - 1)
    def _():
        mask_low = same_head().astype(BF16)
        gain_grad[...] = jnp.zeros_like(gain_grad)
        shift_grad[...] = jnp.zeros_like(shift_grad)
        for index in range(tiles):
            span = pl.ds(index * tile, tile)
            unit, inverse = normalize(hidden_two[span, :])
            grad = acc_grad[span, :]
            gain_grad[...] += jnp.sum(grad * unit, axis=0, keepdims=True)
            shift_grad[...] += jnp.sum(grad, axis=0, keepdims=True)
            two = cot_ref[span, :].astype(F32) + norm_back(grad, as_row(gain_ref), unit, inverse)
            grad_two_ref[span, :] = two
            low = two.astype(BF16)
            normed_ref[span, :] = low
            grad_att[span, :] = dot_nt(low, cross_mat[...]).astype(BF16)
            grad_copy(index).start()
        grad_store = pltpu.make_async_copy(grad_att, grads_hbm.at[side], load_sem.at[0])
        grad_store.start()

        def one_caption(cap, carry):
            span = pl.ds(pl.multiple_of(cap * length, length), length)
            for group in range(GROUPS):
                lo = group * LANES
                product = grad_att[span, lo : lo + LANES].astype(F32) * att_full[span, lo : lo + LANES]
                delta_own[cap, group : group + 1] = rows_to_lanes(product, mask_low)
            return carry

        lax.fori_loop(0, captions, one_caption, 0)
        delta_copy().start()
        delta_store = pltpu.make_async_copy(delta_own, delta_out.at[side], load_sem.at[1])
        delta_store.start()
        grad_cross = dot_tn(att_low[...], normed_ref[...])
        for part in range(2):
            cut(cross_pair.at[part], grad_cross[:, part * half : (part + 1) * half])
        cross_copy().start()
        out_ref[...] = acc_out[...].astype(BF16)
        take(steps - 1, (steps - 1) % 2)
        cross_copy().wait()

        def one(block, carry):
            cross_sum[block] = add_low(cross_pair[side, block], cross_got[block])
            return carry

        lax.fori_loop(0, blocks, one, 0)
        for copy in [lse_copy(), lse_store(), delta_copy(), delta_store, grad_store]:
            copy.wait()
        for index in range(tiles):
            grad_copy(index).wait()


def feed(part, lse_part, hidden, cot, cross_mat, gain, shift, up_mat, down_mat, length, size):
    rows, width = hidden.shape
    captions = rows // length
    units = up_mat.shape[1]
    sub = 256
    steps = units // 2 // sub
    tile = min(256, rows)
    half = width // 2
    block = width // size
    bits = list(range(size.bit_length() - 1))
    stat = (captions, GROUPS, LANES)
    sds = jax.ShapeDtypeStruct
    once = lambda shape: pl.BlockSpec(shape, lambda *_: (0,) * len(shape), pipeline_mode=pl.Buffered(1))
    hbm = pl.BlockSpec(memory_space=pl.ANY)
    copies = 9 + rows // tile
    f32_rows = lambda: pltpu.VMEM((rows, width), F32)
    low_rows = lambda: pltpu.VMEM((rows, width), BF16)
    quarter = (size // 4, block, units // 2)
    return pl.pallas_call(
        functools.partial(feed_body, length=length, tile=tile, bits=bits, steps=steps),
        grid=(steps,),
        in_specs=[
            hbm, hbm, once((rows, width)), once((rows, width)), once((width, width)),
            once((width,)), once((width,)),
            pl.BlockSpec((width, sub), lambda i: (0, i)),
            pl.BlockSpec((width, sub), lambda i: (0, i + steps)),
            pl.BlockSpec((2, sub, width), lambda i: (0, i, 0)),
        ],
        out_specs=[
            whole((rows, width)), whole((rows, width)), hbm, hbm, hbm,
            whole(quarter), whole(quarter), whole(quarter), whole(quarter),
            whole((2, units // 4, half)), whole((2, units // 4, half)),
            whole((size, block, half)), whole((1, width)), whole((1, width)),
        ],
        out_shape=[
            sds((rows, width), BF16), sds((rows, width), F32), sds((2, rows, width), BF16),
            sds((2,) + stat, F32), sds((2,) + stat, F32),
            sds(quarter, BF16), sds(quarter, BF16), sds(quarter, BF16), sds(quarter, BF16),
            sds((2, units // 4, half), BF16), sds((2, units // 4, half), BF16),
            sds((size, block, half), BF16), sds((1, width), F32), sds((1, width), F32),
        ],
        scratch_shapes=[
            pltpu.SemaphoreType.DMA((copies,)), pltpu.SemaphoreType.DMA((copies,)),
            pltpu.SemaphoreType.DMA((3,)),
            low_rows(), low_rows(), pltpu.VMEM(stat, F32), pltpu.VMEM(stat, F32), f32_rows(), low_rows(),
            f32_rows(), low_rows(), f32_rows(), f32_rows(), low_rows(),
            pltpu.VMEM(stat, F32), pltpu.VMEM(stat, F32),
            pltpu.VMEM((2, 2, size, block, sub), BF16), pltpu.VMEM((2, size, block, sub), BF16),
            pltpu.VMEM((2, 2, 2, sub, half), BF16), pltpu.VMEM((2, 2, sub, half), BF16),
            pltpu.VMEM((2, size, block, half), BF16), pltpu.VMEM((size, block, half), BF16),
        ],
        compiler_params=pltpu.CompilerParams(
            vmem_limit_bytes=VMEM_MOST, collective_id=1, has_side_effects=True
        ),
        name="feed",
    )(
        part.reshape(2, rows, width), lse_part.reshape((2,) + stat), hidden, cot, cross_mat, gain, shift,
        up_mat, up_mat, down_mat.reshape(2, units // 2, width),
    )


def cross_back_body(
    valid_ref, side_ref, kv_ref, query_ref, grad_ref, lse_ref, delta_ref, kv_mat, img_ref,
    grad_query_ref, grad_img_ref, mine_ref, send_ref, grad_kv_ref, acc_ref, *, short
):
    step = pl.program_id(0)
    batch, slots, _ = kv_ref.shape
    width = query_ref.shape[2]
    held = img_ref.shape[0]
    base = step % (held // batch) * batch
    valids = [valid_ref[step * batch + cap] for cap in range(batch)]
    longest = most(valids)

    @pl.when(step == 0)
    def _():
        acc_ref[...] = jnp.zeros_like(acc_ref)

    def work(count):
        mask = same_head()
        row = iota((count, LANES), 0)

        def image_back(cap, part):
            place = base + cap if held > batch else cap
            lo = part * LANES
            columns = dot_nt(grad_kv_ref[place, :count], kv_mat[lo : lo + LANES, :])
            grad_img_ref[cap, :count, lo : lo + LANES] = columns.astype(BF16)

        for cap, valid in enumerate(valids):
            place = base + cap if held > batch else cap
            inside = row < valid
            for group in range(GROUPS):
                lo = group * LANES
                key = kv_ref[cap, :count, lo : lo + LANES]
                value = kv_ref[cap, :count, width + lo : width + lo + LANES]
                query = spread(query_ref[cap, :, lo : lo + LANES], mask)
                grad = spread(grad_ref[cap, :, lo : lo + LANES], mask)
                scores = dot_nt(key, query)
                probs = jnp.where(inside, jnp.exp(scores - lse_ref[cap, group : group + 1]), 0.0)
                grad_probs = dot_nt(value, grad)
                if cap > 0:
                    image_back(cap - 1, group)
                grad_scores = (probs * (grad_probs - delta_ref[cap, group : group + 1])).astype(BF16)
                back = gather_heads(dot_tn(grad_scores, key)) * SCALE
                grad_query_ref[cap, :, lo : lo + LANES] = back.astype(BF16)
                grad_kv_ref[place, :count, lo : lo + LANES] = dot(grad_scores, query).astype(BF16)
                grad_kv_ref[place, :count, width + lo : width + lo + LANES] = dot(
                    probs.astype(BF16), grad
                ).astype(BF16)
            if count < slots:
                grad_kv_ref[place, count:] = jnp.zeros((slots - count, 2 * width), BF16)
                grad_img_ref[cap, count:] = jnp.zeros((slots - count, width), BF16)
        for group in range(GROUPS):
            image_back(batch - 1, group)

    @pl.when(longest <= 0)
    def _():
        grad_query_ref[...] = jnp.zeros_like(grad_query_ref)
        for cap in range(batch):
            grad_kv_ref[base + cap] = jnp.zeros((slots, 2 * width), BF16)
        grad_img_ref[...] = jnp.zeros_like(grad_img_ref)

    if short < slots and batch <= 2:
        pl.when((longest > 0) & (longest <= short))(lambda: work(short))
        pl.when(longest > short)(lambda: work(slots))
    else:
        pl.when(longest > 0)(lambda: work(slots))

    @pl.when(base == held - batch)
    def _():
        left = img_ref[...].reshape(held * slots, width)
        right = grad_kv_ref[...].reshape(held * slots, 2 * width)
        acc_ref[...] += dot_tn(left, right)

    @pl.when(step == pl.num_programs(0) - 1)
    def _():
        side = side_ref[0]
        own = pl.ds(pl.multiple_of(side * width, width), width)
        other = pl.ds(pl.multiple_of((1 - side) * width, width), width)
        mine_ref[...] = acc_ref[:, own].astype(BF16)
        send_ref[...] = acc_ref[:, other].astype(BF16)


def cross_back(valid, side, kv, queries, grads, lse, delta, kv_mat, images, short):
    caps, slots, double = kv.shape
    width = double // 2
    length = queries.shape[1]
    held = 4 if caps % 4 == 0 else 1
    batch = min(4, held)
    block = lambda *shape: pl.BlockSpec((batch,) + shape, lambda i, *_: (i, 0, 0))
    sds = jax.ShapeDtypeStruct
    return pl.pallas_call(
        functools.partial(cross_back_body, short=short),
        grid_spec=pltpu.PrefetchScalarGridSpec(
            num_scalar_prefetch=2,
            grid=(caps // batch,),
            in_specs=[
                block(slots, double), block(length, width), block(length, width),
                block(GROUPS, LANES), block(GROUPS, LANES), whole(kv_mat.shape),
                pl.BlockSpec((held, slots, width), lambda i, *_: (i // (held // batch), 0, 0)),
            ],
            out_specs=[
                block(length, width), block(slots, width), whole((width, width)), whole((width, width)),
            ],
            scratch_shapes=[
                pltpu.VMEM((held, slots, double), BF16), pltpu.VMEM((width, double), F32),
            ],
        ),
        out_shape=[
            sds((caps, length, width), BF16), sds((caps, slots, width), BF16),
            sds((width, width), BF16), sds((width, width), BF16),
        ],
        compiler_params=pltpu.CompilerParams(vmem_limit_bytes=VMEM_LIMIT),
        name="cross_back",
    )(valid, side, kv, queries, grads, lse, delta, kv_mat, images)


def add_low(first, second):
    return first + second


def cut_blocks(target, value):
    height = target.shape[-2]
    count = len(target.shape) - 2
    if height % 16 == 0:
        target[...] = value.astype(BF16).reshape(target.shape)
    else:
        for i in range(1 << count):
            lead = tuple((i >> (count - 1 - d)) % 2 for d in range(count))
            target[lead] = value[i * height : (i + 1) * height].astype(BF16)


class Piece:
    def __init__(self, sums, source, out, col, width, bits, order, recvs, mine=None, send=None, kv_recv=None):
        self.sums, self.out, self.col, self.width = sums, out, col, width
        self.bits, self.order, self.recvs = list(bits), list(order), recvs
        self.mine, self.send, self.kv_recv = mine, send, kv_recv
        self.now, self.holds, self.pending = 0, source, None

    def columns(self, ref):
        return (slice(None), pl.ds(self.col, self.width) if ref.shape[-1] != self.width else slice(None))

    def start_kv(self):
        whole_lead = (slice(None),) * len(self.bits)
        self.pending = self.sums.copy(
            self.send.at[whole_lead + self.columns(self.send)], self.kv_recv, {"kv": 1 - self.sums.side}
        )
        self.pending.start()

    def start(self):
        bit = self.order[self.now]
        lead = tuple(1 - self.sums.own(bit) if b == bit else slice(None) for b in self.bits)
        self.pending = self.sums.copy(
            self.holds.at[lead + self.columns(self.holds)], self.recvs[self.now], self.sums.partner(bit)
        )
        self.pending.start()

    def add(self, kept, arrived, cols, left, fixed):
        def one(i, carry):
            inner = {b: (i // (1 << (len(left) - 1 - d))) % 2 for d, b in enumerate(left)}
            lead = tuple(inner[b] if b in inner else fixed[b] for b in self.bits)
            into = tuple(inner[b] for b in left)
            arrived[into] = add_low(kept[lead + cols], arrived[into])
            return carry

        lax.fori_loop(0, 1 << len(left), one, 0)

    def advance(self):
        if self.pending is None:
            return True
        self.pending.wait()
        self.pending = None
        if self.holds is None:
            self.add(self.mine, self.kv_recv, self.columns(self.mine), self.bits, {})
            self.holds = self.kv_recv
            self.start()
            return False
        bit = self.order[self.now]
        arrived, cols = self.recvs[self.now], self.columns(self.holds)
        left = [b for b in self.bits if b != bit]
        if not left:
            total = self.holds[(self.sums.own(bit),) + cols].astype(F32) + arrived[...].astype(F32)
            self.out[:, self.col : self.col + self.width] = total
            return True
        self.add(self.holds, arrived, cols, left, {bit: self.sums.own(bit)})
        self.bits, self.holds, self.now = left, arrived, self.now + 1
        self.start()
        return False


class Sums:
    def __init__(self, send_sem, recv_sem):
        self.send_sem, self.recv_sem, self.count = send_sem, recv_sem, 0
        self.me, self.side = lax.axis_index("dp"), lax.axis_index("kv")

    def own(self, bit):
        return (self.me // (1 << bit)) % 2

    def partner(self, bit):
        return {"dp": self.me + (1 - 2 * self.own(bit)) * (1 << bit)}

    def copy(self, src, dst, device):
        index = self.count
        self.count += 1
        return pltpu.make_async_remote_copy(
            src_ref=src, dst_ref=dst, send_sem=self.send_sem.at[index], recv_sem=self.recv_sem.at[index],
            device_id=device, device_id_type=pl.DeviceIdType.MESH,
        )

    def greet(self, bits):
        barrier = pltpu.get_barrier_semaphore()
        for device in [{"kv": 1 - self.side}] + [self.partner(bit) for bit in bits]:
            pl.semaphore_signal(barrier, inc=1, device_id=device, device_id_type=pl.DeviceIdType.MESH)
        pl.semaphore_wait(barrier, 1 + len(bits))


def turned(bits, by):
    first = bits[:-1]
    by %= len(first)
    return first[by:] + first[:by] + bits[-1:]


def end_body(
    back_hbm, hidden_hbm, grad_two_hbm, att_hbm, qkv_hbm, tok_hbm, qkv_mat_hbm, out_mat_hbm, query_mat_hbm,
    gain_one, shift_one, gain_two, shift_two, gain_three, shift_three,
    up_keep, up_first, up_second, up_both, down_keep, down_away, cross_ref, kv_mine, kv_send,
    grad_tok, up_out, down_out, cross_out, qkv_out, out_out, query_out, kv_out, gains_out,
    *scratch, plan, bits, length, tile
):
    scratch = list(scratch)
    (
        send_sem, recv_sem, load_sem, back_one, back_two, hidden, grad_two, att, qkv, tok, qkv_mat,
        out_mat, query_mat, back_sum, normed, low, grad_att, grad_qkv, gains_all, gain_kv,
        gain_buf, gain_recv, qkv_mine, qkv_send, out_mine, out_send, query_mine, query_send,
        up_ref, down_ref,
    ) = scratch[:30]
    rest = scratch[30:]
    sums = Sums(send_sem, recv_sem)
    side = sums.side
    captions = back_one.shape[0]
    rows, width = hidden.shape
    half = width // 2
    named = dict(
        up=(up_ref, None, None, up_out), down=(down_ref, None, None, down_out),
        cross=(cross_ref, None, None, cross_out), qkv=(None, qkv_mine, qkv_send, qkv_out),
        out=(None, out_mine, out_send, out_out), query=(None, query_mine, query_send, query_out),
        kv=(None, kv_mine, kv_send, kv_out),
    )
    pieces = {}
    for name, col, cols, axes, order, kv in plan:
        source, mine, send, out = named[name]
        kv_recv = rest.pop(0) if kv else None
        recvs = [rest.pop(0) for _ in order]
        pieces.setdefault(name, []).append(
            Piece(sums, source, out, col, cols, axes, order, recvs, mine, send, kv_recv)
        )
    early = pieces["up"] + pieces["down"] + pieces["cross"]
    image = pieces["kv"]
    middle = pieces["query"] + pieces["out"]
    late = pieces["qkv"]

    own_caps = pl.ds(pl.multiple_of(side * captions, captions), captions)
    other_caps = pl.ds(pl.multiple_of((1 - side) * captions, captions), captions)
    pairs = [
        (back_hbm.at[own_caps], back_one), (hidden_hbm, hidden), (query_mat_hbm, query_mat),
        (grad_two_hbm, grad_two), (out_mat_hbm, out_mat), (att_hbm, att), (qkv_hbm, qkv),
        (tok_hbm, tok), (qkv_mat_hbm, qkv_mat),
    ]
    loads = [pltpu.make_async_copy(src, dst, load_sem.at[i]) for i, (src, dst) in enumerate(pairs)]
    for load in loads:
        load.start()
    sums.greet(bits)
    swap = sums.copy(back_hbm.at[other_caps], back_two, {"kv": 1 - side})
    swap.start()
    for piece in image:
        piece.start_kv()

    def sum_terms(target, terms):
        count = len(target.shape) - 2

        def one(i, carry):
            lead = tuple((i // (1 << (count - 1 - d))) % 2 for d in range(count))
            total = terms[0][lead].astype(F32)
            for term in terms[1:]:
                total += term[lead].astype(F32)
            target[lead] = total.astype(BF16)
            return carry

        lax.fori_loop(0, 1 << count, one, 0)

    sum_terms(up_ref, (up_keep, up_first, up_second, up_both))
    sum_terms(down_ref, (down_keep, down_away))
    for piece in early:
        piece.start()
    gains_all[...] = jnp.zeros_like(gains_all)
    gains_all[4:5] = gain_three[...]
    gains_all[5:6] = shift_three[...]
    for load in loads[:5]:
        load.wait()
    swap.wait()

    def rows_at(index):
        return pl.ds(pl.multiple_of(index * tile, tile), tile)

    def query_back(index, carry):
        span = rows_at(index)
        caps = pl.ds(index * (tile // length), tile // length)
        back = add_low(back_one[caps], back_two[caps]).reshape(tile, width)
        back_sum[span, :] = back
        unit, inverse = normalize(hidden[span, :])
        normed[span, :] = (unit * as_row(gain_two) + as_row(shift_two)).astype(BF16)
        grad = dot_nt(back, query_mat[...])
        gains_all[2:3] += jnp.sum(grad * unit, axis=0, keepdims=True)
        gains_all[3:4] += jnp.sum(grad, axis=0, keepdims=True)
        grad_one = grad_two[span, :] + norm_back(grad, as_row(gain_two), unit, inverse)
        grad_two[span, :] = grad_one
        low[span, :] = grad_one.astype(BF16)
        grad_att[span, :] = dot_nt(grad_one.astype(BF16), out_mat[...]).astype(BF16)
        return carry

    lax.fori_loop(0, rows // tile, query_back, 0)
    for piece in image:
        piece.advance()

    def weight(left, right, target, which):
        cols = target.shape[-1]
        start = pl.multiple_of(which * cols, 128)
        cut_blocks(target, dot_tn(left[...], right[:, pl.ds(start, cols)]))

    def weights(left, right, mine, send, group):
        weight(left, right, send, 1 - side)
        for piece in group:
            piece.start_kv()
        weight(left, right, mine, side)

    weights(normed, back_sum, query_mine, query_send, pieces["query"])
    loads[5].wait()
    loads[6].wait()
    weights(att, low, out_mine, out_send, pieces["out"])
    for piece in middle + pieces["cross"] + pieces["up"]:
        piece.advance()

    mask = same_head()
    causal = causal_mask(length)

    def attend(cap):
        span = pl.ds(pl.multiple_of(cap * length, length), length)
        for group in range(GROUPS):
            lo = group * LANES
            query = spread(qkv[span, lo : lo + LANES] * SCALE, mask)
            key = qkv[span, width + lo : width + lo + LANES]
            value = qkv[span, 2 * width + lo : 2 * width + lo + LANES]
            cot = spread(grad_att[span, lo : lo + LANES], mask)
            scores = jnp.where(causal, dot_nt(key, query), NEG)
            exponent = jnp.exp(scores - jnp.max(scores, axis=0, keepdims=True))
            probs = exponent / jnp.sum(exponent, axis=0, keepdims=True)
            grad_probs = dot_nt(value, cot)
            mean = jnp.sum(probs * grad_probs, axis=0, keepdims=True)
            grad_scores = (probs * (grad_probs - mean)).astype(BF16)
            grad_q = gather_heads(dot_tn(grad_scores, key)) * SCALE
            grad_qkv[span, lo : lo + LANES] = grad_q.astype(BF16)
            grad_qkv[span, width + lo : width + lo + LANES] = dot(grad_scores, query).astype(BF16)
            grad_qkv[span, 2 * width + lo : 2 * width + lo + LANES] = dot(
                probs.astype(BF16), cot
            ).astype(BF16)

    together = 2 if captions % 2 == 0 else 1

    def attend_some(index, carry):
        for cap in range(together):
            attend(index * together + cap)
        return carry

    rounds = captions // together
    lax.fori_loop(0, rounds // 2, attend_some, 0)
    for piece in image + pieces["down"]:
        piece.advance()
    lax.fori_loop(rounds // 2, rounds, attend_some, 0)
    for piece in early + image + middle:
        piece.advance()
    loads[7].wait()
    loads[8].wait()

    def token_norm(index, carry):
        span = rows_at(index)
        unit, _ = normalize(tok[span, :].astype(F32))
        normed[span, :] = (unit * as_row(gain_one) + as_row(shift_one)).astype(BF16)
        return carry

    lax.fori_loop(0, rows // tile, token_norm, 0)
    weights(normed, grad_qkv, qkv_mine, qkv_send, late)
    for piece in late + early + middle + image:
        piece.advance()

    def token_back(index, carry):
        span = rows_at(index)
        unit, inverse = normalize(tok[span, :].astype(F32))
        grad = dot_nt(grad_qkv[span, :], qkv_mat[...])
        gains_all[0:1] += jnp.sum(grad * unit, axis=0, keepdims=True)
        gains_all[1:2] += jnp.sum(grad, axis=0, keepdims=True)
        back = grad_two[span, :] + norm_back(grad, as_row(gain_one), unit, inverse)
        grad_tok[span, :] = back.astype(BF16)
        return carry

    lax.fori_loop(0, rows // tile, token_back, 0)
    own_cols = pl.ds(pl.multiple_of(side * half, 128), half)
    other_cols = pl.ds(pl.multiple_of((1 - side) * half, 128), half)
    gain_copy = sums.copy(gains_all.at[:, other_cols], gain_kv, {"kv": 1 - side})
    gain_copy.start()
    stage = -1
    everything = late + early + image + middle
    while stage < len(bits) or not all(piece.pending is None for piece in everything):
        if stage < len(bits):
            gain_copy.wait()
            if stage < 0:
                gain_buf[0] = gains_all[:, own_cols] + gain_kv[...]
            else:
                gain_buf[stage + 1] = gain_buf[stage] + gain_recv[stage]
            stage += 1
            if stage < len(bits):
                gain_copy = sums.copy(gain_buf.at[stage], gain_recv.at[stage], sums.partner(bits[stage]))
                gain_copy.start()
            else:
                gains_out[...] = gain_buf[stage]
        for piece in everything:
            piece.advance()


def end(
    back, hidden, grad_two, att, qkv, tokens, qkv_mat, out_mat, query_mat, gain_one, shift_one,
    gain_two, shift_two, gain_three, shift_three, early, kv_mine, kv_send, length, size
):
    bits = list(range(size.bit_length() - 1))
    axes = bits[::-1]
    rows, width = hidden.shape
    captions = rows // length
    tile = min(256, rows)
    block = width // size
    lead = (2,) * len(bits)
    up_terms, down_terms, cross = early
    up, down = up_terms[0], down_terms[0]
    third = width // 3
    plan = [("up", 0, up.shape[-1], axes[:-2], bits[2:], False)]
    down_axes = axes[:1] + axes[2:]
    plan.append(("down", 0, down.shape[-1], down_axes, [b for b in bits if b in down_axes], False))
    plan.append(("cross", 0, cross.shape[-1], axes, bits[1:2] + bits[:1] + bits[2:], False))
    plan.append(("query", 0, width // 2, axes, turned(bits, 0), True))
    plan.append(("out", 0, width // 2, axes, turned(bits, 1), True))
    for by in range(3):
        plan.append(("kv", by * third, third, axes, turned(bits, by), True))
    for by in range(3):
        plan.append(("qkv", by * (width // 2), width // 2, axes, turned(bits, by), True))
    heights = dict(up=up.shape[-2], down=down.shape[-2], cross=cross.shape[-2])
    buffers = []
    copies = 2 + len(bits)
    for name, col, cols, piece_axes, order, kv in plan:
        shape = (heights.get(name, block), cols)
        for count in range(len(order) if kv else len(order) - 1, -1, -1):
            buffers.append(pltpu.VMEM((2,) * count + shape, BF16))
            copies += 1
    vmem = pl.BlockSpec(memory_space=pltpu.VMEM)
    hbm = pl.BlockSpec(memory_space=pl.ANY)
    sds = jax.ShapeDtypeStruct
    cut = lambda cols: pltpu.VMEM(lead + (block, cols), BF16)
    outs = [sds((rows, width), BF16)]
    outs += [sds(v.shape[-2:], F32) for v in (up, down, cross)]
    outs += [sds((block, cols), F32) for cols in (3 * width // 2, width // 2, width // 2, width)]
    outs += [sds((8, width // 2), F32)]
    low_rows = lambda cols: pltpu.VMEM((rows, cols), BF16)
    return pl.pallas_call(
        functools.partial(end_body, plan=plan, bits=bits, length=length, tile=tile),
        in_specs=[hbm] * 9 + [vmem] * 6 + [vmem] * 8 + [hbm],
        out_specs=[vmem] * len(outs),
        out_shape=outs,
        scratch_shapes=[
            pltpu.SemaphoreType.DMA((copies,)), pltpu.SemaphoreType.DMA((copies,)),
            pltpu.SemaphoreType.DMA((9,)),
            pltpu.VMEM((captions, length, width), BF16), pltpu.VMEM((captions, length, width), BF16),
            pltpu.VMEM((rows, width), F32), pltpu.VMEM((rows, width), F32), low_rows(width),
            low_rows(3 * width), low_rows(width), pltpu.VMEM(qkv_mat.shape, BF16),
            pltpu.VMEM(out_mat.shape, BF16), pltpu.VMEM(query_mat.shape, BF16),
            low_rows(width), low_rows(width), low_rows(width), low_rows(width), low_rows(3 * width),
            pltpu.VMEM((8, width), F32),
            pltpu.VMEM((8, width // 2), F32), pltpu.VMEM((len(bits) + 1, 8, width // 2), F32),
            pltpu.VMEM((len(bits), 8, width // 2), F32),
            cut(3 * width // 2), cut(3 * width // 2), cut(width // 2), cut(width // 2),
            cut(width // 2), cut(width // 2), pltpu.VMEM(up.shape, BF16), pltpu.VMEM(down.shape, BF16),
        ] + buffers,
        compiler_params=pltpu.CompilerParams(
            vmem_limit_bytes=VMEM_MOST, collective_id=0, has_side_effects=True
        ),
        name="end",
    )(
        back, hidden, grad_two, att, qkv, tokens, qkv_mat, out_mat, query_mat, gain_one, shift_one,
        gain_two, shift_two, gain_three, shift_three, *up_terms, *down_terms, cross, kv_mine, kv_send,
    )


def hand_over_body(gains_ref, *refs):
    count = len(refs) // 2 - 3
    for source, target in zip(refs[:count], refs[count : 2 * count]):
        target[...] = source[...]
    for index, target in enumerate(refs[2 * count :]):
        target[...] = gains_ref[index : index + 1, :].reshape(target.shape)


def hand_over(gains, *arrays):
    vmem = pl.BlockSpec(memory_space=pltpu.VMEM)
    shapes = [jax.ShapeDtypeStruct(v.shape, v.dtype) for v in arrays]
    shapes += [jax.ShapeDtypeStruct(gains.shape[1:], gains.dtype)] * 6
    return pl.pallas_call(
        hand_over_body,
        in_specs=[vmem] * (1 + len(arrays)),
        out_specs=[vmem] * len(shapes),
        out_shape=shapes,
        name="hand_over",
    )(gains, *arrays)


def exchange(value, axis, bit, size):
    return lax.ppermute(value, axis, [(i, i ^ bit) for i in range(size)])


def split_rows(array, size):
    bits = size.bit_length() - 1
    return array.reshape((2,) * bits + (array.shape[0] // size, array.shape[1]))


def body(
    tokens, images, image_counts, cotangent, norm1_gain, norm1_shift, self_qkv, self_out,
    norm2_gain, norm2_shift, cross_q, cross_kv, cross_out, norm3_gain, norm3_shift, w_up, w_down,
):
    captions, length, width = tokens.shape
    caps, slots, _ = images.shape
    side = lax.axis_index("kv")
    me = lax.axis_index("dp")
    groups = lax.axis_size("dp")
    side_arr = side.reshape(1)
    tok = tokens.reshape(captions * length, width)
    cot = cotangent.reshape(captions * length, width)
    short = -(-SHORT // 16) * 16
    valid = jnp.clip(image_counts - side * slots, 0, slots)

    qkv, att, hidden, queries = token_start(
        tok, norm1_gain, norm1_shift, self_qkv, self_out, norm2_gain,
        norm2_shift, cross_q, length,
    )

    queries = queries.reshape(caps, length, width)
    kv, part, lse_part = cross_start(valid, images, cross_kv, queries, short)
    (
        layer_out, grad_two, grads, lse, delta, up_keep, up_first, up_second, up_both, down_keep,
        down_away, cross_sum, gain3, shift3,
    ) = feed(
        part, lse_part, hidden, cot, cross_out, norm3_gain, norm3_shift, w_up, w_down, length, groups
    )
    bits = groups.bit_length() - 1
    cubes = lambda v, count: v.reshape((2,) * count + (v.shape[0] * v.shape[1] >> count, v.shape[2]))
    up_terms = [up_keep] + [
        exchange(away, "dp", flip, groups) for away, flip in ((up_first, 1), (up_second, 2), (up_both, 3))
    ]
    down_terms = [down_keep, exchange(down_away, "dp", 1 << (bits - 2), groups)]
    early = (
        [cubes(v, bits - 2) for v in up_terms], [cubes(v, bits - 1) for v in down_terms],
        cubes(cross_sum, bits),
    )

    stats = lambda v: v.reshape(caps, GROUPS, LANES)
    back, images_grad, kv_mine, kv_send = cross_back(
        valid, side_arr, kv, queries, grads.reshape(caps, length, width), stats(lse), stats(delta),
        cross_kv, images, short
    )
    cut = lambda v: split_rows(v, groups)
    *sums, gains = end(
        back, hidden, grad_two, att, qkv, tok, self_qkv, self_out, cross_q, norm1_gain, norm1_shift,
        norm2_gain, norm2_shift, gain3, shift3, early, cut(kv_mine), cut(kv_send), length, groups,
    )
    (
        tokens_grad, w_up_grad, down_grad, cross_out_grad, self_qkv_grad, self_out_grad, cross_q_grad,
        cross_kv_grad, layer_out, *gains,
    ) = hand_over(gains, *sums, layer_out)
    return (
        layer_out.reshape(captions, length, width),
        tokens_grad.reshape(captions, length, width),
        images_grad,
        gains[0], gains[1], self_qkv_grad, self_out_grad, gains[2], gains[3], cross_q_grad,
        cross_kv_grad, cross_out_grad, gains[4], gains[5], w_up_grad, down_grad,
    )


def solution(mesh):
    return jax.shard_map(
        body,
        mesh=mesh,
        in_specs=(
            P(("dp", "kv"), None, None), P("dp", "kv", None), P("dp"), P(("dp", "kv"), None, None),
        ) + (P(),) * 13,
        out_specs=(
            P(("dp", "kv"), None, None), P(("dp", "kv"), None, None), P("dp", "kv", None),
            P("kv"), P("kv"), P("dp", "kv"), P("dp", "kv"), P("kv"), P("kv"), P("dp", "kv"),
            P("dp", "kv"), P("dp", "kv"), P("kv"), P("kv"), P("dp", "kv"), P("dp", "kv"),
        ),
        check_vma=False,
    )
```
